256 devices in a mesh: tile: 64 (over x, z, core), depth: 4 (over y).
Axes of the slice: x: 4, y: 4, z: 8, core: 2. Of those that a mesh axis runs over, the one named last changes fastest.
Arguments:
- soil_state: float32 [16, 512, 6, 128], P('depth', 'tile')
- tile_count: int32 [16, 512], P('depth', 'tile'), may hold values from 64 to 128, as said below
- tile_neighbors: int32 [16, 512, 6], P('depth', 'tile'), may hold values from 0 to 8, as said below
- marker_pos: float32 [3, 1048576], P(None, ('tile', 'depth')), may hold values from -1 to 1
- marker_vel: float32 [3, 1048576], P(None, ('tile', 'depth')), may hold values from -5 to 5
- marker_tile: int32 [1048576], P(('tile', 'depth')), may hold values from 0 to 31
- marker_owner: int32 [1048576, 1], P(('tile', 'depth')), may hold values from 0 to 63; in each aligned block of 4096 rows (0 to 4095, 4096 to 8191, ...) at most 256 rows name the same one
- marker_slot: int32 [1048576], P(('tile', 'depth')), may hold values from 0 to 127
- body_state: float32 [9, 8192], P(None, 'tile'), may hold values from -4 to 4
- body_inertia: float32 [4, 8192], P(None, 'tile'), may hold values from 0.5 to 2
Outputs:
- soil_accel: float32 [16, 512, 3, 128], P('depth', 'tile')
- body_next: float32 [9, 8192], P(None, 'tile')
- marker_vel_next: float32 [3, 1048576], P(None, ('tile', 'depth'))
The draws below stay inside these ranges and needn't reach their ends.
Inputs may be any that keep to these rules, and one draw needn't show every extreme that they name: `tile_count`: number of real particles of the tile; slots from it on are padding. `tile_neighbors`: a code c names the tile at layer offset c // 3 - 1 and horizontal offset c % 3 - 1; each tile lists 6 distinct codes, the first being 4 (itself). `marker_tile`: index among the 4 x 8 tiles of the device that holds the marker, layer-major. `marker_owner`: in each aligned block of 4096 markers (those of one device) no owner is named more than 256 times, a bound that some block reaches.
All inputs are finite; a program needn't handle non-finite values.
Results may differ from the reference program's by a relative error of at most 0.0001.
Values sent between devices are 32-bit elements; how exact they have to be, the bound alone decides.
No kernel may reach another device: no remote copies, remote signals or barrier semaphores. Data moves between devices by JAX's collectives and lax.ppermute only.
A program may use at most 64 MiB of HBM per device.

```python
import math
import jax
import jax.numpy as jnp
import numpy as np
from jax import lax

ZL = 4
HL = 8
TP = 128
NEIGH = 6
BODY_TILE = 128
DEPTH_DEVS = 4
NZT = 16
NHT = 512
BODIES = 8192
MKD = 4096
MARKERS = 1048576
CAP = 256
N_TILE = 64


def draw_soil_state(key, part):
    key_places, key_speeds = jax.random.split(key)
    places = jax.random.uniform(key_places, (NZT, NHT, 3, TP), jnp.float32, -1.0, 1.0)
    speeds = jax.random.normal(key_speeds, (NZT, NHT, 3, TP), jnp.float32)
    return jnp.concatenate([places, speeds], axis=2)


def draw_tile_count(key, part):
    counts = jax.random.randint(key, (NZT, NHT), TP // 2, TP + 1)
    counts = counts.at[0, 0].set(TP).at[0, NHT - 1].set(TP // 2)
    return counts.astype(jnp.int32)


def draw_tile_neighbors(key, part):
    scores = jax.random.randint(key, (NZT, NHT, 8), 0, 1 << 20) * 8 + jnp.arange(8, dtype=jnp.int32)
    ranking = jnp.argsort(scores, axis=2, stable=True)
    others = jnp.array([0, 1, 2, 3, 5, 6, 7, 8], jnp.int32)[ranking[:, :, 0:NEIGH - 1]]
    itself = jnp.full((NZT, NHT, 1), 4, jnp.int32)
    return jnp.concatenate([itself, others], axis=2).astype(jnp.int32)


def touch_ends(drawn, rng, low, largest):
    shape = drawn.shape
    place = [jax.random.randint(jax.random.fold_in(rng, axis), (), 0, shape[axis]) for axis in range(len(shape))]
    drawn = drawn.at[tuple(place)].set(low)
    longest = shape.index(max(shape))
    place[longest] = (place[longest] + 1) % shape[longest]
    return drawn.at[tuple(place)].set(largest)


def block_scale(own_key, extent, cuts, low, largest):
    def one(position, shards_of):
        steps = jax.random.uniform(jax.random.fold_in(jax.random.fold_in(own_key, 6), position), (shards_of,), jnp.float32, low / len(cuts), largest / len(cuts))
        return jnp.repeat(jnp.exp(steps), extent[position] // shards_of).reshape((-1,) + (1,) * (len(extent) - position - 1))

    gain = one(*cuts[0])
    for cut in cuts[1:]:
        gain = gain * one(*cut)
    return gain


def shared_out(own_key, own, number, rows, count, top, most, lean):
    order = jax.random.permutation(own_key, count)
    crowded, ordinary = load_shares(count, rows * top, most, lean, True), load_shares(count, rows * top, most, lean, False)
    places = jnp.arange(count)

    def named(tallies, rotation):
        used = int((tallies > 0).sum())
        fixed = max(1, used // 4)
        passed = fixed + (places - fixed + rotation * (used - fixed)) % max(1, count - fixed)
        return jnp.zeros((count,), jnp.int32).at[order[jnp.where(places < fixed, places, passed)]].set(jnp.asarray(tallies, jnp.int32))

    tallies = jnp.where(number % 4 == 0, named(crowded, number // 4), named(ordinary, number - number // 4 - 1))
    mixed = jax.random.permutation(jax.random.fold_in(own, 3), count)
    giver, sink = mixed[0:count // 2 * 2:2], mixed[1:count // 2 * 2:2]
    margin = jnp.minimum(tallies[giver] - 1, most - tallies[sink]) // 2
    margin = jnp.where((giver == order[0]) | (sink == order[0]) | (tallies[sink] == 0), 0, jnp.maximum(margin, 0))
    passed = jax.random.randint(jax.random.fold_in(own, 4), (count // 2,), 0, 1 << 20) % (margin + 1)
    tallies = tallies.at[giver].add(-passed).at[sink].add(passed)
    labels = jnp.searchsorted(jnp.cumsum(tallies), jnp.arange(rows * top), side="right").astype(jnp.int32)
    table = labels.reshape(top, rows).T
    table = table[jax.random.permutation(jax.random.fold_in(own, 1), rows)]
    rotation = jax.random.randint(jax.random.fold_in(own, 2), (rows, 1), 0, top)
    return jnp.take_along_axis(table, (jnp.arange(top)[None, :] + rotation) % top, axis=1)


def load_shares(count, total, bound, slope, full):
    weights = [(1 << 20) // math.isqrt(standing ** slope) + 1 for standing in range(1, count + 1)]
    largest = bound if full else min(bound, max(-(-total // count), total * weights[0] // sum(weights)))
    least = 1 if total - largest >= count - 1 else 0
    given, rest = [largest] + [least] * (count - 1), total - largest - least * (count - 1)
    while rest > 0:
        candidates = [i for i in range(1, count) if given[i] < largest] or [i for i in range(1, count) if given[i] < bound]
        mass, left = sum([weights[i] for i in candidates]), rest
        for i in candidates:
            addition = min(bound - given[i], max(1, left * weights[i] // mass), rest)
            given[i] = given[i] + addition
            rest = rest - addition
    return np.array(given)


def normal_values(rng, shape, deviation, bound, cuts=(), held_as=jnp.bfloat16):
    factor_of = block_scale(rng, shape, cuts, -0.22, 0.18) if cuts else 1.0
    values = jax.random.normal(rng, shape, jnp.float32) * deviation * factor_of
    return jnp.minimum(jnp.maximum(values, -bound), bound).astype(held_as)


def setup_inputs(seed: int = 0) -> dict:
    keys = jax.random.split(jax.random.key(seed), 11)
    soil_state = draw_soil_state(jax.random.fold_in(keys[10], 71), 0)
    tile_count = draw_tile_count(jax.random.fold_in(keys[10], 71), 0)
    tile_neighbors = draw_tile_neighbors(jax.random.fold_in(keys[10], 71), 0)
    marker_pos = jnp.clip(jax.random.uniform(keys[3], (3, MARKERS), jnp.float32, -1.0, 1.0) * block_scale(keys[3], (3, MARKERS), ((1, 256),), -0.4, 0.0), -1.0, 1.0)
    marker_vel = normal_values(keys[4], (3, MARKERS), 1.0, 5.0, ((1, 256),), jnp.float32)
    marker_tile = touch_ends(jax.random.randint(keys[5], (MARKERS,), 0, ZL * HL), jax.random.fold_in(keys[5], 1), 0, (ZL * HL) - 1).astype(jnp.int32)
    marker_owner_keys = jax.random.split(jax.random.fold_in(keys[6], 1), MARKERS // MKD)
    marker_owner_turns = jax.random.permutation(jax.random.fold_in(keys[6], 3), MARKERS // MKD)
    marker_owner = jax.vmap(lambda own, number: shared_out(jax.random.fold_in(keys[6], 2), own, number, MKD, N_TILE, 1, CAP, 2))(marker_owner_keys, marker_owner_turns).reshape((MARKERS, 1))
    marker_slot = touch_ends(jax.random.randint(keys[7], (MARKERS,), 0, BODY_TILE), jax.random.fold_in(keys[7], 1), 0, BODY_TILE - 1).astype(jnp.int32)
    body_state = normal_values(keys[8], (9, BODIES), 1.0, 4.0, ((1, 64),), jnp.float32)
    body_inertia = jnp.clip(jnp.exp(math.log(2.0) - 1.3862944 * jax.random.uniform(keys[9], (4, BODIES), jnp.float32) ** block_scale(keys[9], (4, BODIES), ((1, 64),), -0.2, 0.2)), 0.5, 2.0)
    return {"soil_state": soil_state, "tile_count": tile_count, "tile_neighbors": tile_neighbors, "marker_pos": marker_pos, "marker_vel": marker_vel, "marker_tile": marker_tile, "marker_owner": marker_owner, "marker_slot": marker_slot, "body_state": body_state, "body_inertia": body_inertia}


stiffness = 40.0
rest_density = 2.0
viscosity = 20.0
time_step = 0.05
gravity = 1.0


def cross(first_vec, second_vec):
    return jnp.stack([first_vec[1] * second_vec[2] - first_vec[2] * second_vec[1],
                      first_vec[2] * second_vec[0] - first_vec[0] * second_vec[2],
                      first_vec[0] * second_vec[1] - first_vec[1] * second_vec[0]], axis=0)


def pair_weights(left_pos, right_pos, right_live):
    distance = jnp.zeros((left_pos.shape[0], left_pos.shape[2], right_pos.shape[2]), jnp.float32)
    for component in range(3):
        offset = left_pos[:, component, :, None] - right_pos[:, component, None, :]
        distance = distance + offset * offset
    return right_live[:, None, :] * jnp.exp(-distance)


def block_density(own_tiles, nbr_ids, table):
    summed = jnp.zeros((own_tiles.shape[0], own_tiles.shape[2]), jnp.float32)
    for entry_num in range(nbr_ids.shape[1]):
        neighbor = table[nbr_ids[:, entry_num]]
        summed = summed + jnp.sum(pair_weights(own_tiles[:, 0:3], neighbor[:, 0:3], neighbor[:, 6]), axis=2)
    return 1.0 + summed / own_tiles.shape[2]


def block_accel(own_tiles, own_extra, nbr_ids, table, extra_table):
    accel_parts = [jnp.zeros((own_tiles.shape[0], own_tiles.shape[2]), jnp.float32) for component in range(3)]
    for entry_num in range(nbr_ids.shape[1]):
        neighbor = table[nbr_ids[:, entry_num]]
        neighbor_extra = extra_table[nbr_ids[:, entry_num]]
        weight = pair_weights(own_tiles[:, 0:3], neighbor[:, 0:3], neighbor[:, 6])
        press = 2.0 * (own_extra[:, 0, :, None] + neighbor_extra[:, 0, None, :])
        damping = viscosity * neighbor_extra[:, 1, None, :]
        for component in range(3):
            offset = own_tiles[:, component, :, None] - neighbor[:, component, None, :]
            relative = neighbor[:, 3 + component, None, :] - own_tiles[:, 3 + component, :, None]
            accel_parts[component] = accel_parts[component] + jnp.sum(weight * (press * offset + damping * relative), axis=2)
    accel_out = jnp.stack(accel_parts, axis=1) / own_tiles.shape[2]
    return accel_out * own_tiles[:, 6:7, :]


def marker_force(marker_place, marker_speed, source):
    distance = jnp.zeros((source.shape[0], source.shape[2]), jnp.float32)
    for component in range(3):
        offset = marker_place[:, component, None] - source[:, component, :]
        distance = distance + offset * offset
    weight = source[:, 6, :] * jnp.exp(-distance)
    forces = []
    for component in range(3):
        offset = marker_place[:, component, None] - source[:, component, :]
        relative = source[:, 3 + component, :] - marker_speed[:, component, None]
        forces.append(jnp.sum(weight * (2.0 * source[:, 7, :] * offset + viscosity * source[:, 8, :] * relative), axis=1))
    return jnp.stack(forces, axis=1) / source.shape[2]


def advance(totals, body_state, body_inertia):
    center = body_state[0:3]
    velocity = body_state[3:6]
    spin = body_state[6:9]
    inv_mass = body_inertia[0:1]
    moment = body_inertia[1:4]
    force_sum = totals[0:3]
    moment_sum = totals[3:6]
    torque = moment_sum - cross(center, force_sum)
    down = jnp.array([0.0, 0.0, -gravity], jnp.float32)[:, None]
    new_vel = velocity + time_step * (inv_mass * force_sum + down)
    new_spin = spin + time_step * (torque - cross(spin, moment * spin)) / moment
    new_center = center + time_step * new_vel
    return (jnp.concatenate([new_center, new_vel, new_spin], axis=0),
            jnp.concatenate([center, new_vel, new_spin], axis=0))


def reference(soil_state, tile_count, tile_neighbors, marker_pos, marker_vel, marker_tile, marker_owner, marker_slot, body_state, body_inertia):
    live_mask = (lax.broadcasted_iota(jnp.int32, (NZT, NHT, TP), 2) < tile_count[:, :, None]).astype(jnp.float32)
    packed = jnp.concatenate([soil_state, live_mask[:, :, None, :]], axis=2)
    padded = jnp.pad(packed, ((1, 1), (1, 1), (0, 0), (0, 0))).reshape(((NZT + 2) * (NHT + 2), 7, TP))
    layer_ids = lax.broadcasted_iota(jnp.int32, (NZT, NHT, NEIGH), 0)
    column_ids = lax.broadcasted_iota(jnp.int32, (NZT, NHT, NEIGH), 1)
    nbr_ids = ((layer_ids + tile_neighbors // 3) * (NHT + 2) + column_ids + tile_neighbors % 3).astype(jnp.int32)
    tile_total = NZT * NHT
    block_size = math.gcd(tile_total, 64)
    own_tiles = packed.reshape((tile_total // block_size, block_size, 7, TP))
    grouped_ids = nbr_ids.reshape((tile_total // block_size, block_size, NEIGH))
    density = lax.map(lambda operands: block_density(operands[0], operands[1], padded), (own_tiles, grouped_ids))
    density = density.reshape((NZT, NHT, TP))
    extra_rows = jnp.stack([stiffness * (density - rest_density) / (density * density), 1.0 / density], axis=2)
    extra_padded = jnp.pad(extra_rows, ((1, 1), (1, 1), (0, 0), (0, 0))).reshape(((NZT + 2) * (NHT + 2), 2, TP))
    accel_out = lax.map(lambda operands: block_accel(operands[0], operands[1], operands[2], padded, extra_padded),
                        (own_tiles, extra_rows.reshape((tile_total // block_size, block_size, 2, TP)), grouped_ids))
    soil_accel = accel_out.reshape((NZT, NHT, 3, TP))

    marker_ids = jnp.arange(MARKERS, dtype=jnp.int32)
    device_ids = marker_ids // MKD
    layer_of = (device_ids % DEPTH_DEVS) * ZL + marker_tile // HL
    column_of = (device_ids // DEPTH_DEVS) * HL + marker_tile % HL
    source_ids = (layer_of * NHT + column_of).astype(jnp.int32)
    source_table = jnp.concatenate([packed, extra_rows], axis=2).reshape((tile_total, 9, TP))
    marker_block = math.gcd(MARKERS, 1024)
    blocks = MARKERS // marker_block
    forces = lax.map(lambda operands: marker_force(operands[0], operands[1], source_table[operands[2]]),
                     (marker_pos.T.reshape((blocks, marker_block, 3)), marker_vel.T.reshape((blocks, marker_block, 3)),
                      source_ids.reshape((blocks, marker_block))))
    forces = forces.reshape((MARKERS, 3)).T
    moments = cross(marker_pos, forces)
    body_ids = (marker_owner[:, 0] * BODY_TILE + marker_slot).astype(jnp.int32)
    totals = jax.ops.segment_sum(jnp.concatenate([forces, moments], axis=0).T, body_ids, num_segments=BODIES).T
    body_next, refresh = advance(totals, body_state, body_inertia)
    picked = refresh[:, body_ids]
    lever = marker_pos - picked[0:3]
    marker_vel_next = picked[3:6] + cross(picked[6:9], lever)
    return soil_accel, body_next, marker_vel_next
```

```python
import functools

import jax
import jax.numpy as jnp
from jax import lax
from jax.experimental import pallas as pl
from jax.experimental.pallas import tpu as pltpu
from jax.sharding import PartitionSpec as P

stiffness = 40.0
rest_density = 2.0
viscosity = 20.0
time_step = 0.05
gravity = 1.0
VMEM = pltpu.VMEM
SMEM = pltpu.SMEM
TP = 128
ROWS = 16


def vspec():
    return pl.BlockSpec(memory_space=VMEM)


def with_halo(shard, sides):
    for axis, dim in sides:
        size, length = (lax.axis_size(axis), shard.shape[dim])
        up = [(i, (i + 1) % size) for i in range(size - 1)]
        down = [(j, i) for i, j in up]
        last = lax.slice_in_dim(shard, length - 1, length, axis=dim)
        first = lax.slice_in_dim(shard, 0, 1, axis=dim)
        before = lax.ppermute(last, axis, up)
        after = lax.ppermute(first, axis, down)
        shard = jnp.concatenate([before, shard, after], axis=dim)
    return shard


def neighbor_id(codes, layer, column, entry, width):
    code = codes[layer, column, entry]
    down = (code * 11) >> 5
    return (layer + down) * width + column + code - 3 * down


def rows_of(ref, ident, row, count):
    return jnp.broadcast_to(ref[ident, row : row + 1, :], (count, TP))


def to_row(column_sums, eye):
    return jnp.sum(jnp.where(eye, column_sums, 0.0), axis=0, keepdims=True)


def density_kernel(codes, own, ext, out, *, columns):
    eye = lax.broadcasted_iota(jnp.int32, (TP, TP), 0) == lax.broadcasted_iota(
        jnp.int32, (TP, TP), 1
    )

    def tile_step(tile, carry):
        layer, column = tile // columns, tile % columns
        idents = [neighbor_id(codes, layer, column, k, columns + 2) for k in range(6)]
        mine = own[layer, column]
        cols = jnp.transpose(mine)
        sums = []
        for block in range(TP // ROWS):
            here = cols[block * ROWS : (block + 1) * ROWS]
            place = [jnp.broadcast_to(here[:, c : c + 1], (ROWS, TP)) for c in range(3)]
            total = jnp.zeros((ROWS, TP), jnp.float32)
            for ident in idents:
                distance = None
                for c in range(3):
                    offset = place[c] - rows_of(ext, ident, c, ROWS)
                    square = offset * offset
                    distance = square if distance is None else distance + square
                total = total + rows_of(ext, ident, 6, ROWS) * jnp.exp(-distance)
            sums.append(jnp.sum(total, axis=1, keepdims=True))
        summed = to_row(jnp.concatenate(sums, axis=0), eye)
        density = 1.0 + summed / TP
        press = (2.0 * stiffness) * (density - rest_density) / (density * density)
        damp = viscosity / density
        live = mine[6:7]
        out[layer, column] = jnp.concatenate(
            [press, damp, press * live, damp * live, jnp.zeros((4, TP), jnp.float32)], axis=0
        )
        return carry

    lax.fori_loop(0, own.shape[0] * columns, tile_step, 0)


def accel_kernel(codes, own, extra, ext, ext_extra, out, *, columns):
    eye = lax.broadcasted_iota(jnp.int32, (TP, TP), 0) == lax.broadcasted_iota(
        jnp.int32, (TP, TP), 1
    )

    def tile_step(tile, carry):
        layer, column = tile // columns, tile % columns
        idents = [neighbor_id(codes, layer, column, k, columns + 2) for k in range(6)]
        mine = own[layer, column]
        cols = jnp.transpose(mine)
        more = jnp.transpose(extra[layer, column])
        sums = [[], [], []]
        for block in range(TP // ROWS):
            span = slice(block * ROWS, (block + 1) * ROWS)
            here = cols[span]
            place = [jnp.broadcast_to(here[:, c : c + 1], (ROWS, TP)) for c in range(3)]
            speed = [jnp.broadcast_to(here[:, 3 + c : 4 + c], (ROWS, TP)) for c in range(3)]
            press_here = jnp.broadcast_to(more[span, 0:1], (ROWS, TP))
            total = [jnp.zeros((ROWS, TP), jnp.float32) for c in range(3)]
            for ident in idents:
                offsets = [place[c] - rows_of(ext, ident, c, ROWS) for c in range(3)]
                distance = offsets[0] * offsets[0] + offsets[1] * offsets[1]
                distance = distance + offsets[2] * offsets[2]
                weight = rows_of(ext, ident, 6, ROWS) * jnp.exp(-distance)
                press = weight * (press_here + rows_of(ext_extra, ident, 0, ROWS))
                damp = weight * rows_of(ext_extra, ident, 1, ROWS)
                for c in range(3):
                    relative = rows_of(ext, ident, 3 + c, ROWS) - speed[c]
                    total[c] = total[c] + (press * offsets[c] + damp * relative)
            for c in range(3):
                sums[c].append(jnp.sum(total[c], axis=1, keepdims=True))
        scale = mine[6:7] * (1.0 / TP)
        for c in range(3):
            row = to_row(jnp.concatenate(sums[c], axis=0), eye)
            out[layer, column, c : c + 1, :] = row * scale
        return carry

    lax.fori_loop(0, own.shape[0] * columns, tile_step, 0)


def marker_kernel(own, extra, place, speed, tiles, owners, slots, out, table, terms):
    layers, columns = own.shape[0], own.shape[1]
    count = layers * columns
    blocks = place.shape[1] // TP
    owner_count = out.shape[0]
    states = own[...].reshape((count, 8, TP))
    extras = extra[...].reshape((count, 8, TP))
    blank = jnp.zeros((TP - count, TP), jnp.float32)
    for field in range(8):
        part = states[:, field, :] if field < 6 else extras[:, field - 4, :]
        table[field] = jnp.transpose(jnp.concatenate([part, blank], axis=0))

    def block_step(block, carry):
        lanes = pl.ds(pl.multiple_of(block * TP, TP), TP)
        which = jnp.broadcast_to(tiles[pl.ds(block, 1), :], (8, TP))
        y = place[:, lanes]
        u = speed[:, lanes]
        at = [jnp.broadcast_to(y[c : c + 1], (8, TP)) for c in range(3)]
        moving = [jnp.broadcast_to(u[c : c + 1], (8, TP)) for c in range(3)]
        total = [jnp.zeros((8, TP), jnp.float32) for c in range(3)]
        for group in range(TP // 8):
            span = slice(group * 8, group * 8 + 8)
            fields = [
                jnp.take_along_axis(table[field, span, :], which, axis=1) for field in range(8)
            ]
            offsets = [at[c] - fields[c] for c in range(3)]
            distance = offsets[0] * offsets[0] + offsets[1] * offsets[1]
            distance = distance + offsets[2] * offsets[2]
            weight = jnp.exp(-distance)
            press = weight * fields[6]
            damp = weight * fields[7]
            for c in range(3):
                total[c] = total[c] + (press * offsets[c] + damp * (fields[3 + c] - moving[c]))
        force = [jnp.sum(total[c], axis=0, keepdims=True) * (1.0 / TP) for c in range(3)]
        where = [y[c : c + 1] for c in range(3)]
        moment = [
            where[1] * force[2] - where[2] * force[1],
            where[2] * force[0] - where[0] * force[2],
            where[0] * force[1] - where[1] * force[0],
        ]
        terms[:, lanes] = jnp.concatenate(
            force + moment + [jnp.zeros((2, TP), jnp.float32)], axis=0
        )
        return carry

    lax.fori_loop(0, blocks, block_step, 0)
    out[...] = jnp.zeros(out.shape, jnp.float32)
    wide = 2

    def sum_step(step, carry):
        left, right = [], []
        for part in range(wide):
            block = step * wide + part
            lanes = pl.ds(pl.multiple_of(block * TP, TP), TP)
            value = terms[:, lanes]
            high = value.astype(jnp.bfloat16).astype(jnp.float32)
            low = value - high
            owner = jnp.broadcast_to(owners[pl.ds(block, 1), :], (8, TP))
            slot = jnp.broadcast_to(slots[pl.ds(block, 1), :], (TP, TP))
            hot = (slot == lax.broadcasted_iota(jnp.int32, (TP, TP), 0)).astype(jnp.bfloat16)
            masks = [owner == o for o in range(owner_count)]
            for piece in (high, low):
                left.append(
                    jnp.concatenate(
                        [jnp.where(mask, piece, 0.0) for mask in masks], axis=0
                    ).astype(jnp.bfloat16)
                )
                right.append(hot)
        summed = lax.dot_general(
            jnp.concatenate(left, axis=1),
            jnp.concatenate(right, axis=1),
            (((1,), (1,)), ((), ())),
            preferred_element_type=jnp.float32,
        )
        out[...] = out[...] + summed.reshape(out.shape)
        return carry

    lax.fori_loop(0, blocks // wide, sum_step, 0)


def share_kernel(blocks, out):
    out[...] = jnp.sum(blocks[...], axis=0)


def cross(a, b):
    return [
        a[1] * b[2] - a[2] * b[1],
        a[2] * b[0] - a[0] * b[2],
        a[0] * b[1] - a[1] * b[0],
    ]


def advance_kernel(first, second, third, fourth, state, inertia, out, sent):
    totals = (first[...] + second[...]) + (third[...] + fourth[...])
    row = lambda ref, r: ref[r : r + 1, :]
    force = [totals[c : c + 1] for c in range(3)]
    moments = [totals[3 + c : 4 + c] for c in range(3)]
    center = [row(state, c) for c in range(3)]
    velocity = [row(state, 3 + c) for c in range(3)]
    spin = [row(state, 6 + c) for c in range(3)]
    inv_mass = row(inertia, 0)
    moment = [row(inertia, 1 + c) for c in range(3)]
    arm = cross(center, force)
    gyro = cross(spin, [moment[c] * spin[c] for c in range(3)])
    pull = [0.0, 0.0, -gravity]
    new_vel = [velocity[c] + time_step * (inv_mass * force[c] + pull[c]) for c in range(3)]
    new_spin = [
        spin[c] + time_step * ((moments[c] - arm[c]) - gyro[c]) / moment[c] for c in range(3)
    ]
    new_center = [center[c] + time_step * new_vel[c] for c in range(3)]
    out[...] = jnp.concatenate(new_center + new_vel + new_spin, axis=0)
    swing = cross(new_spin, center)
    base = [new_vel[c] - swing[c] for c in range(3)]
    block = jnp.concatenate(base + new_spin + [jnp.zeros((2, TP), jnp.float32)], axis=0)
    sent[...] = jnp.broadcast_to(block[None], sent.shape)


def pick_kernel(states, place, owners, slots, out):
    blocks = place.shape[1] // TP

    def block_step(block, carry):
        lanes = pl.ds(pl.multiple_of(block * TP, TP), TP)
        slot = jnp.broadcast_to(slots[pl.ds(block, 1), :], (8, TP))
        owner = jnp.broadcast_to(owners[pl.ds(block, 1), :], (8, TP))
        picked = jnp.zeros((8, TP), jnp.float32)
        for o in range(states.shape[0]):
            found = jnp.take_along_axis(states[o], slot, axis=1)
            picked = jnp.where(owner == o, found, picked)
        y = place[:, lanes]
        turn = cross([picked[3 + c : 4 + c] for c in range(3)], [y[c : c + 1] for c in range(3)])
        out[:, lanes] = picked[0:3] + jnp.concatenate(turn, axis=0)
        return carry

    lax.fori_loop(0, blocks, block_step, 0)


def cost(flops, moved, heavy=0):
    return pl.CostEstimate(flops=flops, bytes_accessed=moved, transcendentals=heavy)


def local(
    soil_state,
    tile_count,
    tile_neighbors,
    marker_pos,
    marker_vel,
    marker_tile,
    marker_owner,
    marker_slot,
    body_state,
    body_inertia,
):
    layers, columns, fields, tile_size = soil_state.shape
    marker_count = marker_pos.shape[1]
    tile_devs = lax.axis_size("tile")
    depth_devs = lax.axis_size("depth")
    f32 = jnp.float32
    smem = pl.BlockSpec(memory_space=SMEM)
    live = (
        lax.broadcasted_iota(jnp.int32, (layers, columns, 1, tile_size), 3)
        < tile_count[:, :, None, None]
    ).astype(f32)
    packed = jnp.concatenate(
        [soil_state, live, jnp.zeros((layers, columns, 1, tile_size), f32)], axis=2
    )
    sides = (("tile", 1), ("depth", 0))
    ext_count = (layers + 2) * (columns + 2)
    ext = with_halo(packed, sides).reshape((ext_count, 8, tile_size))
    pairs = layers * columns * 6 * tile_size * tile_size
    extra = pl.pallas_call(
        functools.partial(density_kernel, columns=columns),
        out_shape=jax.ShapeDtypeStruct((layers, columns, 8, tile_size), f32),
        in_specs=[smem, vspec(), vspec()],
        out_specs=vspec(),
        cost_estimate=cost(pairs * 12, 1 << 18, pairs),
        name="density",
    )(tile_neighbors, packed, ext)
    owners = marker_owner.reshape((marker_count // TP, TP))
    slots = marker_slot.reshape((marker_count // TP, TP))
    tiles = marker_tile.reshape((marker_count // TP, TP))
    partial_sums = pl.pallas_call(
        marker_kernel,
        out_shape=jax.ShapeDtypeStruct((tile_devs, 8, TP), f32),
        in_specs=[vspec()] * 7,
        out_specs=vspec(),
        scratch_shapes=[VMEM((8, TP, TP), f32), VMEM((8, marker_count), f32)],
        cost_estimate=cost(marker_count * TP * 25, 1 << 19, marker_count * TP),
        name="markers",
    )(packed, extra, marker_pos, marker_vel, tiles, owners, slots)
    arrived = lax.all_to_all(partial_sums, "tile", 0, 0, tiled=True)
    ext_extra = with_halo(extra, sides).reshape((ext_count, 8, tile_size))
    soil_accel = pl.pallas_call(
        functools.partial(accel_kernel, columns=columns),
        out_shape=jax.ShapeDtypeStruct((layers, columns, 3, tile_size), f32),
        in_specs=[smem] + [vspec()] * 4,
        out_specs=vspec(),
        cost_estimate=cost(pairs * 30, 1 << 19, pairs),
        name="accel",
    )(tile_neighbors, packed, extra, ext, ext_extra)
    share = pl.pallas_call(
        share_kernel,
        out_shape=jax.ShapeDtypeStruct((8, TP), f32),
        in_specs=[vspec()],
        out_specs=vspec(),
        name="share",
    )(arrived)
    others = [
        lax.ppermute(share, "depth", [(i, (i + k) % depth_devs) for i in range(depth_devs)])
        for k in range(1, depth_devs)
    ]
    body_next, sent = pl.pallas_call(
        advance_kernel,
        out_shape=(
            jax.ShapeDtypeStruct((9, TP), f32),
            jax.ShapeDtypeStruct((tile_devs, 8, TP), f32),
        ),
        in_specs=[vspec()] * 6,
        out_specs=(vspec(), vspec()),
        name="advance",
    )(share, *others, body_state, body_inertia)
    states = lax.all_to_all(sent, "tile", 0, 0, tiled=True)
    marker_vel_next = pl.pallas_call(
        pick_kernel,
        out_shape=jax.ShapeDtypeStruct((3, marker_count), f32),
        in_specs=[vspec()] * 4,
        out_specs=vspec(),
        name="pick",
    )(states, marker_pos, owners, slots)
    return (soil_accel, body_next, marker_vel_next)


def solution(mesh):
    placed = (
        P("depth", "tile", None, None),
        P("depth", "tile"),
        P("depth", "tile", None),
        P(None, ("tile", "depth")),
        P(None, ("tile", "depth")),
        P(("tile", "depth")),
        P(("tile", "depth"), None),
        P(("tile", "depth")),
        P(None, "tile"),
        P(None, "tile"),
    )
    return jax.shard_map(
        local,
        mesh=mesh,
        in_specs=placed,
        out_specs=(P("depth", "tile", None, None), P(None, "tile"), P(None, ("tile", "depth"))),
        check_vma=False,
    )
```

```python
import functools

import jax
import jax.numpy as jnp
from jax import lax
from jax.experimental import pallas as pl
from jax.experimental.pallas import tpu as pltpu
from jax.sharding import PartitionSpec as P

stiffness = 40.0
rest_density = 2.0
viscosity = 20.0
time_step = 0.05
gravity = 1.0
VMEM = pltpu.VMEM
SMEM = pltpu.SMEM
TP = 128
ROWS = 16
AUG = 48
FACTORS = 80
SCALE = (2.0 * 1.4426950408889634) ** 0.5
FAR = 1e30
PLACE_LIMIT = 4.0
SPEED_LIMIT = 256.0
F32 = jnp.float32
BF16 = jnp.bfloat16
NT = (((1,), (1,)), ((), ()))


def vspec():
    return pl.BlockSpec(memory_space=VMEM)


def sspec():
    return pl.BlockSpec(memory_space=SMEM)


def params(limit=16 << 20):
    return pltpu.CompilerParams(vmem_limit_bytes=limit)


def cost(flops, moved, heavy=0):
    return pl.CostEstimate(flops=flops, bytes_accessed=moved, transcendentals=heavy)


def row_mask():
    return lax.broadcasted_iota(jnp.int32, (8, TP), 0)


def eye_mask():
    return lax.broadcasted_iota(jnp.int32, (TP, TP), 0) == lax.broadcasted_iota(
        jnp.int32, (TP, TP), 1
    )


def split3(value):
    high = value.astype(BF16).astype(F32)
    rest = value - high
    middle = rest.astype(BF16).astype(F32)
    return high, middle, rest - middle


def augmented(raw, source):
    row = row_mask()
    scaled = raw * SCALE
    square = scaled * scaled
    norm = -0.5 * (square[0:1] + square[1:2] + square[2:3])
    if source:
        third, fourth = norm + (raw[6:7] - 1.0) * FAR, jnp.ones((1, TP), F32)
    else:
        third, fourth = jnp.ones((1, TP), F32), norm
    full = jnp.where(
        row < 3, scaled, jnp.where(row == 3, third, jnp.where(row == 4, fourth, 0.0))
    )
    h, m, l = split3(full)
    return jnp.concatenate([h, m, h, m, l, h] if source else [h, h, m, m, h, l], axis=0)


def assemble(own, west, east, up, down, ext):
    layers, columns = own.shape[0], own.shape[1]
    ext[0:2] = up[...]
    ext[layers + 2 : layers + 4] = down[...]
    ext[2 : layers + 2, 0:2] = west[...]
    ext[2 : layers + 2, columns + 2 : columns + 4] = east[...]
    ext[2 : layers + 2, 2 : columns + 2] = own[...]


def moderate(ext):
    span, width = ext.shape[0], ext.shape[1]
    flat = ext[...].reshape((span * width, 8, TP))
    peak = jnp.max(jnp.abs(flat), axis=0)
    row = row_mask()
    ratio = jnp.where(
        row < 3, peak / PLACE_LIMIT, jnp.where(row < 6, peak / SPEED_LIMIT, 0.0)
    )
    return jnp.max(ratio) <= 1.0


def near(codes, layer, column, row, col):
    places = []
    for k in range(6):
        code = codes[k, layer, column]
        down = (code * 11) >> 5
        places.append((row + down - 1, col + code - 3 * down - 1))
    return places


def to_row(total, eye):
    sums = jnp.sum(total, axis=1, keepdims=True)
    return jnp.sum(jnp.where(eye, sums, 0.0), axis=0, keepdims=True)


def fast_weights(left, btab, places):
    weights = []
    for p in range(3):
        right = jnp.concatenate([btab[places[2 * p]], btab[places[2 * p + 1]]], axis=1)
        weights.append(
            jnp.exp2(lax.dot_general(left, right, (((1,), (0,)), ((), ())), preferred_element_type=F32))
        )
    return weights


def fast_sum(left, btab, places, eye):
    total = None
    for weight in fast_weights(left, btab, places):
        part = weight[:, 0:TP] + weight[:, TP : 2 * TP]
        total = part if total is None else total + part
    return to_row(total, eye)


def rows_of(ref, place, row, count):
    return jnp.broadcast_to(ref[place[0], place[1], row : row + 1, :], (count, TP))


def slow_sum(ext, row, col, places, eye):
    cols = jnp.transpose(ext[row, col])
    sums = []
    for block in range(TP // ROWS):
        here = cols[block * ROWS : (block + 1) * ROWS]
        spot = [jnp.broadcast_to(here[:, c : c + 1], (ROWS, TP)) for c in range(3)]
        total = jnp.zeros((ROWS, TP), F32)
        for place in places:
            distance = None
            for c in range(3):
                offset = spot[c] - rows_of(ext, place, c, ROWS)
                square = offset * offset
                distance = square if distance is None else distance + square
            total = total + rows_of(ext, place, 6, ROWS) * jnp.exp(-distance)
        sums.append(jnp.sum(total, axis=1, keepdims=True))
    return jnp.sum(jnp.where(eye, jnp.concatenate(sums, axis=0), 0.0), axis=0, keepdims=True)


def slow_accel(ext, press_ref, damp_ref, row, col, places, eye):
    cols = jnp.transpose(ext[row, col])
    more = jnp.transpose(
        jnp.broadcast_to(press_ref[row - 1, pl.ds(col - 1, 1), :], (8, TP))
    )
    sums = [[], [], []]
    for block in range(TP // ROWS):
        span = slice(block * ROWS, (block + 1) * ROWS)
        here = cols[span]
        spot = [jnp.broadcast_to(here[:, c : c + 1], (ROWS, TP)) for c in range(3)]
        speed = [jnp.broadcast_to(here[:, 3 + c : 4 + c], (ROWS, TP)) for c in range(3)]
        press_here = jnp.broadcast_to(more[span, 0:1], (ROWS, TP))
        total = [jnp.zeros((ROWS, TP), F32) for c in range(3)]
        for place in places:
            offsets = [spot[c] - rows_of(ext, place, c, ROWS) for c in range(3)]
            distance = offsets[0] * offsets[0] + offsets[1] * offsets[1]
            distance = distance + offsets[2] * offsets[2]
            weight = rows_of(ext, place, 6, ROWS) * jnp.exp(-distance)
            there = (place[0] - 1, pl.ds(place[1] - 1, 1), slice(None))
            press = weight * (press_here + jnp.broadcast_to(press_ref[there], (ROWS, TP)))
            damp = weight * jnp.broadcast_to(damp_ref[there], (ROWS, TP))
            for c in range(3):
                relative = rows_of(ext, place, 3 + c, ROWS) - speed[c]
                total[c] = total[c] + (press * offsets[c] + damp * relative)
        for c in range(3):
            sums[c].append(jnp.sum(total[c], axis=1, keepdims=True))
    return [
        jnp.sum(jnp.where(eye, jnp.concatenate(part, axis=0), 0.0), axis=0, keepdims=True)
        for part in sums
    ]


def state_of(summed):
    density = 1.0 + summed * (1.0 / TP)
    press = (2.0 * stiffness) * (density - rest_density) / (density * density)
    return press, viscosity / density


def fill_sources(ext, btab, first, last, left, right):
    def step(index, carry):
        row, col = first + index // (right - left), left + index % (right - left)
        btab[row, col] = augmented(ext[row, col], True).astype(BF16)
        return carry

    lax.fori_loop(0, (last - first) * (right - left), step, 0, unroll=4)


def left_of(ext, row, col):
    return jnp.transpose(augmented(ext[row, col], False)).astype(BF16)


def prep_kernel(counts, codes, soil, out):
    layers, columns = out.shape[0], out.shape[1]
    lane = lax.broadcasted_iota(jnp.int32, (1, TP), 1)
    for layer in range(layers):
        for column in range(columns):
            listed = jnp.zeros((1, TP), jnp.int32)
            for k in range(6):
                listed = jnp.where(lane == k, codes[k, layer, column], listed)
            live = jnp.where(lane < counts[layer, column], 1.0, 0.0)
            rows = [soil[layer, c, column : column + 1, :] for c in range(6)]
            out[layer, column] = jnp.concatenate(rows + [live, listed.astype(F32)], axis=0)


def density_kernel(codes, own, west, east, up, down, out, ext, btab, sums, lives):
    layers, columns = own.shape[0], own.shape[1]
    assemble(own, west, east, up, down, ext)
    eye = eye_mask()
    fast = moderate(ext)

    @pl.when(fast)
    def _():
        fill_sources(ext, btab, 1, layers + 3, 1, columns + 3)

        def step(pair, carry):
            for half in range(2):
                tile = pair * 2 + half
                layer, column = tile // columns, tile % columns
                places = near(codes, layer, column, layer + 2, column + 2)
                left = left_of(ext, layer + 2, column + 2)
                sums[pl.ds(tile, 1), :] = fast_sum(left, btab, places, eye)
            return carry

        lax.fori_loop(0, layers * columns // 2, step, 0)

    @pl.when(jnp.logical_not(fast))
    def _():
        def step(tile, carry):
            layer, column = tile // columns, tile % columns
            places = near(codes, layer, column, layer + 2, column + 2)
            sums[pl.ds(tile, 1), :] = slow_sum(ext, layer + 2, column + 2, places, eye)
            return carry

        lax.fori_loop(0, layers * columns, step, 0)

    for layer in range(layers):
        for column in range(columns):
            tile = layer * columns + column
            lives[tile : tile + 1, :] = own[layer, column, 6:7, :]
    press, damp = state_of(sums[...])
    live = lives[...]
    out[0] = press
    out[1] = damp
    out[2] = press * live
    out[3] = damp * live


def accel_kernel(
    codes, own, west, east, up, down, extra, out, ext, btab, ftab, press_ref, damp_ref
):
    layers, columns = own.shape[0], own.shape[1]
    assemble(own, west, east, up, down, ext)
    eye = eye_mask()
    fast = moderate(ext)
    for layer in range(layers):
        span = slice(layer * columns, (layer + 1) * columns)
        press_ref[layer + 1, 1 : columns + 1, :] = extra[0, span, :]
        damp_ref[layer + 1, 1 : columns + 1, :] = extra[1, span, :]

    def ring(handle):
        def across(index, carry):
            handle(1, index + 1)
            handle(layers + 2, index + 1)
            return carry

        def along(index, carry):
            handle(index + 2, 1)
            handle(index + 2, columns + 2)
            return carry

        lax.fori_loop(0, columns + 2, across, 0)
        lax.fori_loop(0, layers, along, 0)

    def keep(row, col, summed):
        press, damp = state_of(summed)
        press_ref[row - 1, pl.ds(col - 1, 1), :] = press
        damp_ref[row - 1, pl.ds(col - 1, 1), :] = damp

    @pl.when(fast)
    def _():
        fill_sources(ext, btab, 0, layers + 4, 0, columns + 4)

        def ring_sum(row, col):
            places = near(codes, row, col, row, col)
            keep(row, col, fast_sum(left_of(ext, row, col), btab, places, eye))

        ring(ring_sum)

        def factors(index, carry):
            row, col = 1 + index // (columns + 2), 1 + index % (columns + 2)
            raw = ext[row, col]
            press = jnp.broadcast_to(press_ref[row - 1, pl.ds(col - 1, 1), :], (8, TP))
            damp = jnp.broadcast_to(damp_ref[row - 1, pl.ds(col - 1, 1), :], (8, TP))
            value = jnp.concatenate([raw, press * raw, damp * raw], axis=0)
            parts = split3(value)
            ftab[row, col] = jnp.concatenate(
                list(parts) + [jnp.zeros((FACTORS - 72, TP), F32)], axis=0
            ).astype(BF16)
            return carry

        lax.fori_loop(0, (layers + 2) * (columns + 2), factors, 0, unroll=2)

        def step(pair, carry):
            for half in range(2):
                tile = pair * 2 + half
                layer, column = tile // columns, tile % columns
                row, col = layer + 2, column + 2
                places = near(codes, row, col, row, col)
                weights = fast_weights(left_of(ext, row, col), btab, places)
                highs = [w.astype(BF16) for w in weights]
                lows = [(w - h.astype(F32)).astype(BF16) for w, h in zip(weights, highs)]
                sources = [ftab[place] for place in places]
                summed = lax.dot_general(
                    jnp.concatenate(sources + sources, axis=1),
                    jnp.concatenate(highs + lows, axis=1),
                    NT,
                    preferred_element_type=F32,
                )
                summed = summed[0:24] + summed[24:48] + summed[48:72]
                plain, pressed, damped = summed[0:8], summed[8:16], summed[16:24]
                raw = ext[row, col]
                press = press_ref[row - 1, pl.ds(col - 1, 1), :]
                push = raw * (press * plain[6:7] + pressed[6:7]) - (press * plain + pressed)
                drag = damped - raw * damped[6:7]
                total = (push[0:3] + drag[3:6]) * (raw[6:7] * (1.0 / TP))
                for c in range(3):
                    out[layer, c, pl.ds(column, 1), :] = total[c : c + 1]
            return carry

        lax.fori_loop(0, layers * columns // 2, step, 0)

    @pl.when(jnp.logical_not(fast))
    def _():
        def ring_sum(row, col):
            places = near(codes, row, col, row, col)
            keep(row, col, slow_sum(ext, row, col, places, eye))

        ring(ring_sum)

        def step(tile, carry):
            layer, column = tile // columns, tile % columns
            row, col = layer + 2, column + 2
            places = near(codes, row, col, row, col)
            rows = slow_accel(ext, press_ref, damp_ref, row, col, places, eye)
            scale = ext[row, col, 6:7, :] * (1.0 / TP)
            for c in range(3):
                out[layer, c, pl.ds(column, 1), :] = rows[c] * scale
            return carry

        lax.fori_loop(0, layers * columns, step, 0)


def marker_kernel(soil, extra, place, speed, tiles, owners, slots, out, table):
    layers, columns = soil.shape[0], soil.shape[2]
    count = layers * columns
    pairs = place.shape[1] // (2 * TP)
    owner_count = out.shape[0]
    groups = TP // 16
    for field in range(8):
        if field < 6:
            part = jnp.concatenate([soil[layer, field] for layer in range(layers)], axis=0)
        else:
            part = extra[field - 4]
        pieces = list(split3(part)) + [jnp.zeros((TP - 3 * count, TP), F32)]
        turned = jnp.transpose(jnp.concatenate(pieces, axis=0)).astype(BF16)
        for group in range(groups):
            at = group * TP + field * 16
            table[at : at + 16, :] = turned[group * 16 : group * 16 + 16]
    entry = lax.broadcasted_iota(jnp.int32, (TP, TP), 0)
    listed = jnp.where(entry < 3 * count, lax.rem(entry, count), -1)
    out[...] = jnp.zeros(out.shape, F32)

    def add_terms(pair, terms):
        left, right = [], []
        for part in range(2):
            block = pair * 2 + part
            high = terms[part].astype(BF16).astype(F32)
            low = terms[part] - high
            owner = jnp.broadcast_to(owners[pl.ds(block, 1), :], (8, TP))
            slot = jnp.broadcast_to(slots[pl.ds(block, 1), :], (TP, TP))
            hot = jnp.where(slot == entry, 1.0, 0.0).astype(BF16)
            masks = [owner == o for o in range(owner_count)]
            for piece in (high, low):
                left.append(
                    jnp.concatenate(
                        [jnp.where(mask, piece, 0.0) for mask in masks], axis=0
                    ).astype(BF16)
                )
                right.append(hot)
        summed = lax.dot_general(
            jnp.concatenate(left, axis=1),
            jnp.concatenate(right, axis=1),
            NT,
            preferred_element_type=F32,
        )
        out[...] = out[...] + summed.reshape(out.shape)

    def forces_on(block):
        lanes = pl.ds(pl.multiple_of(block * TP, TP), TP)
        which = jnp.broadcast_to(tiles[pl.ds(block, 1), :], (TP, TP))
        hot = jnp.where(which == listed, 1.0, 0.0).astype(BF16)
        y = place[:, lanes]
        u = speed[:, lanes]
        at = [jnp.broadcast_to(y[c : c + 1], (16, TP)) for c in range(3)]
        total = [jnp.zeros((16, TP), F32) for c in range(3)]
        drag = jnp.zeros((16, TP), F32)
        for group in range(groups):
            picked = lax.dot_general(
                table[group * TP : (group + 1) * TP, :],
                hot,
                (((1,), (0,)), ((), ())),
                preferred_element_type=F32,
            )
            fields = [picked[16 * field : 16 * field + 16] for field in range(8)]
            offsets = [at[c] - fields[c] for c in range(3)]
            distance = offsets[0] * offsets[0] + offsets[1] * offsets[1]
            distance = distance + offsets[2] * offsets[2]
            weight = jnp.exp2(distance * (-0.5 * SCALE * SCALE))
            press = weight * fields[6]
            damp = weight * fields[7]
            drag = drag + damp
            for c in range(3):
                total[c] = total[c] + (press * offsets[c] + damp * fields[3 + c])
        slowed = jnp.sum(drag, axis=0, keepdims=True)
        force = [
            (jnp.sum(total[c], axis=0, keepdims=True) - u[c : c + 1] * slowed) * (1.0 / TP)
            for c in range(3)
        ]
        where = [y[c : c + 1] for c in range(3)]
        moment = cross(where, force)
        return jnp.concatenate(force + moment + [jnp.zeros((2, TP), F32)], axis=0)

    def step(pair, terms):
        add_terms(jnp.maximum(pair - 1, 0), terms)
        return (forces_on(pair * 2), forces_on(pair * 2 + 1))

    blank = jnp.zeros((8, TP), F32)
    terms = lax.fori_loop(0, pairs, step, (blank, blank))
    add_terms(pairs - 1, terms)


def cross(a, b):
    return [
        a[1] * b[2] - a[2] * b[1],
        a[2] * b[0] - a[0] * b[2],
        a[0] * b[1] - a[1] * b[0],
    ]


def advance_kernel(first, second, third, fourth, state, inertia, out, sent):
    totals = (first[...] + second[...]) + (third[...] + fourth[...])
    row = lambda ref, r: ref[r : r + 1, :]
    force = [totals[c : c + 1] for c in range(3)]
    moments = [totals[3 + c : 4 + c] for c in range(3)]
    center = [row(state, c) for c in range(3)]
    velocity = [row(state, 3 + c) for c in range(3)]
    spin = [row(state, 6 + c) for c in range(3)]
    inv_mass = row(inertia, 0)
    moment = [row(inertia, 1 + c) for c in range(3)]
    arm = cross(center, force)
    gyro = cross(spin, [moment[c] * spin[c] for c in range(3)])
    pull = [0.0, 0.0, -gravity]
    new_vel = [velocity[c] + time_step * (inv_mass * force[c] + pull[c]) for c in range(3)]
    new_spin = [
        spin[c] + time_step * ((moments[c] - arm[c]) - gyro[c]) / moment[c] for c in range(3)
    ]
    new_center = [center[c] + time_step * new_vel[c] for c in range(3)]
    out[...] = jnp.concatenate(new_center + new_vel + new_spin, axis=0)
    swing = cross(new_spin, center)
    base = [new_vel[c] - swing[c] for c in range(3)]
    block = jnp.concatenate(base + new_spin + [jnp.zeros((2, TP), F32)], axis=0)
    sent[...] = jnp.broadcast_to(block[None], sent.shape)


def pick_kernel(states, place, owners, slots, out):
    pairs = place.shape[1] // (2 * TP)
    owner_count = states.shape[0]

    def step(pair, carry):
        for half in range(2):
            block = pair * 2 + half
            lanes = pl.ds(pl.multiple_of(block * TP, TP), TP)
            slot = jnp.broadcast_to(slots[pl.ds(block, 1), :], (8, TP))
            owner = jnp.broadcast_to(owners[pl.ds(block, 1), :], (8, TP))
            found = [jnp.zeros((8, TP), F32) for lane in range(4)]
            for o in range(owner_count):
                here = jnp.take_along_axis(states[o], slot, axis=1)
                found[o % 4] = jnp.where(owner == o, here, found[o % 4])
            picked = (found[0] + found[1]) + (found[2] + found[3])
            y = place[:, lanes]
            turn = cross(
                [picked[3 + c : 4 + c] for c in range(3)], [y[c : c + 1] for c in range(3)]
            )
            out[:, lanes] = picked[0:3] + jnp.concatenate(turn, axis=0)
        return carry

    lax.fori_loop(0, pairs, step, 0)


def shifted(shard, axis, dim, width):
    size, length = lax.axis_size(axis), shard.shape[dim]
    up = [(i, i + 1) for i in range(size - 1)]
    down = [(j, i) for i, j in up]
    last = lax.slice_in_dim(shard, length - width, length, axis=dim)
    first = lax.slice_in_dim(shard, 0, width, axis=dim)
    return lax.ppermute(last, axis, up), lax.ppermute(first, axis, down)


def local(
    soil_state,
    tile_count,
    tile_neighbors,
    marker_pos,
    marker_vel,
    marker_tile,
    marker_owner,
    marker_slot,
    body_state,
    body_inertia,
):
    layers, columns, fields, tile_size = soil_state.shape
    marker_count = marker_pos.shape[1]
    tile_devs = lax.axis_size("tile")
    depth_devs = lax.axis_size("depth")
    soil = jnp.transpose(soil_state, (0, 2, 1, 3))
    codes = jnp.transpose(tile_neighbors, (2, 0, 1))
    own = pl.pallas_call(
        prep_kernel,
        out_shape=jax.ShapeDtypeStruct((layers, columns, 8, TP), F32),
        in_specs=[sspec(), sspec(), vspec()],
        out_specs=vspec(),
        compiler_params=params(),
        name="prep",
    )(tile_count, codes, soil)
    west, east = shifted(own, "tile", 1, 2)
    top = jnp.concatenate([west[:2], own[:2], east[:2]], axis=1)
    bottom = jnp.concatenate([west[-2:], own[-2:], east[-2:]], axis=1)
    rim = jnp.concatenate([top, bottom], axis=0)
    up, down = shifted(rim, "depth", 0, 2)
    pieces = (own, west, east, up, down)
    span, width = layers + 4, columns + 4
    pairs = layers * columns * 6 * TP * TP
    extra = pl.pallas_call(
        density_kernel,
        out_shape=jax.ShapeDtypeStruct((4, layers * columns, TP), F32),
        in_specs=[sspec()] + [vspec()] * 5,
        out_specs=vspec(),
        scratch_shapes=[
            VMEM((span, width, 8, TP), F32),
            VMEM((span, width, AUG, TP), BF16),
            VMEM((layers * columns, TP), F32),
            VMEM((layers * columns, TP), F32),
        ],
        cost_estimate=cost(pairs * 12, 1 << 18, pairs),
        compiler_params=params(),
        name="density",
    )(codes, *pieces)
    owners = marker_owner.reshape((marker_count // TP, TP))
    slots = marker_slot.reshape((marker_count // TP, TP))
    tiles = marker_tile.reshape((marker_count // TP, TP))
    partial_sums = pl.pallas_call(
        marker_kernel,
        out_shape=jax.ShapeDtypeStruct((tile_devs, 8, TP), F32),
        in_specs=[vspec()] * 7,
        out_specs=vspec(),
        scratch_shapes=[VMEM((8 * TP, TP), BF16)],
        cost_estimate=cost(marker_count * TP * 25, 1 << 19, marker_count * TP),
        compiler_params=params(),
        name="markers",
    )(soil, extra, marker_pos, marker_vel, tiles, owners, slots)
    arrived = lax.all_to_all(partial_sums, "tile", 0, 0, tiled=True)
    ring_codes = jnp.concatenate(
        [
            part[:, :, 7, 0:6]
            for part in (up, jnp.concatenate([west, own, east], axis=1), down)
        ],
        axis=0,
    )
    ring_codes = jnp.transpose(ring_codes.astype(jnp.int32), (2, 0, 1))
    accel = pl.pallas_call(
        accel_kernel,
        out_shape=jax.ShapeDtypeStruct((layers, 3, columns, TP), F32),
        in_specs=[sspec()] + [vspec()] * 6,
        out_specs=vspec(),
        scratch_shapes=[
            VMEM((span, width, 8, TP), F32),
            VMEM((span, width, AUG, TP), BF16),
            VMEM((span, width, FACTORS, TP), BF16),
            VMEM((layers + 2, 16, TP), F32),
            VMEM((layers + 2, 16, TP), F32),
        ],
        cost_estimate=cost(pairs * 30, 1 << 19, pairs),
        compiler_params=params(),
        name="accel",
    )(ring_codes, *pieces, extra)
    soil_accel = jnp.transpose(accel, (0, 2, 1, 3))
    share = jnp.sum(arrived, axis=0)
    others = [
        lax.ppermute(share, "depth", [(i, (i + k) % depth_devs) for i in range(depth_devs)])
        for k in range(1, depth_devs)
    ]
    body_next, sent = pl.pallas_call(
        advance_kernel,
        out_shape=(
            jax.ShapeDtypeStruct((9, TP), F32),
            jax.ShapeDtypeStruct((tile_devs, 8, TP), F32),
        ),
        in_specs=[vspec()] * 6,
        out_specs=(vspec(), vspec()),
        compiler_params=params(),
        name="advance",
    )(share, *others, body_state, body_inertia)
    states = lax.all_to_all(sent, "tile", 0, 0, tiled=True)
    marker_vel_next = pl.pallas_call(
        pick_kernel,
        out_shape=jax.ShapeDtypeStruct((3, marker_count), F32),
        in_specs=[vspec()] * 4,
        out_specs=vspec(),
        compiler_params=params(),
        name="pick",
    )(states, marker_pos, owners, slots)
    return (soil_accel, body_next, marker_vel_next)


def solution(mesh):
    placed = (
        P("depth", "tile", None, None),
        P("depth", "tile"),
        P("depth", "tile", None),
        P(None, ("tile", "depth")),
        P(None, ("tile", "depth")),
        P(("tile", "depth")),
        P(("tile", "depth"), None),
        P(("tile", "depth")),
        P(None, "tile"),
        P(None, "tile"),
    )
    return jax.shard_map(
        local,
        mesh=mesh,
        in_specs=placed,
        out_specs=(P("depth", "tile", None, None), P(None, "tile"), P(None, ("tile", "depth"))),
        check_vma=False,
    )
```

```python
import functools

import jax
import jax.numpy as jnp
from jax import lax
from jax.experimental import pallas as pl
from jax.experimental.pallas import tpu as pltpu
from jax.sharding import PartitionSpec as P

stiffness = 40.0
rest_density = 2.0
viscosity = 20.0
time_step = 0.05
gravity = 1.0
VMEM = pltpu.VMEM
SMEM = pltpu.SMEM
TP = 128
ROWS = 16
AUG = 48
FACTORS = 80
TILES = 4
SCALE = (2.0 * 1.4426950408889634) ** 0.5
FAR = 1e30
PLACE_LIMIT = 4.0
CLIP = 1e4
SPEED_LIMIT = 256.0
F32 = jnp.float32
BF16 = jnp.bfloat16
NT = (((1,), (1,)), ((), ()))


def vspec():
    return pl.BlockSpec(memory_space=VMEM)


def sspec():
    return pl.BlockSpec(memory_space=SMEM)


def params(limit=16 << 20):
    return pltpu.CompilerParams(vmem_limit_bytes=limit)


def cost(flops, moved, heavy=0):
    return pl.CostEstimate(flops=flops, bytes_accessed=moved, transcendentals=heavy)


def row_mask():
    return lax.broadcasted_iota(jnp.int32, (8, TP), 0)


def eye_mask():
    return lax.broadcasted_iota(jnp.int32, (TP, TP), 0) == lax.broadcasted_iota(
        jnp.int32, (TP, TP), 1
    )


def split3(value):
    high = value.astype(BF16).astype(F32)
    rest = value - high
    middle = rest.astype(BF16).astype(F32)
    return high, middle, rest - middle


def augmented(raw, source):
    row = row_mask()
    scaled = raw * SCALE
    square = scaled * scaled
    norm = -0.5 * (square[0:1] + square[1:2] + square[2:3])
    if source:
        third, fourth = norm + (raw[6:7] - 1.0) * FAR, jnp.ones((1, TP), F32)
    else:
        third, fourth = jnp.ones((1, TP), F32), norm
    full = jnp.where(
        row < 3, scaled, jnp.where(row == 3, third, jnp.where(row == 4, fourth, 0.0))
    )
    h, m, l = split3(full)
    return jnp.concatenate([h, m, h, m, l, h] if source else [h, h, m, m, h, l], axis=0)


def assemble(own, west, east, up, down, ext):
    layers, columns = own.shape[0], own.shape[1]
    ext[0:2] = up[...]
    ext[layers + 2 : layers + 4] = down[...]
    ext[2 : layers + 2, 0:2] = west[...]
    ext[2 : layers + 2, columns + 2 : columns + 4] = east[...]
    ext[2 : layers + 2, 2 : columns + 2] = own[...]


def moderate(ext):
    span, width = ext.shape[0], ext.shape[1]
    flat = ext[...].reshape((span * width, 8, TP))
    peak = jnp.max(jnp.abs(flat), axis=0)
    row = row_mask()
    ratio = jnp.where(
        row < 3, peak / PLACE_LIMIT, jnp.where(row < 6, peak / SPEED_LIMIT, 0.0)
    )
    return jnp.max(ratio) <= 1.0


def near(codes, layer, column, row, col):
    places = []
    for k in range(6):
        code = codes[k, layer, column]
        down = (code * 11) >> 5
        places.append((row + down - 1, col + code - 3 * down - 1))
    return places


def to_row(total, eye):
    sums = jnp.sum(total, axis=1, keepdims=True)
    return jnp.sum(jnp.where(eye, sums, 0.0), axis=0, keepdims=True)


def fast_weights(left, btab, places):
    weights = []
    for p in range(3):
        right = jnp.concatenate([btab[places[2 * p]], btab[places[2 * p + 1]]], axis=1)
        weights.append(
            jnp.exp2(lax.dot_general(left, right, (((1,), (0,)), ((), ())), preferred_element_type=F32))
        )
    return weights


def fast_sum(left, btab, places, eye):
    total = None
    for weight in fast_weights(left, btab, places):
        part = weight[:, 0:TP] + weight[:, TP : 2 * TP]
        total = part if total is None else total + part
    return to_row(total, eye)


def rows_of(ref, place, row, count):
    return jnp.broadcast_to(ref[place[0], place[1], row : row + 1, :], (count, TP))


def slow_sum(ext, row, col, places, eye):
    cols = jnp.transpose(ext[row, col])
    sums = []
    for block in range(TP // ROWS):
        here = cols[block * ROWS : (block + 1) * ROWS]
        spot = [jnp.broadcast_to(here[:, c : c + 1], (ROWS, TP)) for c in range(3)]
        total = jnp.zeros((ROWS, TP), F32)
        for place in places:
            distance = None
            for c in range(3):
                offset = spot[c] - rows_of(ext, place, c, ROWS)
                square = offset * offset
                distance = square if distance is None else distance + square
            total = total + rows_of(ext, place, 6, ROWS) * jnp.exp(-distance)
        sums.append(jnp.sum(total, axis=1, keepdims=True))
    return jnp.sum(jnp.where(eye, jnp.concatenate(sums, axis=0), 0.0), axis=0, keepdims=True)


def slow_accel(ext, press_ref, damp_ref, row, col, places, eye):
    cols = jnp.transpose(ext[row, col])
    more = jnp.transpose(
        jnp.broadcast_to(press_ref[row - 1, pl.ds(col - 1, 1), :], (8, TP))
    )
    sums = [[], [], []]
    for block in range(TP // ROWS):
        span = slice(block * ROWS, (block + 1) * ROWS)
        here = cols[span]
        spot = [jnp.broadcast_to(here[:, c : c + 1], (ROWS, TP)) for c in range(3)]
        speed = [jnp.broadcast_to(here[:, 3 + c : 4 + c], (ROWS, TP)) for c in range(3)]
        press_here = jnp.broadcast_to(more[span, 0:1], (ROWS, TP))
        total = [jnp.zeros((ROWS, TP), F32) for c in range(3)]
        for place in places:
            offsets = [spot[c] - rows_of(ext, place, c, ROWS) for c in range(3)]
            distance = offsets[0] * offsets[0] + offsets[1] * offsets[1]
            distance = distance + offsets[2] * offsets[2]
            weight = rows_of(ext, place, 6, ROWS) * jnp.exp(-distance)
            there = (place[0] - 1, pl.ds(place[1] - 1, 1), slice(None))
            press = weight * (press_here + jnp.broadcast_to(press_ref[there], (ROWS, TP)))
            damp = weight * jnp.broadcast_to(damp_ref[there], (ROWS, TP))
            for c in range(3):
                relative = rows_of(ext, place, 3 + c, ROWS) - speed[c]
                total[c] = total[c] + (press * offsets[c] + damp * relative)
        for c in range(3):
            sums[c].append(jnp.sum(total[c], axis=1, keepdims=True))
    return [
        jnp.sum(jnp.where(eye, jnp.concatenate(part, axis=0), 0.0), axis=0, keepdims=True)
        for part in sums
    ]


def state_of(summed):
    density = 1.0 + summed * (1.0 / TP)
    press = (2.0 * stiffness) * (density - rest_density) / (density * density)
    return press, viscosity / density


def fill_sources(ext, btab, first, last, left, right):
    def step(index, carry):
        row, col = first + index // (right - left), left + index % (right - left)
        btab[row, col] = augmented(ext[row, col], True).astype(BF16)
        return carry

    lax.fori_loop(0, (last - first) * (right - left), step, 0, unroll=4)


def left_of(ext, row, col):
    return jnp.transpose(augmented(ext[row, col], False)).astype(BF16)


def prep_kernel(counts_in, codes_in, soil_in, out, counts, codes, soil, sems):
    copies = [
        pltpu.make_async_copy(counts_in, counts, sems.at[0]),
        pltpu.make_async_copy(codes_in, codes, sems.at[1]),
        pltpu.make_async_copy(soil_in, soil, sems.at[2]),
    ]
    for copy in copies:
        copy.start()
    for copy in copies:
        copy.wait()
    layers, columns = out.shape[0], out.shape[1]
    lane = lax.broadcasted_iota(jnp.int32, (1, TP), 1)
    for layer in range(layers):
        for column in range(columns):
            listed = jnp.zeros((1, TP), jnp.int32)
            for k in range(6):
                listed = jnp.where(lane == k, codes[k, layer, column], listed)
            live = jnp.where(lane < counts[layer, column], 1.0, 0.0)
            rows = [soil[layer, c, column : column + 1, :] for c in range(6)]
            out[layer, column] = jnp.concatenate(rows + [live, listed.astype(F32)], axis=0)


def density_kernel(codes, own, west, east, up, down, out, ext, btab, sums, lives):
    layers, columns = own.shape[0], own.shape[1]
    assemble(own, west, east, up, down, ext)
    eye = eye_mask()
    fast = moderate(ext)

    @pl.when(fast)
    def _():
        fill_sources(ext, btab, 1, layers + 3, 1, columns + 3)

        def step(group, carry):
            for part in range(TILES):
                tile = group * TILES + part
                layer, column = tile // columns, tile % columns
                places = near(codes, layer, column, layer + 2, column + 2)
                left = left_of(ext, layer + 2, column + 2)
                sums[pl.ds(tile, 1), :] = fast_sum(left, btab, places, eye)
            return carry

        lax.fori_loop(0, layers * columns // TILES, step, 0)

    @pl.when(jnp.logical_not(fast))
    def _():
        def step(tile, carry):
            layer, column = tile // columns, tile % columns
            places = near(codes, layer, column, layer + 2, column + 2)
            sums[pl.ds(tile, 1), :] = slow_sum(ext, layer + 2, column + 2, places, eye)
            return carry

        lax.fori_loop(0, layers * columns, step, 0)

    for layer in range(layers):
        for column in range(columns):
            tile = layer * columns + column
            lives[tile : tile + 1, :] = own[layer, column, 6:7, :]
    press, damp = state_of(sums[...])
    live = lives[...]
    out[0] = press
    out[1] = damp
    out[2] = press * live
    out[3] = damp * live


def ring_kernel(
    codes, own, west, east, up, down, extra, ext, btab, ftab, press_ref, damp_ref
):
    layers, columns = own.shape[0], own.shape[1]
    assemble(own, west, east, up, down, ext)
    eye = eye_mask()
    fast = moderate(ext)
    for layer in range(layers):
        span = slice(layer * columns, (layer + 1) * columns)
        press_ref[layer + 1, 1 : columns + 1, :] = extra[0, span, :]
        damp_ref[layer + 1, 1 : columns + 1, :] = extra[1, span, :]

    def ring(handle):
        def across(index, carry):
            handle(1, index + 1)
            handle(layers + 2, index + 1)
            return carry

        def along(index, carry):
            handle(index + 2, 1)
            handle(index + 2, columns + 2)
            return carry

        lax.fori_loop(0, columns + 2, across, 0)
        lax.fori_loop(0, layers, along, 0)

    def keep(row, col, summed):
        press, damp = state_of(summed)
        press_ref[row - 1, pl.ds(col - 1, 1), :] = press
        damp_ref[row - 1, pl.ds(col - 1, 1), :] = damp

    @pl.when(fast)
    def _():
        fill_sources(ext, btab, 0, layers + 4, 0, columns + 4)

        def ring_sum(row, col):
            places = near(codes, row, col, row, col)
            keep(row, col, fast_sum(left_of(ext, row, col), btab, places, eye))

        ring(ring_sum)

        def factors(index, carry):
            row, col = 1 + index // (columns + 2), 1 + index % (columns + 2)
            raw = ext[row, col]
            press = jnp.broadcast_to(press_ref[row - 1, pl.ds(col - 1, 1), :], (8, TP))
            damp = jnp.broadcast_to(damp_ref[row - 1, pl.ds(col - 1, 1), :], (8, TP))
            value = jnp.concatenate([raw, press * raw, damp * raw], axis=0)
            parts = split3(value)
            ftab[row, col] = jnp.concatenate(
                list(parts) + [jnp.zeros((FACTORS - 72, TP), F32)], axis=0
            ).astype(BF16)
            return carry

        lax.fori_loop(0, (layers + 2) * (columns + 2), factors, 0, unroll=2)

    @pl.when(jnp.logical_not(fast))
    def _():
        def ring_sum(row, col):
            places = near(codes, row, col, row, col)
            keep(row, col, slow_sum(ext, row, col, places, eye))

        ring(ring_sum)


def accel_kernel(codes, ext, btab, ftab, press_ref, damp_ref, out):
    layers, columns = out.shape[0], out.shape[2]
    eye = eye_mask()
    fast = moderate(ext)

    @pl.when(fast)
    def _():
        def step(pair, carry):
            for half in range(2):
                tile = pair * 2 + half
                layer, column = tile // columns, tile % columns
                row, col = layer + 2, column + 2
                places = near(codes, layer, column, row, col)
                weights = fast_weights(left_of(ext, row, col), btab, places)
                highs = [w.astype(BF16) for w in weights]
                lows = [(w - h.astype(F32)).astype(BF16) for w, h in zip(weights, highs)]
                sources = [ftab[place] for place in places]
                summed = lax.dot_general(
                    jnp.concatenate(sources + sources, axis=1),
                    jnp.concatenate(highs + lows, axis=1),
                    NT,
                    preferred_element_type=F32,
                )
                summed = summed[0:24] + summed[24:48] + summed[48:72]
                plain, pressed, damped = summed[0:8], summed[8:16], summed[16:24]
                raw = ext[row, col]
                press = press_ref[row - 1, pl.ds(col - 1, 1), :]
                push = raw * (press * plain[6:7] + pressed[6:7]) - (press * plain + pressed)
                drag = damped - raw * damped[6:7]
                total = (push[0:3] + drag[3:6]) * (raw[6:7] * (1.0 / TP))
                for c in range(3):
                    out[layer, c, pl.ds(column, 1), :] = total[c : c + 1]
            return carry

        lax.fori_loop(0, layers * columns // 2, step, 0)

    @pl.when(jnp.logical_not(fast))
    def _():
        def step(tile, carry):
            layer, column = tile // columns, tile % columns
            row, col = layer + 2, column + 2
            places = near(codes, layer, column, row, col)
            rows = slow_accel(ext, press_ref, damp_ref, row, col, places, eye)
            scale = ext[row, col, 6:7, :] * (1.0 / TP)
            for c in range(3):
                out[layer, c, pl.ds(column, 1), :] = rows[c] * scale
            return carry

        lax.fori_loop(0, layers * columns, step, 0)


def marker_kernel(soil, extra, place, speed, tiles, owners, slots, out, table):
    layers, columns = soil.shape[0], soil.shape[2]
    count = layers * columns
    pairs = place.shape[1] // (2 * TP)
    owner_count = out.shape[0]
    groups = TP // 16
    field_of = lambda f: jnp.concatenate([soil[layer, f] for layer in range(layers)], axis=0)
    spots = [field_of(c) for c in range(3)]
    moves = [field_of(3 + c) for c in range(3)]
    press, damp = extra[2], extra[3]
    scaled = [jnp.clip(spot, -CLIP, CLIP) * SCALE for spot in spots]
    norm = -0.5 * (scaled[0] * scaled[0] + scaled[1] * scaled[1] + scaled[2] * scaled[2])
    fields = scaled + [norm, press, damp]
    fields = fields + [damp * moves[c] - press * spots[c] for c in range(3)]
    for number, field in enumerate(fields):
        pieces = list(split3(field)) + [jnp.zeros((TP - 3 * count, TP), F32)]
        turned = jnp.transpose(jnp.concatenate(pieces, axis=0)).astype(BF16)
        for group in range(groups):
            at = (group * 9 + number) * 16
            table[at : at + 16, :] = turned[group * 16 : group * 16 + 16]
    entry = lax.broadcasted_iota(jnp.int32, (TP, TP), 0)
    listed = jnp.where(entry < 3 * count, lax.rem(entry, count), -1)
    out[...] = jnp.zeros(out.shape, F32)

    def add_terms(pair, terms):
        left, right = [], []
        for part in range(2):
            block = pair * 2 + part
            value = terms[:, part * TP : (part + 1) * TP]
            high = value.astype(BF16).astype(F32)
            low = value - high
            owner = jnp.broadcast_to(owners[pl.ds(block, 1), :], (8, TP))
            slot = jnp.broadcast_to(slots[pl.ds(block, 1), :], (TP, TP))
            hot = jnp.where(slot == entry, 1.0, 0.0).astype(BF16)
            masks = [owner == o for o in range(owner_count)]
            for piece in (high, low):
                left.append(
                    jnp.concatenate(
                        [jnp.where(mask, piece, 0.0) for mask in masks], axis=0
                    ).astype(BF16)
                )
                right.append(hot)
        summed = lax.dot_general(
            jnp.concatenate(left, axis=1),
            jnp.concatenate(right, axis=1),
            NT,
            preferred_element_type=F32,
        )
        out[...] = out[...] + summed.reshape(out.shape)

    def forces_on(pair):
        wide = 2 * TP
        lanes = pl.ds(pl.multiple_of(pair * wide, wide), wide)
        hots = []
        for part in range(2):
            which = jnp.broadcast_to(tiles[pl.ds(pair * 2 + part, 1), :], (TP, TP))
            hots.append(jnp.where(which == listed, 1.0, 0.0).astype(BF16))
        hot = jnp.concatenate(hots, axis=1)
        y = place[:, lanes]
        u = speed[:, lanes]
        spread = y * SCALE
        at = [jnp.broadcast_to(spread[c : c + 1], (16, wide)) for c in range(3)]
        totals = [jnp.zeros((16, wide), F32) for number in range(5)]
        for group in range(groups):
            picked = lax.dot_general(
                table[group * 144 : (group + 1) * 144, :],
                hot,
                (((1,), (0,)), ((), ())),
                preferred_element_type=F32,
            )
            got = [picked[16 * number : 16 * number + 16] for number in range(9)]
            power = (got[3] + at[0] * got[0]) + (at[1] * got[1] + at[2] * got[2])
            weight = jnp.exp2(power)
            for number in range(5):
                totals[number] = totals[number] + weight * got[4 + number]
        sums = [jnp.sum(total, axis=0, keepdims=True) for total in totals]
        square = spread * spread
        scale = jnp.exp2(-0.5 * (square[0:1] + square[1:2] + square[2:3])) * (1.0 / TP)
        where = [y[c : c + 1] for c in range(3)]
        force = [
            (where[c] * sums[0] + (sums[2 + c] - u[c : c + 1] * sums[1])) * scale
            for c in range(3)
        ]
        moment = cross(where, force)
        return jnp.concatenate(force + moment + [jnp.zeros((2, wide), F32)], axis=0)

    def step(pair, terms):
        add_terms(jnp.maximum(pair - 1, 0), terms)
        return forces_on(pair)

    terms = lax.fori_loop(0, pairs, step, jnp.zeros((8, 2 * TP), F32))
    add_terms(pairs - 1, terms)


def cross(a, b):
    return [
        a[1] * b[2] - a[2] * b[1],
        a[2] * b[0] - a[0] * b[2],
        a[0] * b[1] - a[1] * b[0],
    ]


def advance_kernel(first, second, third, fourth, state, inertia, out, sent):
    totals = (first[...] + second[...]) + (third[...] + fourth[...])
    row = lambda ref, r: ref[r : r + 1, :]
    force = [totals[c : c + 1] for c in range(3)]
    moments = [totals[3 + c : 4 + c] for c in range(3)]
    center = [row(state, c) for c in range(3)]
    velocity = [row(state, 3 + c) for c in range(3)]
    spin = [row(state, 6 + c) for c in range(3)]
    inv_mass = row(inertia, 0)
    moment = [row(inertia, 1 + c) for c in range(3)]
    arm = cross(center, force)
    gyro = cross(spin, [moment[c] * spin[c] for c in range(3)])
    pull = [0.0, 0.0, -gravity]
    new_vel = [velocity[c] + time_step * (inv_mass * force[c] + pull[c]) for c in range(3)]
    new_spin = [
        spin[c] + time_step * ((moments[c] - arm[c]) - gyro[c]) / moment[c] for c in range(3)
    ]
    new_center = [center[c] + time_step * new_vel[c] for c in range(3)]
    out[...] = jnp.concatenate(new_center + new_vel + new_spin, axis=0)
    swing = cross(new_spin, center)
    base = [new_vel[c] - swing[c] for c in range(3)]
    block = jnp.concatenate(base + new_spin + [jnp.zeros((2, TP), F32)], axis=0)
    sent[...] = jnp.broadcast_to(block[None], sent.shape)


def pick_kernel(states, place, owners, slots, out):
    steps = place.shape[1] // (4 * TP)
    owner_count = states.shape[0]

    def step(quad, carry):
        for part in range(4):
            block = quad * 4 + part
            lanes = pl.ds(pl.multiple_of(block * TP, TP), TP)
            slot = jnp.broadcast_to(slots[pl.ds(block, 1), :], (8, TP))
            owner = jnp.broadcast_to(owners[pl.ds(block, 1), :], (8, TP))
            found = [jnp.zeros((8, TP), F32) for lane in range(2)]
            for o in range(owner_count):
                here = jnp.take_along_axis(states[o], slot, axis=1)
                found[o % 2] = jnp.where(owner == o, here, found[o % 2])
            picked = found[0] + found[1]
            y = place[:, lanes]
            turn = cross(
                [picked[3 + c : 4 + c] for c in range(3)], [y[c : c + 1] for c in range(3)]
            )
            out[:, lanes] = picked[0:3] + jnp.concatenate(turn, axis=0)
        return carry

    lax.fori_loop(0, steps, step, 0)


def shifted(shard, axis, dim, width):
    size, length = lax.axis_size(axis), shard.shape[dim]
    up = [(i, i + 1) for i in range(size - 1)]
    down = [(j, i) for i, j in up]
    last = lax.slice_in_dim(shard, length - width, length, axis=dim)
    first = lax.slice_in_dim(shard, 0, width, axis=dim)
    return lax.ppermute(last, axis, up), lax.ppermute(first, axis, down)


def local(
    soil_state,
    tile_count,
    tile_neighbors,
    marker_pos,
    marker_vel,
    marker_tile,
    marker_owner,
    marker_slot,
    body_state,
    body_inertia,
):
    layers, columns, fields, tile_size = soil_state.shape
    marker_count = marker_pos.shape[1]
    tile_devs = lax.axis_size("tile")
    depth_devs = lax.axis_size("depth")
    soil = jnp.transpose(soil_state, (0, 2, 1, 3))
    codes = jnp.transpose(tile_neighbors, (2, 0, 1))
    own = pl.pallas_call(
        prep_kernel,
        out_shape=jax.ShapeDtypeStruct((layers, columns, 8, TP), F32),
        in_specs=[pl.BlockSpec(memory_space=pltpu.HBM)] * 3,
        out_specs=vspec(),
        scratch_shapes=[
            SMEM((layers, columns), jnp.int32),
            SMEM((6, layers, columns), jnp.int32),
            VMEM((layers, fields, columns, TP), F32),
            pltpu.SemaphoreType.DMA((3,)),
        ],
        compiler_params=params(),
        name="prep",
    )(tile_count, codes, soil)
    west, east = shifted(own, "tile", 1, 2)
    top = jnp.concatenate([west[:2], own[:2], east[:2]], axis=1)
    bottom = jnp.concatenate([west[-2:], own[-2:], east[-2:]], axis=1)
    rim = jnp.concatenate([top, bottom], axis=0)
    up, down = shifted(rim, "depth", 0, 2)
    pieces = (own, west, east, up, down)
    span, width = layers + 4, columns + 4
    pairs = layers * columns * 6 * TP * TP
    extra = pl.pallas_call(
        density_kernel,
        out_shape=jax.ShapeDtypeStruct((4, layers * columns, TP), F32),
        in_specs=[sspec()] + [vspec()] * 5,
        out_specs=vspec(),
        scratch_shapes=[
            VMEM((span, width, 8, TP), F32),
            VMEM((span, width, AUG, TP), BF16),
            VMEM((layers * columns, TP), F32),
            VMEM((layers * columns, TP), F32),
        ],
        cost_estimate=cost(pairs * 12, 1 << 18, pairs),
        compiler_params=params(),
        name="density",
    )(codes, *pieces)
    owners = marker_owner.reshape((marker_count // TP, TP))
    slots = marker_slot.reshape((marker_count // TP, TP))
    tiles = marker_tile.reshape((marker_count // TP, TP))
    partial_sums = pl.pallas_call(
        marker_kernel,
        out_shape=jax.ShapeDtypeStruct((tile_devs, 8, TP), F32),
        in_specs=[vspec()] * 7,
        out_specs=vspec(),
        scratch_shapes=[VMEM((9 * TP, TP), BF16)],
        cost_estimate=cost(marker_count * TP * 25, 1 << 19, marker_count * TP),
        compiler_params=params(),
        name="markers",
    )(soil, extra, marker_pos, marker_vel, tiles, owners, slots)
    partial_sums, later = lax.optimization_barrier((partial_sums, (pieces, extra)))
    arrived = lax.all_to_all(partial_sums, "tile", 0, 0, tiled=True)
    pieces, extra = later
    own, west, east, up, down = pieces
    ring_codes = jnp.concatenate(
        [
            part[:, :, 7, 0:6]
            for part in (up, jnp.concatenate([west, own, east], axis=1), down)
        ],
        axis=0,
    )
    ring_codes = jnp.transpose(ring_codes.astype(jnp.int32), (2, 0, 1))
    shapes = (
        jax.ShapeDtypeStruct((span, width, 8, TP), F32),
        jax.ShapeDtypeStruct((span, width, AUG, TP), BF16),
        jax.ShapeDtypeStruct((span, width, FACTORS, TP), BF16),
        jax.ShapeDtypeStruct((layers + 2, 16, TP), F32),
        jax.ShapeDtypeStruct((layers + 2, 16, TP), F32),
    )
    tables = pl.pallas_call(
        ring_kernel,
        out_shape=shapes,
        in_specs=[sspec()] + [vspec()] * 6,
        out_specs=(vspec(),) * 5,
        cost_estimate=cost(pairs * 15, 1 << 19, pairs),
        compiler_params=params(),
        name="ring",
    )(ring_codes, *pieces, extra)
    arrived, tables = lax.optimization_barrier((arrived, tables))
    share = jnp.sum(arrived, axis=0)
    others = [
        lax.ppermute(share, "depth", [(i, (i + k) % depth_devs) for i in range(depth_devs)])
        for k in range(1, depth_devs)
    ]
    body_next, sent = pl.pallas_call(
        advance_kernel,
        out_shape=(
            jax.ShapeDtypeStruct((9, TP), F32),
            jax.ShapeDtypeStruct((tile_devs, 8, TP), F32),
        ),
        in_specs=[vspec()] * 6,
        out_specs=(vspec(), vspec()),
        compiler_params=params(),
        name="advance",
    )(share, *others, body_state, body_inertia)
    sent, tables = lax.optimization_barrier((sent, tables))
    states = lax.all_to_all(sent, "tile", 0, 0, tiled=True)
    accel = pl.pallas_call(
        accel_kernel,
        out_shape=jax.ShapeDtypeStruct((layers, 3, columns, TP), F32),
        in_specs=[sspec()] + [vspec()] * 5,
        out_specs=vspec(),
        cost_estimate=cost(pairs * 15, 1 << 19, pairs),
        compiler_params=params(),
        name="accel",
    )(codes, *tables)
    states, accel = lax.optimization_barrier((states, accel))
    soil_accel = jnp.transpose(accel, (0, 2, 1, 3))
    marker_vel_next = pl.pallas_call(
        pick_kernel,
        out_shape=jax.ShapeDtypeStruct((3, marker_count), F32),
        in_specs=[vspec()] * 4,
        out_specs=vspec(),
        compiler_params=params(),
        name="pick",
    )(states, marker_pos, owners, slots)
    return (soil_accel, body_next, marker_vel_next)


def solution(mesh):
    placed = (
        P("depth", "tile", None, None),
        P("depth", "tile"),
        P("depth", "tile", None),
        P(None, ("tile", "depth")),
        P(None, ("tile", "depth")),
        P(("tile", "depth")),
        P(("tile", "depth"), None),
        P(("tile", "depth")),
        P(None, "tile"),
        P(None, "tile"),
    )
    return jax.shard_map(
        local,
        mesh=mesh,
        in_specs=placed,
        out_specs=(P("depth", "tile", None, None), P(None, "tile"), P(None, ("tile", "depth"))),
        check_vma=False,
    )
```

```python
import functools

import jax
import jax.numpy as jnp
from jax import lax
from jax.experimental import pallas as pl
from jax.experimental.pallas import tpu as pltpu
from jax.sharding import PartitionSpec as P

stiffness = 40.0
rest_density = 2.0
viscosity = 20.0
time_step = 0.05
gravity = 1.0
VMEM = pltpu.VMEM
SMEM = pltpu.SMEM
TP = 128
ROWS = 16
AUG = 48
FACTORS = 48
TILES = 10
ONEHOT = 9
SCALE = (2.0 * 1.4426950408889634) ** 0.5
FAR = 1e30
PLACE_LIMIT = 4.0
CLIP = 1e4
SPEED_LIMIT = 8.0
F32 = jnp.float32
BF16 = jnp.bfloat16
NT = (((1,), (1,)), ((), ()))


def vspec():
    return pl.BlockSpec(memory_space=VMEM)


def sspec():
    return pl.BlockSpec(memory_space=SMEM)


def params(limit=16 << 20):
    return pltpu.CompilerParams(vmem_limit_bytes=limit)


def cost(flops, moved, heavy=0):
    return pl.CostEstimate(flops=flops, bytes_accessed=moved, transcendentals=heavy)


def row_mask():
    return lax.broadcasted_iota(jnp.int32, (8, TP), 0)


def eye_mask():
    return lax.broadcasted_iota(jnp.int32, (TP, TP), 0) == lax.broadcasted_iota(
        jnp.int32, (TP, TP), 1
    )


def split3(value):
    high = value.astype(BF16).astype(F32)
    rest = value - high
    middle = rest.astype(BF16).astype(F32)
    return high, middle, rest - middle


def augmented(raw, source):
    row = row_mask()
    scaled = raw * SCALE
    square = scaled * scaled
    norm = -0.5 * (square[0:1] + square[1:2] + square[2:3])
    if source:
        third, fourth = norm + (raw[6:7] - 1.0) * FAR, jnp.ones((1, TP), F32)
    else:
        third, fourth = jnp.ones((1, TP), F32), norm
    full = jnp.where(
        row < 3, scaled, jnp.where(row == 3, third, jnp.where(row == 4, fourth, 0.0))
    )
    h, m, l = split3(full)
    return jnp.concatenate([h, m, h, m, l, h] if source else [h, h, m, m, h, l], axis=0)


def assemble(own, west, east, up, down, ext):
    layers, columns = own.shape[0], own.shape[1]
    ext[0:2] = up[...]
    ext[layers + 2 : layers + 4] = down[...]
    ext[2 : layers + 2, 0:2] = west[...]
    ext[2 : layers + 2, columns + 2 : columns + 4] = east[...]
    ext[2 : layers + 2, 2 : columns + 2] = own[...]


def moderate(ext):
    span, width = ext.shape[0], ext.shape[1]
    flat = ext[...].reshape((span * width, 8, TP))
    peak = jnp.max(jnp.abs(flat), axis=0)
    row = row_mask()
    ratio = jnp.where(
        row < 3, peak / PLACE_LIMIT, jnp.where(row < 6, peak / SPEED_LIMIT, 0.0)
    )
    return jnp.max(ratio) <= 1.0


def near(codes, layer, column, row, col):
    places = []
    for k in range(6):
        code = codes[k, layer, column]
        down = (code * 11) >> 5
        places.append((row + down - 1, col + code - 3 * down - 1))
    return places


def to_row(total, eye):
    sums = jnp.sum(total, axis=1, keepdims=True)
    return jnp.sum(jnp.where(eye, sums, 0.0), axis=0, keepdims=True)


def fast_weights(left, btab, places):
    weights = []
    for p in range(3):
        right = jnp.concatenate([btab[places[2 * p]], btab[places[2 * p + 1]]], axis=1)
        weights.append(
            jnp.exp2(lax.dot_general(left, right, (((1,), (0,)), ((), ())), preferred_element_type=F32))
        )
    return weights


def fast_sum(left, btab, places, eye):
    total = None
    for weight in fast_weights(left, btab, places):
        part = weight[:, 0:TP] + weight[:, TP : 2 * TP]
        total = part if total is None else total + part
    return to_row(total, eye)


def rows_of(ref, place, row, count):
    return jnp.broadcast_to(ref[place[0], place[1], row : row + 1, :], (count, TP))


def slow_sum(ext, row, col, places, eye):
    cols = jnp.transpose(ext[row, col])
    sums = []
    for block in range(TP // ROWS):
        here = cols[block * ROWS : (block + 1) * ROWS]
        spot = [jnp.broadcast_to(here[:, c : c + 1], (ROWS, TP)) for c in range(3)]
        total = jnp.zeros((ROWS, TP), F32)
        for place in places:
            distance = None
            for c in range(3):
                offset = spot[c] - rows_of(ext, place, c, ROWS)
                square = offset * offset
                distance = square if distance is None else distance + square
            total = total + rows_of(ext, place, 6, ROWS) * jnp.exp(-distance)
        sums.append(jnp.sum(total, axis=1, keepdims=True))
    return jnp.sum(jnp.where(eye, jnp.concatenate(sums, axis=0), 0.0), axis=0, keepdims=True)


def slow_accel(ext, press_ref, damp_ref, row, col, places, eye):
    cols = jnp.transpose(ext[row, col])
    more = jnp.transpose(
        jnp.broadcast_to(press_ref[row - 1, pl.ds(col - 1, 1), :], (8, TP))
    )
    sums = [[], [], []]
    for block in range(TP // ROWS):
        span = slice(block * ROWS, (block + 1) * ROWS)
        here = cols[span]
        spot = [jnp.broadcast_to(here[:, c : c + 1], (ROWS, TP)) for c in range(3)]
        speed = [jnp.broadcast_to(here[:, 3 + c : 4 + c], (ROWS, TP)) for c in range(3)]
        press_here = jnp.broadcast_to(more[span, 0:1], (ROWS, TP))
        total = [jnp.zeros((ROWS, TP), F32) for c in range(3)]
        for place in places:
            offsets = [spot[c] - rows_of(ext, place, c, ROWS) for c in range(3)]
            distance = offsets[0] * offsets[0] + offsets[1] * offsets[1]
            distance = distance + offsets[2] * offsets[2]
            weight = rows_of(ext, place, 6, ROWS) * jnp.exp(-distance)
            there = (place[0] - 1, pl.ds(place[1] - 1, 1), slice(None))
            press = weight * (press_here + jnp.broadcast_to(press_ref[there], (ROWS, TP)))
            damp = weight * jnp.broadcast_to(damp_ref[there], (ROWS, TP))
            for c in range(3):
                relative = rows_of(ext, place, 3 + c, ROWS) - speed[c]
                total[c] = total[c] + (press * offsets[c] + damp * relative)
        for c in range(3):
            sums[c].append(jnp.sum(total[c], axis=1, keepdims=True))
    return [
        jnp.sum(jnp.where(eye, jnp.concatenate(part, axis=0), 0.0), axis=0, keepdims=True)
        for part in sums
    ]


def state_of(summed):
    density = 1.0 + summed * (1.0 / TP)
    press = (2.0 * stiffness) * (density - rest_density) / (density * density)
    return press, viscosity / density


def fill_sources(ext, btab, first, last, left, right):
    def step(row, carry):
        for col in range(left, right):
            btab[row, col] = augmented(ext[row, col], True).astype(BF16)
        return carry

    lax.fori_loop(first, last, step, 0)


def left_of(ext, row, col):
    return jnp.transpose(augmented(ext[row, col], False)).astype(BF16)


def prep_kernel(counts_in, codes_in, soil_in, out, counts, codes, soil, sems):
    copies = [
        pltpu.make_async_copy(counts_in, counts, sems.at[0]),
        pltpu.make_async_copy(codes_in, codes, sems.at[1]),
        pltpu.make_async_copy(soil_in, soil, sems.at[2]),
    ]
    for copy in copies:
        copy.start()
    for copy in copies:
        copy.wait()
    layers, columns = out.shape[0], out.shape[1]
    lane = lax.broadcasted_iota(jnp.int32, (1, TP), 1)
    for layer in range(layers):
        for column in range(columns):
            listed = jnp.zeros((1, TP), jnp.int32)
            for k in range(6):
                listed = jnp.where(lane == k, codes[k, layer, column], listed)
            live = jnp.where(lane < counts[layer, column], 1.0, 0.0)
            rows = [soil[layer, c, column : column + 1, :] for c in range(6)]
            out[layer, column] = jnp.concatenate(rows + [live, listed.astype(F32)], axis=0)


def rim_tile(index, layers, columns):
    side = index - 2 * columns
    on_side, last = side >= 0, index >= columns
    layer = jnp.where(on_side, 1 + (side >> 1), jnp.where(last, layers - 1, 0))
    column = jnp.where(
        on_side, (columns - 1) * (side & 1), jnp.where(last, index - columns, index)
    )
    return layer, column


def inner_kernel(codes, own, lefts, sums, btab):
    layers, columns = own.shape[0], own.shape[1]
    eye = eye_mask()
    fill_sources(own, btab, 0, layers, 0, columns)

    def turn(layer, carry):
        for column in range(columns):
            lefts[layer, column] = left_of(own, layer, column)
        return carry

    lax.fori_loop(0, layers, turn, 0)

    def step(layer, carry):
        for column in range(1, columns - 1):
            places = near(codes, layer, column, layer, column)
            row = fast_sum(lefts[layer, column], btab, places, eye)
            sums[layer, column : column + 1, :] = row
        return carry

    lax.fori_loop(1, layers - 1, step, 0)


def density_kernel(codes, own, west, east, up, down, lefts, inner, out, ext, btab, sums):
    layers, columns = own.shape[0], own.shape[1]
    assemble(own, west, east, up, down, ext)
    eye = eye_mask()
    fast = moderate(ext)
    sums[...] = inner[...]

    @pl.when(fast)
    def _():
        fill_sources(ext, btab, 1, layers + 3, 1, columns + 3)
        rim = 2 * columns + 2 * (layers - 2)

        def step(group, carry):
            for part in range(TILES):
                index = group * TILES + part
                layer, column = rim_tile(index, layers, columns)
                places = near(codes, layer, column, layer + 2, column + 2)
                row = fast_sum(lefts[layer, column], btab, places, eye)
                sums[layer, pl.ds(column, 1), :] = row
            return carry

        lax.fori_loop(0, rim // TILES, step, 0)

    @pl.when(jnp.logical_not(fast))
    def _():
        def step(tile, carry):
            layer, column = tile // columns, tile % columns
            places = near(codes, layer, column, layer + 2, column + 2)
            row = slow_sum(ext, layer + 2, column + 2, places, eye)
            sums[layer, pl.ds(column, 1), :] = row
            return carry

        lax.fori_loop(0, layers * columns, step, 0)

    for layer in range(layers):
        span = slice(layer * columns, (layer + 1) * columns)
        press, damp = state_of(sums[layer])
        live = jnp.concatenate([own[layer, c, 6:7, :] for c in range(columns)], axis=0)
        out[0, span, :] = press
        out[1, span, :] = damp
        out[2, span, :] = press * live
        out[3, span, :] = damp * live


def ring_kernel(
    codes, own, west, east, up, down, extra, ext, sources, ftab, press_ref, damp_ref, btab
):
    layers, columns = own.shape[0], own.shape[1]
    assemble(own, west, east, up, down, ext)
    eye = eye_mask()
    fast = moderate(ext)
    for layer in range(layers):
        span = slice(layer * columns, (layer + 1) * columns)
        press_ref[layer + 1, 1 : columns + 1, :] = extra[0, span, :]
        damp_ref[layer + 1, 1 : columns + 1, :] = extra[1, span, :]

    def ring(handle):
        def across(index, carry):
            handle(1, index + 1)
            handle(layers + 2, index + 1)
            return carry

        def along(index, carry):
            handle(index + 2, 1)
            handle(index + 2, columns + 2)
            return carry

        lax.fori_loop(0, columns + 2, across, 0)
        lax.fori_loop(0, layers, along, 0)

    def keep(row, col, summed):
        press, damp = state_of(summed)
        press_ref[row - 1, pl.ds(col - 1, 1), :] = press
        damp_ref[row - 1, pl.ds(col - 1, 1), :] = damp

    @pl.when(fast)
    def _():
        fill_sources(ext, btab, 0, layers + 4, 0, columns + 4)

        sources[...] = btab[1 : layers + 3, 1 : columns + 3]

        def ring_sum(row, col):
            places = near(codes, row, col, row, col)
            keep(row, col, fast_sum(left_of(ext, row, col), btab, places, eye))

        ring(ring_sum)

        def factors(row, carry):
            for col in range(1, columns + 3):
                raw = ext[row, col]
                press = jnp.broadcast_to(press_ref[row - 1, col - 1 : col, :], (8, TP))
                damp = jnp.broadcast_to(damp_ref[row - 1, col - 1 : col, :], (8, TP))
                value = jnp.concatenate([raw, press * raw, damp * raw], axis=0)
                high = value.astype(BF16).astype(F32)
                ftab[row - 1, col - 1] = jnp.concatenate([high, value - high], axis=0).astype(BF16)
            return carry

        lax.fori_loop(1, layers + 3, factors, 0)

    @pl.when(jnp.logical_not(fast))
    def _():
        def ring_sum(row, col):
            places = near(codes, row, col, row, col)
            keep(row, col, slow_sum(ext, row, col, places, eye))

        ring(ring_sum)


def accel_kernel(codes, ext, btab, ftab, press_ref, damp_ref, out, pairs, lefts):
    layers, columns = out.shape[0], out.shape[2]
    eye = eye_mask()
    fast = moderate(ext)

    def weigh(layer):
        for column in range(columns):
            lefts[column] = left_of(ext, layer + 2, column + 2)
        for column in range(columns):
            places = near(codes, layer, column, layer + 1, column + 1)
            for p, weight in enumerate(fast_weights(lefts[column], btab, places)):
                high = weight.astype(BF16)
                pairs[column, p, :, 0 : 2 * TP] = high
                pairs[column, p, :, 2 * TP : 4 * TP] = (weight - high.astype(F32)).astype(BF16)

    def gather(layer):
        for column in range(columns):
            row, col = layer + 2, column + 2
            places = near(codes, layer, column, row - 1, col - 1)
            summed = None
            for p in range(3):
                source = jnp.concatenate([ftab[places[2 * p]], ftab[places[2 * p + 1]]], axis=1)
                part = lax.dot_general(
                    jnp.concatenate([source, source], axis=1),
                    pairs[column, p],
                    NT,
                    preferred_element_type=F32,
                )
                summed = part if summed is None else summed + part
            summed = summed[0:24] + summed[24:48]
            plain, pressed, damped = summed[0:8], summed[8:16], summed[16:24]
            raw = ext[row, col]
            press = press_ref[row - 1, col - 1 : col, :]
            push = raw * (press * plain[6:7] + pressed[6:7]) - (press * plain + pressed)
            drag = damped - raw * damped[6:7]
            total = (push[0:3] + drag[3:6]) * (raw[6:7] * (1.0 / TP))
            for c in range(3):
                out[layer, c, column : column + 1, :] = total[c : c + 1]

    @pl.when(fast)
    def _():
        def step(layer, carry):
            weigh(layer)
            gather(layer)
            return carry

        lax.fori_loop(0, layers, step, 0)

    @pl.when(jnp.logical_not(fast))
    def _():
        def step(tile, carry):
            layer, column = tile // columns, tile % columns
            row, col = layer + 2, column + 2
            places = near(codes, layer, column, row, col)
            rows = slow_accel(ext, press_ref, damp_ref, row, col, places, eye)
            scale = ext[row, col, 6:7, :] * (1.0 / TP)
            for c in range(3):
                out[layer, c, pl.ds(column, 1), :] = rows[c] * scale
            return carry

        lax.fori_loop(0, layers * columns, step, 0)


def marker_kernel(soil, extra, place, speed, tiles, owners, slots, out, table, lookup):
    layers, columns = soil.shape[0], soil.shape[2]
    count = layers * columns
    pairs = place.shape[1] // (2 * TP)
    owner_count = out.shape[0]
    groups = TP // 16
    field_of = lambda f: jnp.concatenate([soil[layer, f] for layer in range(layers)], axis=0)
    spots = [field_of(c) for c in range(3)]
    moves = [field_of(3 + c) for c in range(3)]
    press, damp = extra[2], extra[3]
    scaled = [jnp.clip(spot, -CLIP, CLIP) * SCALE for spot in spots]
    norm = -0.5 * (scaled[0] * scaled[0] + scaled[1] * scaled[1] + scaled[2] * scaled[2])
    fields = scaled + [norm, press, damp]
    fields = fields + [damp * moves[c] - press * spots[c] for c in range(3)]
    for number, field in enumerate(fields):
        if number < ONEHOT:
            pieces = list(split3(field)) + [jnp.zeros((TP - 3 * count, TP), F32)]
            turned = jnp.transpose(jnp.concatenate(pieces, axis=0)).astype(BF16)
            for group in range(groups):
                at = (group * ONEHOT + number) * 16
                table[at : at + 16, :] = turned[group * 16 : group * 16 + 16]
        else:
            pieces = [field, jnp.zeros((TP - count, TP), F32)]
            lookup[number - ONEHOT] = jnp.transpose(jnp.concatenate(pieces, axis=0))
    entry = lax.broadcasted_iota(jnp.int32, (TP, TP), 0)
    listed = jnp.where(entry < 3 * count, lax.rem(entry, count), -1)
    out[...] = jnp.zeros(out.shape, F32)

    def add_terms(pair, terms):
        left, right = [], []
        for part in range(2):
            block = pair * 2 + part
            value = terms[:, part * TP : (part + 1) * TP]
            high = value.astype(BF16).astype(F32)
            low = value - high
            owner = jnp.broadcast_to(owners[pl.ds(block, 1), :], (8, TP))
            slot = jnp.broadcast_to(slots[pl.ds(block, 1), :], (TP, TP))
            hot = jnp.where(slot == entry, 1.0, 0.0).astype(BF16)
            masks = [owner == o for o in range(owner_count)]
            for piece in (high, low):
                left.append(
                    jnp.concatenate(
                        [jnp.where(mask, piece, 0.0) for mask in masks], axis=0
                    ).astype(BF16)
                )
                right.append(hot)
        summed = lax.dot_general(
            jnp.concatenate(left, axis=1),
            jnp.concatenate(right, axis=1),
            NT,
            preferred_element_type=F32,
        )
        out[...] = out[...] + summed.reshape(out.shape)

    def forces_on(pair):
        wide = 2 * TP
        lanes = pl.ds(pl.multiple_of(pair * wide, wide), wide)
        which = [
            jnp.broadcast_to(tiles[pl.ds(pair * 2 + part, 1), :], (TP, TP)) for part in range(2)
        ]
        hot = jnp.concatenate(
            [jnp.where(w == listed, 1.0, 0.0).astype(BF16) for w in which], axis=1
        )
        y = place[:, lanes]
        u = speed[:, lanes]
        spread = y * SCALE
        at = [jnp.broadcast_to(spread[c : c + 1], (16, wide)) for c in range(3)]
        totals = [jnp.zeros((16, wide), F32) for number in range(5)]
        for group in range(groups):
            span = slice(group * 16, group * 16 + 16)
            rows = slice(group * 16 * ONEHOT, (group + 1) * 16 * ONEHOT)
            got = []
            if ONEHOT:
                picked = lax.dot_general(
                    table[rows, :], hot, (((1,), (0,)), ((), ())), preferred_element_type=F32
                )
                got = [picked[16 * number : 16 * number + 16] for number in range(ONEHOT)]
            for number in range(9 - ONEHOT):
                source = lookup[number, span, :]
                got.append(
                    jnp.concatenate(
                        [jnp.take_along_axis(source, w[0:16], axis=1) for w in which], axis=1
                    )
                )
            power = (got[3] + at[0] * got[0]) + (at[1] * got[1] + at[2] * got[2])
            weight = jnp.exp2(power)
            for number in range(5):
                totals[number] = totals[number] + weight * got[4 + number]
        sums = [jnp.sum(total, axis=0, keepdims=True) for total in totals]
        square = spread * spread
        scale = jnp.exp2(-0.5 * (square[0:1] + square[1:2] + square[2:3])) * (1.0 / TP)
        where = [y[c : c + 1] for c in range(3)]
        force = [
            (where[c] * sums[0] + (sums[2 + c] - u[c : c + 1] * sums[1])) * scale
            for c in range(3)
        ]
        moment = cross(where, force)
        return jnp.concatenate(force + moment + [jnp.zeros((2, wide), F32)], axis=0)

    def step(pair, terms):
        add_terms(jnp.maximum(pair - 1, 0), terms)
        return forces_on(pair)

    terms = lax.fori_loop(0, pairs, step, jnp.zeros((8, 2 * TP), F32))
    add_terms(pairs - 1, terms)


def cross(a, b):
    return [
        a[1] * b[2] - a[2] * b[1],
        a[2] * b[0] - a[0] * b[2],
        a[0] * b[1] - a[1] * b[0],
    ]


def advance_kernel(first, second, third, fourth, state, inertia, out, sent):
    totals = (first[...] + second[...]) + (third[...] + fourth[...])
    row = lambda ref, r: ref[r : r + 1, :]
    force = [totals[c : c + 1] for c in range(3)]
    moments = [totals[3 + c : 4 + c] for c in range(3)]
    center = [row(state, c) for c in range(3)]
    velocity = [row(state, 3 + c) for c in range(3)]
    spin = [row(state, 6 + c) for c in range(3)]
    inv_mass = row(inertia, 0)
    moment = [row(inertia, 1 + c) for c in range(3)]
    arm = cross(center, force)
    gyro = cross(spin, [moment[c] * spin[c] for c in range(3)])
    pull = [0.0, 0.0, -gravity]
    new_vel = [velocity[c] + time_step * (inv_mass * force[c] + pull[c]) for c in range(3)]
    new_spin = [
        spin[c] + time_step * ((moments[c] - arm[c]) - gyro[c]) / moment[c] for c in range(3)
    ]
    new_center = [center[c] + time_step * new_vel[c] for c in range(3)]
    out[...] = jnp.concatenate(new_center + new_vel + new_spin, axis=0)
    swing = cross(new_spin, center)
    base = [new_vel[c] - swing[c] for c in range(3)]
    block = jnp.concatenate(base + new_spin + [jnp.zeros((2, TP), F32)], axis=0)
    sent[...] = jnp.broadcast_to(block[None], sent.shape)


def pick_kernel(states, place, owners, slots, out):
    steps = place.shape[1] // (4 * TP)
    owner_count = states.shape[0]

    def step(quad, carry):
        for part in range(4):
            block = quad * 4 + part
            lanes = pl.ds(pl.multiple_of(block * TP, TP), TP)
            slot = jnp.broadcast_to(slots[pl.ds(block, 1), :], (8, TP))
            owner = jnp.broadcast_to(owners[pl.ds(block, 1), :], (8, TP))
            found = [jnp.zeros((8, TP), F32) for lane in range(2)]
            for o in range(owner_count):
                here = jnp.take_along_axis(states[o], slot, axis=1)
                found[o % 2] = jnp.where(owner == o, here, found[o % 2])
            picked = found[0] + found[1]
            y = place[:, lanes]
            turn = cross(
                [picked[3 + c : 4 + c] for c in range(3)], [y[c : c + 1] for c in range(3)]
            )
            out[:, lanes] = picked[0:3] + jnp.concatenate(turn, axis=0)
        return carry

    lax.fori_loop(0, steps, step, 0)


def shifted(shard, axis, dim, width):
    size, length = lax.axis_size(axis), shard.shape[dim]
    up = [(i, i + 1) for i in range(size - 1)]
    down = [(j, i) for i, j in up]
    last = lax.slice_in_dim(shard, length - width, length, axis=dim)
    first = lax.slice_in_dim(shard, 0, width, axis=dim)
    return lax.ppermute(last, axis, up), lax.ppermute(first, axis, down)


def local(
    soil_state,
    tile_count,
    tile_neighbors,
    marker_pos,
    marker_vel,
    marker_tile,
    marker_owner,
    marker_slot,
    body_state,
    body_inertia,
):
    layers, columns, fields, tile_size = soil_state.shape
    marker_count = marker_pos.shape[1]
    tile_devs = lax.axis_size("tile")
    depth_devs = lax.axis_size("depth")
    soil = jnp.transpose(soil_state, (0, 2, 1, 3))
    codes = jnp.transpose(tile_neighbors, (2, 0, 1))
    own = pl.pallas_call(
        prep_kernel,
        out_shape=jax.ShapeDtypeStruct((layers, columns, 8, TP), F32),
        in_specs=[pl.BlockSpec(memory_space=pltpu.HBM)] * 3,
        out_specs=vspec(),
        scratch_shapes=[
            SMEM((layers, columns), jnp.int32),
            SMEM((6, layers, columns), jnp.int32),
            VMEM((layers, fields, columns, TP), F32),
            pltpu.SemaphoreType.DMA((3,)),
        ],
        compiler_params=params(),
        name="prep",
    )(*[pltpu.with_memory_space_constraint(x, pltpu.HBM) for x in (tile_count, codes, soil)])
    lefts, inner = pl.pallas_call(
        inner_kernel,
        out_shape=(
            jax.ShapeDtypeStruct((layers, columns, TP, AUG), BF16),
            jax.ShapeDtypeStruct((layers, columns, TP), F32),
        ),
        in_specs=[sspec(), vspec()],
        out_specs=(vspec(), vspec()),
        scratch_shapes=[VMEM((layers, columns, AUG, TP), BF16)],
        cost_estimate=cost(4_000_000, 1 << 18, 1_000_000),
        compiler_params=params(),
        name="inner",
    )(codes, own)
    west, east = shifted(own, "tile", 1, 2)
    top = jnp.concatenate([west[:2], own[:2], east[:2]], axis=1)
    bottom = jnp.concatenate([west[-2:], own[-2:], east[-2:]], axis=1)
    rim = jnp.concatenate([top, bottom], axis=0)
    up, down = shifted(rim, "depth", 0, 2)
    pieces = (own, west, east, up, down)
    span, width = layers + 4, columns + 4
    pairs = layers * columns * 6 * TP * TP
    extra = pl.pallas_call(
        density_kernel,
        out_shape=jax.ShapeDtypeStruct((4, layers * columns, TP), F32),
        in_specs=[sspec()] + [vspec()] * 7,
        out_specs=vspec(),
        scratch_shapes=[
            VMEM((span, width, 8, TP), F32),
            VMEM((span, width, AUG, TP), BF16),
            VMEM((layers, columns, TP), F32),
        ],
        cost_estimate=cost(pairs * 12, 1 << 18, pairs),
        compiler_params=params(),
        name="density",
    )(codes, *pieces, lefts, inner)
    owners = marker_owner.reshape((marker_count // TP, TP))
    slots = marker_slot.reshape((marker_count // TP, TP))
    tiles = marker_tile.reshape((marker_count // TP, TP))
    partial_sums = pl.pallas_call(
        marker_kernel,
        out_shape=jax.ShapeDtypeStruct((tile_devs, 8, TP), F32),
        in_specs=[vspec()] * 7,
        out_specs=vspec(),
        scratch_shapes=[VMEM((9 * TP, TP), BF16), VMEM((9, TP, TP), F32)],
        cost_estimate=cost(marker_count * TP * 25, 1 << 19, marker_count * TP),
        compiler_params=params(),
        name="markers",
    )(soil, extra, marker_pos, marker_vel, tiles, owners, slots)
    partial_sums, extra = lax.optimization_barrier((partial_sums, extra))
    arrived = lax.all_to_all(partial_sums, "tile", 0, 0, tiled=True)
    own, west, east, up, down = pieces
    ring_codes = jnp.concatenate(
        [
            part[:, :, 7, 0:6]
            for part in (up, jnp.concatenate([west, own, east], axis=1), down)
        ],
        axis=0,
    )
    ring_codes = jnp.transpose(ring_codes.astype(jnp.int32), (2, 0, 1))
    shapes = (
        jax.ShapeDtypeStruct((span, width, 8, TP), F32),
        jax.ShapeDtypeStruct((layers + 2, columns + 2, AUG, TP), BF16),
        jax.ShapeDtypeStruct((layers + 2, columns + 2, FACTORS, TP), BF16),
        jax.ShapeDtypeStruct((layers + 2, 16, TP), F32),
        jax.ShapeDtypeStruct((layers + 2, 16, TP), F32),
    )
    tables = pl.pallas_call(
        ring_kernel,
        out_shape=shapes,
        in_specs=[sspec()] + [vspec()] * 6,
        out_specs=(vspec(),) * 5,
        scratch_shapes=[VMEM((span, width, AUG, TP), BF16)],
        cost_estimate=cost(pairs * 15, 1 << 19, pairs),
        compiler_params=params(),
        name="ring",
    )(ring_codes, *pieces, extra)
    arrived, damp = lax.optimization_barrier((arrived, tables[4]))
    share = jnp.sum(arrived, axis=0)

    others = [
        lax.ppermute(share, "depth", [(i, (i + k) % depth_devs) for i in range(depth_devs)])
        for k in range(1, depth_devs)
    ]
    body_next, sent = pl.pallas_call(
        advance_kernel,
        out_shape=(
            jax.ShapeDtypeStruct((9, TP), F32),
            jax.ShapeDtypeStruct((tile_devs, 8, TP), F32),
        ),
        in_specs=[vspec()] * 6,
        out_specs=(vspec(), vspec()),
        compiler_params=params(),
        name="advance",
    )(share, *others, body_state, body_inertia)
    sent, damp = lax.optimization_barrier((sent, damp))
    states = lax.all_to_all(sent, "tile", 0, 0, tiled=True)
    accel = pl.pallas_call(
        accel_kernel,
        out_shape=jax.ShapeDtypeStruct((layers, 3, columns, TP), F32),
        in_specs=[sspec()] + [vspec()] * 5,
        out_specs=vspec(),
        scratch_shapes=[VMEM((columns, 3, TP, 4 * TP), BF16), VMEM((columns, TP, AUG), BF16)],
        cost_estimate=cost(pairs * 15, 1 << 19, pairs),
        compiler_params=params(),
        name="accel",
    )(codes, *tables[:4], damp)
    states, accel = lax.optimization_barrier((states, accel))
    soil_accel = jnp.transpose(accel, (0, 2, 1, 3))
    marker_vel_next = pl.pallas_call(
        pick_kernel,
        out_shape=jax.ShapeDtypeStruct((3, marker_count), F32),
        in_specs=[vspec()] * 4,
        out_specs=vspec(),
        compiler_params=params(),
        name="pick",
    )(states, marker_pos, owners, slots)
    return (soil_accel, body_next, marker_vel_next)


def solution(mesh):
    placed = (
        P("depth", "tile", None, None),
        P("depth", "tile"),
        P("depth", "tile", None),
        P(None, ("tile", "depth")),
        P(None, ("tile", "depth")),
        P(("tile", "depth")),
        P(("tile", "depth"), None),
        P(("tile", "depth")),
        P(None, "tile"),
        P(None, "tile"),
    )
    return jax.shard_map(
        local,
        mesh=mesh,
        in_specs=placed,
        out_specs=(P("depth", "tile", None, None), P(None, "tile"), P(None, ("tile", "depth"))),
        check_vma=False,
    )
```

```python
import functools

import jax
import jax.numpy as jnp
from jax import lax
from jax.experimental import pallas as pl
from jax.experimental.pallas import tpu as pltpu
from jax.sharding import PartitionSpec as P

stiffness = 40.0
rest_density = 2.0
viscosity = 20.0
time_step = 0.05
gravity = 1.0
VMEM = pltpu.VMEM
SMEM = pltpu.SMEM
TP = 128
ROWS = 16
AUG = 48
FACTORS = 48
TILES = 10
ONEHOT = 9
PICK = 4
SCALE = (2.0 * 1.4426950408889634) ** 0.5
FAR = 1e30
PLACE_LIMIT = 4.0
CLIP = 1e4
SPEED_LIMIT = 8.0
F32 = jnp.float32
BF16 = jnp.bfloat16
NT = (((1,), (1,)), ((), ()))


def vspec():
    return pl.BlockSpec(memory_space=VMEM)


def sspec():
    return pl.BlockSpec(memory_space=SMEM)


def params(limit=16 << 20):
    return pltpu.CompilerParams(vmem_limit_bytes=limit)


def cost(flops, moved, heavy=0):
    return pl.CostEstimate(flops=flops, bytes_accessed=moved, transcendentals=heavy)


def row_mask():
    return lax.broadcasted_iota(jnp.int32, (8, TP), 0)


def eye_mask():
    return lax.broadcasted_iota(jnp.int32, (TP, TP), 0) == lax.broadcasted_iota(
        jnp.int32, (TP, TP), 1
    )


def split3(value):
    high = value.astype(BF16).astype(F32)
    rest = value - high
    middle = rest.astype(BF16).astype(F32)
    return high, middle, rest - middle


def augmented(raw, source):
    row = row_mask()
    scaled = raw * SCALE
    square = scaled * scaled
    norm = -0.5 * (square[0:1] + square[1:2] + square[2:3])
    if source:
        third, fourth = norm + (raw[6:7] - 1.0) * FAR, jnp.ones((1, TP), F32)
    else:
        third, fourth = jnp.ones((1, TP), F32), norm
    full = jnp.where(
        row < 3, scaled, jnp.where(row == 3, third, jnp.where(row == 4, fourth, 0.0))
    )
    h, m, l = split3(full)
    return jnp.concatenate([h, m, h, m, l, h] if source else [h, h, m, m, h, l], axis=0)


def assemble(own, west, east, up, down, ext):
    layers, columns = own.shape[0], own.shape[1]
    ext[0:2] = up[...]
    ext[layers + 2 : layers + 4] = down[...]
    ext[2 : layers + 2, 0:2] = west[...]
    ext[2 : layers + 2, columns + 2 : columns + 4] = east[...]
    ext[2 : layers + 2, 2 : columns + 2] = own[...]


def moderate(ext):
    span, width = ext.shape[0], ext.shape[1]
    flat = ext[...].reshape((span * width, 8, TP))
    peak = jnp.max(jnp.abs(flat), axis=0)
    row = row_mask()
    ratio = jnp.where(
        row < 3, peak / PLACE_LIMIT, jnp.where(row < 6, peak / SPEED_LIMIT, 0.0)
    )
    return jnp.max(ratio) <= 1.0


def near(codes, layer, column, row, col):
    places = []
    for k in range(6):
        code = codes[k, layer, column]
        down = (code * 11) >> 5
        places.append((row + down - 1, col + code - 3 * down - 1))
    return places


def to_row(total, eye):
    sums = jnp.sum(total, axis=1, keepdims=True)
    return jnp.sum(jnp.where(eye, sums, 0.0), axis=0, keepdims=True)


def fast_weights(left, btab, places):
    weights = []
    for p in range(3):
        right = jnp.concatenate([btab[places[2 * p]], btab[places[2 * p + 1]]], axis=1)
        weights.append(
            jnp.exp2(lax.dot_general(left, right, (((1,), (0,)), ((), ())), preferred_element_type=F32))
        )
    return weights


def fast_sum(left, btab, places, eye):
    total = None
    for weight in fast_weights(left, btab, places):
        part = weight[:, 0:TP] + weight[:, TP : 2 * TP]
        total = part if total is None else total + part
    return to_row(total, eye)


def rows_of(ref, place, row, count):
    return jnp.broadcast_to(ref[place[0], place[1], row : row + 1, :], (count, TP))


def slow_sum(ext, row, col, places, eye):
    cols = jnp.transpose(ext[row, col])
    sums = []
    for block in range(TP // ROWS):
        here = cols[block * ROWS : (block + 1) * ROWS]
        spot = [jnp.broadcast_to(here[:, c : c + 1], (ROWS, TP)) for c in range(3)]
        total = jnp.zeros((ROWS, TP), F32)
        for place in places:
            distance = None
            for c in range(3):
                offset = spot[c] - rows_of(ext, place, c, ROWS)
                square = offset * offset
                distance = square if distance is None else distance + square
            total = total + rows_of(ext, place, 6, ROWS) * jnp.exp(-distance)
        sums.append(jnp.sum(total, axis=1, keepdims=True))
    return jnp.sum(jnp.where(eye, jnp.concatenate(sums, axis=0), 0.0), axis=0, keepdims=True)


def slow_accel(ext, press_ref, damp_ref, row, col, places, eye):
    cols = jnp.transpose(ext[row, col])
    more = jnp.transpose(
        jnp.broadcast_to(press_ref[row - 1, pl.ds(col - 1, 1), :], (8, TP))
    )
    sums = [[], [], []]
    for block in range(TP // ROWS):
        span = slice(block * ROWS, (block + 1) * ROWS)
        here = cols[span]
        spot = [jnp.broadcast_to(here[:, c : c + 1], (ROWS, TP)) for c in range(3)]
        speed = [jnp.broadcast_to(here[:, 3 + c : 4 + c], (ROWS, TP)) for c in range(3)]
        press_here = jnp.broadcast_to(more[span, 0:1], (ROWS, TP))
        total = [jnp.zeros((ROWS, TP), F32) for c in range(3)]
        for place in places:
            offsets = [spot[c] - rows_of(ext, place, c, ROWS) for c in range(3)]
            distance = offsets[0] * offsets[0] + offsets[1] * offsets[1]
            distance = distance + offsets[2] * offsets[2]
            weight = rows_of(ext, place, 6, ROWS) * jnp.exp(-distance)
            there = (place[0] - 1, pl.ds(place[1] - 1, 1), slice(None))
            press = weight * (press_here + jnp.broadcast_to(press_ref[there], (ROWS, TP)))
            damp = weight * jnp.broadcast_to(damp_ref[there], (ROWS, TP))
            for c in range(3):
                relative = rows_of(ext, place, 3 + c, ROWS) - speed[c]
                total[c] = total[c] + (press * offsets[c] + damp * relative)
        for c in range(3):
            sums[c].append(jnp.sum(total[c], axis=1, keepdims=True))
    return [
        jnp.sum(jnp.where(eye, jnp.concatenate(part, axis=0), 0.0), axis=0, keepdims=True)
        for part in sums
    ]


def state_of(summed):
    density = 1.0 + summed * (1.0 / TP)
    press = (2.0 * stiffness) * (density - rest_density) / (density * density)
    return press, viscosity / density


def fill_sources(ext, btab, first, last, left, right):
    def step(row, carry):
        for col in range(left, right):
            btab[row, col] = augmented(ext[row, col], True).astype(BF16)
        return carry

    lax.fori_loop(first, last, step, 0)


def left_of(ext, row, col):
    return jnp.transpose(augmented(ext[row, col], False)).astype(BF16)


def prep_kernel(counts_in, codes_in, soil_in, out, counts, codes, soil, sems):
    copies = [
        pltpu.make_async_copy(counts_in, counts, sems.at[0]),
        pltpu.make_async_copy(codes_in, codes, sems.at[1]),
        pltpu.make_async_copy(soil_in, soil, sems.at[2]),
    ]
    for copy in copies:
        copy.start()
    for copy in copies:
        copy.wait()
    layers, columns = out.shape[0], out.shape[1]
    lane = lax.broadcasted_iota(jnp.int32, (1, TP), 1)
    for layer in range(layers):
        for column in range(columns):
            listed = jnp.zeros((1, TP), jnp.int32)
            for k in range(6):
                listed = jnp.where(lane == k, codes[k, layer, column], listed)
            live = jnp.where(lane < counts[layer, column], 1.0, 0.0)
            rows = [soil[layer, c, column : column + 1, :] for c in range(6)]
            out[layer, column] = jnp.concatenate(rows + [live, listed.astype(F32)], axis=0)


def rim_tile(index, layers, columns):
    side = index - 2 * columns
    on_side, last = side >= 0, index >= columns
    layer = jnp.where(on_side, 1 + (side >> 1), jnp.where(last, layers - 1, 0))
    column = jnp.where(
        on_side, (columns - 1) * (side & 1), jnp.where(last, index - columns, index)
    )
    return layer, column


def inner_kernel(codes, own, lefts, sums, btab):
    layers, columns = own.shape[0], own.shape[1]
    eye = eye_mask()
    fill_sources(own, btab, 0, layers, 0, columns)

    def turn(layer, carry):
        for column in range(columns):
            lefts[layer, column] = left_of(own, layer, column)
        return carry

    lax.fori_loop(0, layers, turn, 0)

    def step(layer, carry):
        for column in range(1, columns - 1):
            places = near(codes, layer, column, layer, column)
            row = fast_sum(lefts[layer, column], btab, places, eye)
            sums[layer, column : column + 1, :] = row
        return carry

    lax.fori_loop(1, layers - 1, step, 0)


def density_kernel(codes, own, west, east, up, down, lefts, inner, out, ext, btab, sums):
    layers, columns = own.shape[0], own.shape[1]
    assemble(own, west, east, up, down, ext)
    eye = eye_mask()
    fast = moderate(ext)
    sums[...] = inner[...]

    @pl.when(fast)
    def _():
        fill_sources(ext, btab, 1, layers + 3, 1, columns + 3)
        rim = 2 * columns + 2 * (layers - 2)

        def step(group, carry):
            for part in range(TILES):
                index = group * TILES + part
                layer, column = rim_tile(index, layers, columns)
                places = near(codes, layer, column, layer + 2, column + 2)
                row = fast_sum(lefts[layer, column], btab, places, eye)
                sums[layer, pl.ds(column, 1), :] = row
            return carry

        lax.fori_loop(0, rim // TILES, step, 0)

    @pl.when(jnp.logical_not(fast))
    def _():
        def step(tile, carry):
            layer, column = tile // columns, tile % columns
            places = near(codes, layer, column, layer + 2, column + 2)
            row = slow_sum(ext, layer + 2, column + 2, places, eye)
            sums[layer, pl.ds(column, 1), :] = row
            return carry

        lax.fori_loop(0, layers * columns, step, 0)

    for layer in range(layers):
        span = slice(layer * columns, (layer + 1) * columns)
        press, damp = state_of(sums[layer])
        live = jnp.concatenate([own[layer, c, 6:7, :] for c in range(columns)], axis=0)
        out[0, span, :] = press
        out[1, span, :] = damp
        out[2, span, :] = press * live
        out[3, span, :] = damp * live


def ring_kernel(
    codes, own, west, east, up, down, extra, ext, sources, ftab, press_ref, damp_ref, btab
):
    layers, columns = own.shape[0], own.shape[1]
    assemble(own, west, east, up, down, ext)
    eye = eye_mask()
    fast = moderate(ext)
    for layer in range(layers):
        span = slice(layer * columns, (layer + 1) * columns)
        press_ref[layer + 1, 1 : columns + 1, :] = extra[0, span, :]
        damp_ref[layer + 1, 1 : columns + 1, :] = extra[1, span, :]

    def ring(handle):
        def across(index, carry):
            handle(1, index + 1)
            handle(layers + 2, index + 1)
            return carry

        def along(index, carry):
            handle(index + 2, 1)
            handle(index + 2, columns + 2)
            return carry

        lax.fori_loop(0, columns + 2, across, 0)
        lax.fori_loop(0, layers, along, 0)

    def keep(row, col, summed):
        press, damp = state_of(summed)
        press_ref[row - 1, pl.ds(col - 1, 1), :] = press
        damp_ref[row - 1, pl.ds(col - 1, 1), :] = damp

    @pl.when(fast)
    def _():
        fill_sources(ext, btab, 0, layers + 4, 0, columns + 4)

        sources[...] = btab[1 : layers + 3, 1 : columns + 3]

        def ring_sum(row, col):
            places = near(codes, row, col, row, col)
            keep(row, col, fast_sum(left_of(ext, row, col), btab, places, eye))

        ring(ring_sum)

        def factors(row, carry):
            for col in range(1, columns + 3):
                raw = ext[row, col]
                press = jnp.broadcast_to(press_ref[row - 1, col - 1 : col, :], (8, TP))
                damp = jnp.broadcast_to(damp_ref[row - 1, col - 1 : col, :], (8, TP))
                value = jnp.concatenate([raw, press * raw, damp * raw], axis=0)
                high = value.astype(BF16).astype(F32)
                ftab[row - 1, col - 1] = jnp.concatenate([high, value - high], axis=0).astype(BF16)
            return carry

        lax.fori_loop(1, layers + 3, factors, 0)

    @pl.when(jnp.logical_not(fast))
    def _():
        def ring_sum(row, col):
            places = near(codes, row, col, row, col)
            keep(row, col, slow_sum(ext, row, col, places, eye))

        ring(ring_sum)


def accel_kernel(codes, ext, btab, ftab, press_ref, damp_ref, out, pairs, lefts):
    layers, columns = out.shape[0], out.shape[2]
    eye = eye_mask()
    fast = moderate(ext)

    def weigh(layer):
        for column in range(columns):
            lefts[column] = left_of(ext, layer + 2, column + 2)
        for column in range(columns):
            places = near(codes, layer, column, layer + 1, column + 1)
            for p, weight in enumerate(fast_weights(lefts[column], btab, places)):
                high = weight.astype(BF16)
                pairs[column, p, :, 0 : 2 * TP] = high
                pairs[column, p, :, 2 * TP : 4 * TP] = (weight - high.astype(F32)).astype(BF16)

    def gather(layer):
        for column in range(columns):
            row, col = layer + 2, column + 2
            places = near(codes, layer, column, row - 1, col - 1)
            summed = None
            for p in range(3):
                source = jnp.concatenate([ftab[places[2 * p]], ftab[places[2 * p + 1]]], axis=1)
                part = lax.dot_general(
                    jnp.concatenate([source, source], axis=1),
                    pairs[column, p],
                    NT,
                    preferred_element_type=F32,
                )
                summed = part if summed is None else summed + part
            summed = summed[0:24] + summed[24:48]
            plain, pressed, damped = summed[0:8], summed[8:16], summed[16:24]
            raw = ext[row, col]
            press = press_ref[row - 1, col - 1 : col, :]
            push = raw * (press * plain[6:7] + pressed[6:7]) - (press * plain + pressed)
            drag = damped - raw * damped[6:7]
            total = (push[0:3] + drag[3:6]) * (raw[6:7] * (1.0 / TP))
            for c in range(3):
                out[layer, c, column : column + 1, :] = total[c : c + 1]

    @pl.when(fast)
    def _():
        def step(layer, carry):
            weigh(layer)
            gather(layer)
            return carry

        lax.fori_loop(0, layers, step, 0)

    @pl.when(jnp.logical_not(fast))
    def _():
        def step(tile, carry):
            layer, column = tile // columns, tile % columns
            row, col = layer + 2, column + 2
            places = near(codes, layer, column, row, col)
            rows = slow_accel(ext, press_ref, damp_ref, row, col, places, eye)
            scale = ext[row, col, 6:7, :] * (1.0 / TP)
            for c in range(3):
                out[layer, c, pl.ds(column, 1), :] = rows[c] * scale
            return carry

        lax.fori_loop(0, layers * columns, step, 0)


def owner_lags():
    row = row_mask()
    return [(row + 8 * k) // 6 for k in range(3)]


def folded(rows):
    return (rows[0:6] + rows[6:12]) + (rows[12:18] + rows[18:24])


def share_kernel(blocks, out):
    quads = blocks.shape[0] // 24
    rows = folded(jnp.sum(blocks[...].reshape((quads, 24, TP)), axis=0))
    out[...] = jnp.concatenate([rows, jnp.zeros((2, TP), F32)], axis=0)


def marker_kernel(soil, extra, place, speed, tiles, owners, slots, out, table, lookup):
    layers, columns = soil.shape[0], soil.shape[2]
    count = layers * columns
    pairs = place.shape[1] // (2 * TP)
    quads = out.shape[0] // 24
    groups = TP // 16
    field_of = lambda f: jnp.concatenate([soil[layer, f] for layer in range(layers)], axis=0)
    spots = [field_of(c) for c in range(3)]
    moves = [field_of(3 + c) for c in range(3)]
    press, damp = extra[2], extra[3]
    scaled = [jnp.clip(spot, -CLIP, CLIP) * SCALE for spot in spots]
    norm = -0.5 * (scaled[0] * scaled[0] + scaled[1] * scaled[1] + scaled[2] * scaled[2])
    fields = scaled + [norm, press, damp]
    fields = fields + [damp * moves[c] - press * spots[c] for c in range(3)]
    for number, field in enumerate(fields):
        if number < ONEHOT:
            pieces = list(split3(field)) + [jnp.zeros((TP - 3 * count, TP), F32)]
            turned = jnp.transpose(jnp.concatenate(pieces, axis=0)).astype(BF16)
            for group in range(groups):
                at = (group * ONEHOT + number) * 16
                table[at : at + 16, :] = turned[group * 16 : group * 16 + 16]
        else:
            pieces = [field, jnp.zeros((TP - count, TP), F32)]
            lookup[number - ONEHOT] = jnp.transpose(jnp.concatenate(pieces, axis=0))
    entry = lax.broadcasted_iota(jnp.int32, (TP, TP), 0)
    listed = jnp.where(entry < 3 * count, lax.rem(entry, count), -1)
    out[...] = jnp.zeros(out.shape, F32)

    lags = owner_lags()

    def add_terms(pair, terms):
        left, right = [], []
        for part in range(2):
            block = pair * 2 + part
            value = terms[:, part * TP : (part + 1) * TP]
            high = value.astype(BF16).astype(F32)
            owner = jnp.broadcast_to(owners[pl.ds(block, 1), :], (8, TP))
            late = [owner - lag for lag in lags]
            slot = jnp.broadcast_to(slots[pl.ds(block, 1), :], (TP, TP))
            hot = jnp.where(slot == entry, 1.0, 0.0).astype(BF16)
            masks = [late[k] == 4 * quad for quad in range(quads) for k in range(3)]
            for piece in (high, value - high):
                turned = [
                    jnp.concatenate(
                        [piece[(8 * k + r) % 6 : (8 * k + r) % 6 + 1] for r in range(8)], axis=0
                    )
                    for k in range(3)
                ]
                left.append(
                    jnp.concatenate(
                        [jnp.where(mask, turned[n % 3], 0.0) for n, mask in enumerate(masks)],
                        axis=0,
                    ).astype(BF16)
                )
                right.append(hot)
        out[...] = out[...] + lax.dot_general(
            jnp.concatenate(left, axis=1),
            jnp.concatenate(right, axis=1),
            NT,
            preferred_element_type=F32,
        )

    def forces_on(pair):
        wide = 2 * TP
        lanes = pl.ds(pl.multiple_of(pair * wide, wide), wide)
        which = [
            jnp.broadcast_to(tiles[pl.ds(pair * 2 + part, 1), :], (TP, TP)) for part in range(2)
        ]
        hot = jnp.concatenate(
            [jnp.where(w == listed, 1.0, 0.0).astype(BF16) for w in which], axis=1
        )
        y = place[:, lanes]
        u = speed[:, lanes]
        spread = y * SCALE
        at = [jnp.broadcast_to(spread[c : c + 1], (16, wide)) for c in range(3)]
        totals = [jnp.zeros((16, wide), F32) for number in range(5)]
        for group in range(groups):
            span = slice(group * 16, group * 16 + 16)
            rows = slice(group * 16 * ONEHOT, (group + 1) * 16 * ONEHOT)
            got = []
            if ONEHOT:
                picked = lax.dot_general(
                    table[rows, :], hot, (((1,), (0,)), ((), ())), preferred_element_type=F32
                )
                got = [picked[16 * number : 16 * number + 16] for number in range(ONEHOT)]
            for number in range(9 - ONEHOT):
                source = lookup[number, span, :]
                got.append(
                    jnp.concatenate(
                        [jnp.take_along_axis(source, w[0:16], axis=1) for w in which], axis=1
                    )
                )
            power = (got[3] + at[0] * got[0]) + (at[1] * got[1] + at[2] * got[2])
            weight = jnp.exp2(power)
            for number in range(5):
                totals[number] = totals[number] + weight * got[4 + number]
        sums = [jnp.sum(total, axis=0, keepdims=True) for total in totals]
        square = spread * spread
        scale = jnp.exp2(-0.5 * (square[0:1] + square[1:2] + square[2:3])) * (1.0 / TP)
        where = [y[c : c + 1] for c in range(3)]
        force = [
            (where[c] * sums[0] + (sums[2 + c] - u[c : c + 1] * sums[1])) * scale
            for c in range(3)
        ]
        moment = cross(where, force)
        return jnp.concatenate(force + moment + [jnp.zeros((2, wide), F32)], axis=0)

    def step(pair, terms):
        add_terms(jnp.maximum(pair - 1, 0), terms)
        return forces_on(pair)

    terms = lax.fori_loop(0, pairs, step, jnp.zeros((8, 2 * TP), F32))
    add_terms(pairs - 1, terms)


def cross(a, b):
    return [
        a[1] * b[2] - a[2] * b[1],
        a[2] * b[0] - a[0] * b[2],
        a[0] * b[1] - a[1] * b[0],
    ]


def advance_kernel(first, second, third, fourth, state, inertia, out, sent):
    totals = (first[...] + second[...]) + (third[...] + fourth[...])
    row = lambda ref, r: ref[r : r + 1, :]
    force = [totals[c : c + 1] for c in range(3)]
    moments = [totals[3 + c : 4 + c] for c in range(3)]
    center = [row(state, c) for c in range(3)]
    velocity = [row(state, 3 + c) for c in range(3)]
    spin = [row(state, 6 + c) for c in range(3)]
    inv_mass = row(inertia, 0)
    moment = [row(inertia, 1 + c) for c in range(3)]
    arm = cross(center, force)
    gyro = cross(spin, [moment[c] * spin[c] for c in range(3)])
    pull = [0.0, 0.0, -gravity]
    new_vel = [velocity[c] + time_step * (inv_mass * force[c] + pull[c]) for c in range(3)]
    new_spin = [
        spin[c] + time_step * ((moments[c] - arm[c]) - gyro[c]) / moment[c] for c in range(3)
    ]
    new_center = [center[c] + time_step * new_vel[c] for c in range(3)]
    out[...] = jnp.concatenate(new_center + new_vel + new_spin, axis=0)
    swing = cross(new_spin, center)
    base = [new_vel[c] - swing[c] for c in range(3)]
    block = jnp.concatenate((base + new_spin) * 4, axis=0)
    quads = sent.shape[0] // 24
    sent[...] = jnp.broadcast_to(block[None], (quads, 24, TP)).reshape(sent.shape)


def pick_kernel(states, place, owners, slots, out):
    steps = place.shape[1] // (PICK * TP)
    quads = states.shape[0] // 24
    lags = owner_lags()

    def step(index, carry):
        for part in range(PICK):
            block = index * PICK + part
            lanes = pl.ds(pl.multiple_of(block * TP, TP), TP)
            slot = jnp.broadcast_to(slots[pl.ds(block, 1), :], (8, TP))
            owner = jnp.broadcast_to(owners[pl.ds(block, 1), :], (8, TP))
            late = [owner - lag for lag in lags]
            found = [jnp.zeros((8, TP), F32) for k in range(3)]
            for quad in range(quads):
                for k in range(3):
                    at = 24 * quad + 8 * k
                    here = jnp.take_along_axis(states[at : at + 8, :], slot, axis=1)
                    found[k] = jnp.where(late[k] == 4 * quad, here, found[k])
            picked = folded(jnp.concatenate(found, axis=0))
            y = place[:, lanes]
            turn = cross(
                [picked[3 + c : 4 + c] for c in range(3)], [y[c : c + 1] for c in range(3)]
            )
            out[:, lanes] = picked[0:3] + jnp.concatenate(turn, axis=0)
        return carry

    lax.fori_loop(0, steps, step, 0)


def shifted(shard, axis, dim, width):
    size, length = lax.axis_size(axis), shard.shape[dim]
    up = [(i, i + 1) for i in range(size - 1)]
    down = [(j, i) for i, j in up]
    last = lax.slice_in_dim(shard, length - width, length, axis=dim)
    first = lax.slice_in_dim(shard, 0, width, axis=dim)
    return lax.ppermute(last, axis, up), lax.ppermute(first, axis, down)


def local(
    soil_state,
    tile_count,
    tile_neighbors,
    marker_pos,
    marker_vel,
    marker_tile,
    marker_owner,
    marker_slot,
    body_state,
    body_inertia,
):
    layers, columns, fields, tile_size = soil_state.shape
    marker_count = marker_pos.shape[1]
    tile_devs = lax.axis_size("tile")
    depth_devs = lax.axis_size("depth")
    soil = jnp.transpose(soil_state, (0, 2, 1, 3))
    codes = jnp.transpose(tile_neighbors, (2, 0, 1))
    own = pl.pallas_call(
        prep_kernel,
        out_shape=jax.ShapeDtypeStruct((layers, columns, 8, TP), F32),
        in_specs=[pl.BlockSpec(memory_space=pltpu.HBM)] * 3,
        out_specs=vspec(),
        scratch_shapes=[
            SMEM((layers, columns), jnp.int32),
            SMEM((6, layers, columns), jnp.int32),
            VMEM((layers, fields, columns, TP), F32),
            pltpu.SemaphoreType.DMA((3,)),
        ],
        compiler_params=params(),
        name="prep",
    )(*[pltpu.with_memory_space_constraint(x, pltpu.HBM) for x in (tile_count, codes, soil)])
    lefts, inner = pl.pallas_call(
        inner_kernel,
        out_shape=(
            jax.ShapeDtypeStruct((layers, columns, TP, AUG), BF16),
            jax.ShapeDtypeStruct((layers, columns, TP), F32),
        ),
        in_specs=[sspec(), vspec()],
        out_specs=(vspec(), vspec()),
        scratch_shapes=[VMEM((layers, columns, AUG, TP), BF16)],
        cost_estimate=cost(4_000_000, 1 << 18, 1_000_000),
        compiler_params=params(),
        name="inner",
    )(codes, own)
    west, east = shifted(own, "tile", 1, 2)
    top = jnp.concatenate([west[:2], own[:2], east[:2]], axis=1)
    bottom = jnp.concatenate([west[-2:], own[-2:], east[-2:]], axis=1)
    rim = jnp.concatenate([top, bottom], axis=0)
    up, down = shifted(rim, "depth", 0, 2)
    pieces = (own, west, east, up, down)
    span, width = layers + 4, columns + 4
    pairs = layers * columns * 6 * TP * TP
    extra = pl.pallas_call(
        density_kernel,
        out_shape=jax.ShapeDtypeStruct((4, layers * columns, TP), F32),
        in_specs=[sspec()] + [vspec()] * 7,
        out_specs=vspec(),
        scratch_shapes=[
            VMEM((span, width, 8, TP), F32),
            VMEM((span, width, AUG, TP), BF16),
            VMEM((layers, columns, TP), F32),
        ],
        cost_estimate=cost(pairs * 12, 1 << 18, pairs),
        compiler_params=params(),
        name="density",
    )(codes, *pieces, lefts, inner)
    owners = marker_owner.reshape((marker_count // TP, TP))
    slots = marker_slot.reshape((marker_count // TP, TP))
    tiles = marker_tile.reshape((marker_count // TP, TP))
    partial_sums = pl.pallas_call(
        marker_kernel,
        out_shape=jax.ShapeDtypeStruct((tile_devs * 6, TP), F32),
        in_specs=[vspec()] * 7,
        out_specs=vspec(),
        scratch_shapes=[VMEM((9 * TP, TP), BF16), VMEM((9, TP, TP), F32)],
        cost_estimate=cost(marker_count * TP * 25, 1 << 19, marker_count * TP),
        compiler_params=params(),
        name="markers",
    )(soil, extra, marker_pos, marker_vel, tiles, owners, slots)
    partial_sums, extra = lax.optimization_barrier((partial_sums, extra))
    flat = (tile_devs, 1, 6 * TP)
    arrived = lax.all_to_all(partial_sums.reshape(flat), "tile", 0, 0, tiled=True)
    own, west, east, up, down = pieces
    ring_codes = jnp.concatenate(
        [
            part[:, :, 7, 0:6]
            for part in (up, jnp.concatenate([west, own, east], axis=1), down)
        ],
        axis=0,
    )
    ring_codes = jnp.transpose(ring_codes.astype(jnp.int32), (2, 0, 1))
    shapes = (
        jax.ShapeDtypeStruct((span, width, 8, TP), F32),
        jax.ShapeDtypeStruct((layers + 2, columns + 2, AUG, TP), BF16),
        jax.ShapeDtypeStruct((layers + 2, columns + 2, FACTORS, TP), BF16),
        jax.ShapeDtypeStruct((layers + 2, 16, TP), F32),
        jax.ShapeDtypeStruct((layers + 2, 16, TP), F32),
    )
    tables = pl.pallas_call(
        ring_kernel,
        out_shape=shapes,
        in_specs=[sspec()] + [vspec()] * 6,
        out_specs=(vspec(),) * 5,
        scratch_shapes=[VMEM((span, width, AUG, TP), BF16)],
        cost_estimate=cost(pairs * 15, 1 << 19, pairs),
        compiler_params=params(),
        name="ring",
    )(ring_codes, *pieces, extra)
    arrived, damp = lax.optimization_barrier((arrived, tables[4]))
    share = pl.pallas_call(
        share_kernel,
        out_shape=jax.ShapeDtypeStruct((8, TP), F32),
        in_specs=[vspec()],
        out_specs=vspec(),
        compiler_params=params(),
        name="share",
    )(arrived.reshape((tile_devs * 6, TP)))

    others = [
        lax.ppermute(share, "depth", [(i, (i + k) % depth_devs) for i in range(depth_devs)])
        for k in range(1, depth_devs)
    ]
    body_next, sent = pl.pallas_call(
        advance_kernel,
        out_shape=(
            jax.ShapeDtypeStruct((9, TP), F32),
            jax.ShapeDtypeStruct((tile_devs * 6, TP), F32),
        ),
        in_specs=[vspec()] * 6,
        out_specs=(vspec(), vspec()),
        compiler_params=params(),
        name="advance",
    )(share, *others, body_state, body_inertia)
    sent, damp = lax.optimization_barrier((sent, damp))
    states = lax.all_to_all(sent.reshape(flat), "tile", 0, 0, tiled=True)
    accel = pl.pallas_call(
        accel_kernel,
        out_shape=jax.ShapeDtypeStruct((layers, 3, columns, TP), F32),
        in_specs=[sspec()] + [vspec()] * 5,
        out_specs=vspec(),
        scratch_shapes=[VMEM((columns, 3, TP, 4 * TP), BF16), VMEM((columns, TP, AUG), BF16)],
        cost_estimate=cost(pairs * 15, 1 << 19, pairs),
        compiler_params=params(),
        name="accel",
    )(codes, *tables[:4], damp)
    states, accel = lax.optimization_barrier((states, accel))
    soil_accel = jnp.transpose(accel, (0, 2, 1, 3))
    marker_vel_next = pl.pallas_call(
        pick_kernel,
        out_shape=jax.ShapeDtypeStruct((3, marker_count), F32),
        in_specs=[vspec()] * 4,
        out_specs=vspec(),
        compiler_params=params(),
        name="pick",
    )(states.reshape((tile_devs * 6, TP)), marker_pos, owners, slots)
    return (soil_accel, body_next, marker_vel_next)


def solution(mesh):
    placed = (
        P("depth", "tile", None, None),
        P("depth", "tile"),
        P("depth", "tile", None),
        P(None, ("tile", "depth")),
        P(None, ("tile", "depth")),
        P(("tile", "depth")),
        P(("tile", "depth"), None),
        P(("tile", "depth")),
        P(None, "tile"),
        P(None, "tile"),
    )
    return jax.shard_map(
        local,
        mesh=mesh,
        in_specs=placed,
        out_specs=(P("depth", "tile", None, None), P(None, "tile"), P(None, ("tile", "depth"))),
        check_vma=False,
    )
```

```python
import functools

import jax
import jax.numpy as jnp
from jax import lax
from jax.experimental import pallas as pl
from jax.experimental.pallas import tpu as pltpu
from jax.sharding import PartitionSpec as P

stiffness = 40.0
rest_density = 2.0
viscosity = 20.0
time_step = 0.05
gravity = 1.0
VMEM = pltpu.VMEM
SMEM = pltpu.SMEM
TP = 128
ROWS = 16
AUG = 48
FACTORS = 48
TILES = 10
ONEHOT = 9
PICK = 8
SCALE = (2.0 * 1.4426950408889634) ** 0.5
FAR = 1e30
PLACE_LIMIT = 4.0
CLIP = 1e4
SPEED_LIMIT = 8.0
F32 = jnp.float32
BF16 = jnp.bfloat16
NT = (((1,), (1,)), ((), ()))


def vspec():
    return pl.BlockSpec(memory_space=VMEM)


def sspec():
    return pl.BlockSpec(memory_space=SMEM)


def params(limit=16 << 20):
    return pltpu.CompilerParams(vmem_limit_bytes=limit)


def cost(flops, moved, heavy=0):
    return pl.CostEstimate(flops=flops, bytes_accessed=moved, transcendentals=heavy)


def row_mask():
    return lax.broadcasted_iota(jnp.int32, (8, TP), 0)


def eye_mask():
    return lax.broadcasted_iota(jnp.int32, (TP, TP), 0) == lax.broadcasted_iota(
        jnp.int32, (TP, TP), 1
    )


def split3(value):
    high = value.astype(BF16).astype(F32)
    rest = value - high
    middle = rest.astype(BF16).astype(F32)
    return high, middle, rest - middle


def augmented(raw, source):
    row = row_mask()
    scaled = raw * SCALE
    square = scaled * scaled
    norm = -0.5 * (square[0:1] + square[1:2] + square[2:3])
    if source:
        third, fourth = norm + (raw[6:7] - 1.0) * FAR, jnp.ones((1, TP), F32)
    else:
        third, fourth = jnp.ones((1, TP), F32), norm
    full = jnp.where(
        row < 3, scaled, jnp.where(row == 3, third, jnp.where(row == 4, fourth, 0.0))
    )
    h, m, l = split3(full)
    return jnp.concatenate([h, m, h, m, l, h] if source else [h, h, m, m, h, l], axis=0)


def assemble(own, west, east, up, down, ext):
    layers, columns = own.shape[0], own.shape[1]
    ext[0:2] = up[...]
    ext[layers + 2 : layers + 4] = down[...]
    ext[2 : layers + 2, 0:2] = west[...]
    ext[2 : layers + 2, columns + 2 : columns + 4] = east[...]
    ext[2 : layers + 2, 2 : columns + 2] = own[...]


def moderate(ext):
    span, width = ext.shape[0], ext.shape[1]
    flat = ext[...].reshape((span * width, 8, TP))
    peak = jnp.max(jnp.abs(flat), axis=0)
    row = row_mask()
    ratio = jnp.where(
        row < 3, peak / PLACE_LIMIT, jnp.where(row < 6, peak / SPEED_LIMIT, 0.0)
    )
    return jnp.max(ratio) <= 1.0


def near(codes, layer, column, row, col):
    places = []
    for k in range(6):
        code = codes[k, layer, column]
        down = (code * 11) >> 5
        places.append((row + down - 1, col + code - 3 * down - 1))
    return places


def to_row(total, eye):
    sums = jnp.sum(total, axis=1, keepdims=True)
    return jnp.sum(jnp.where(eye, sums, 0.0), axis=0, keepdims=True)


def fast_weights(left, btab, places):
    weights = []
    for p in range(3):
        right = jnp.concatenate([btab[places[2 * p]], btab[places[2 * p + 1]]], axis=1)
        weights.append(
            jnp.exp2(lax.dot_general(left, right, (((1,), (0,)), ((), ())), preferred_element_type=F32))
        )
    return weights


def fast_sum(left, btab, places, eye):
    total = None
    for weight in fast_weights(left, btab, places):
        part = weight[:, 0:TP] + weight[:, TP : 2 * TP]
        total = part if total is None else total + part
    return to_row(total, eye)


def rows_of(ref, place, row, count):
    return jnp.broadcast_to(ref[place[0], place[1], row : row + 1, :], (count, TP))


def slow_sum(ext, row, col, places, eye):
    cols = jnp.transpose(ext[row, col])
    sums = []
    for block in range(TP // ROWS):
        here = cols[block * ROWS : (block + 1) * ROWS]
        spot = [jnp.broadcast_to(here[:, c : c + 1], (ROWS, TP)) for c in range(3)]
        total = jnp.zeros((ROWS, TP), F32)
        for place in places:
            distance = None
            for c in range(3):
                offset = spot[c] - rows_of(ext, place, c, ROWS)
                square = offset * offset
                distance = square if distance is None else distance + square
            total = total + rows_of(ext, place, 6, ROWS) * jnp.exp(-distance)
        sums.append(jnp.sum(total, axis=1, keepdims=True))
    return jnp.sum(jnp.where(eye, jnp.concatenate(sums, axis=0), 0.0), axis=0, keepdims=True)


def slow_accel(ext, press_ref, damp_ref, row, col, places, eye):
    cols = jnp.transpose(ext[row, col])
    more = jnp.transpose(
        jnp.broadcast_to(press_ref[row - 1, pl.ds(col - 1, 1), :], (8, TP))
    )
    sums = [[], [], []]
    for block in range(TP // ROWS):
        span = slice(block * ROWS, (block + 1) * ROWS)
        here = cols[span]
        spot = [jnp.broadcast_to(here[:, c : c + 1], (ROWS, TP)) for c in range(3)]
        speed = [jnp.broadcast_to(here[:, 3 + c : 4 + c], (ROWS, TP)) for c in range(3)]
        press_here = jnp.broadcast_to(more[span, 0:1], (ROWS, TP))
        total = [jnp.zeros((ROWS, TP), F32) for c in range(3)]
        for place in places:
            offsets = [spot[c] - rows_of(ext, place, c, ROWS) for c in range(3)]
            distance = offsets[0] * offsets[0] + offsets[1] * offsets[1]
            distance = distance + offsets[2] * offsets[2]
            weight = rows_of(ext, place, 6, ROWS) * jnp.exp(-distance)
            there = (place[0] - 1, pl.ds(place[1] - 1, 1), slice(None))
            press = weight * (press_here + jnp.broadcast_to(press_ref[there], (ROWS, TP)))
            damp = weight * jnp.broadcast_to(damp_ref[there], (ROWS, TP))
            for c in range(3):
                relative = rows_of(ext, place, 3 + c, ROWS) - speed[c]
                total[c] = total[c] + (press * offsets[c] + damp * relative)
        for c in range(3):
            sums[c].append(jnp.sum(total[c], axis=1, keepdims=True))
    return [
        jnp.sum(jnp.where(eye, jnp.concatenate(part, axis=0), 0.0), axis=0, keepdims=True)
        for part in sums
    ]


def state_of(summed):
    density = 1.0 + summed * (1.0 / TP)
    press = (2.0 * stiffness) * (density - rest_density) / (density * density)
    return press, viscosity / density


def fill_sources(ext, btab, first, last, left, right):
    def step(row, carry):
        for col in range(left, right):
            btab[row, col] = augmented(ext[row, col], True).astype(BF16)
        return carry

    lax.fori_loop(first, last, step, 0)


def left_of(ext, row, col):
    return jnp.transpose(augmented(ext[row, col], False)).astype(BF16)


def prep_kernel(counts_in, codes_in, soil_in, out, counts, codes, soil, sems):
    copies = [
        pltpu.make_async_copy(counts_in, counts, sems.at[0]),
        pltpu.make_async_copy(codes_in, codes, sems.at[1]),
        pltpu.make_async_copy(soil_in, soil, sems.at[2]),
    ]
    for copy in copies:
        copy.start()
    for copy in copies:
        copy.wait()
    layers, columns = out.shape[0], out.shape[1]
    lane = lax.broadcasted_iota(jnp.int32, (1, TP), 1)
    for layer in range(layers):
        for column in range(columns):
            listed = jnp.zeros((1, TP), jnp.int32)
            for k in range(6):
                listed = jnp.where(lane == k, codes[k, layer, column], listed)
            live = jnp.where(lane < counts[layer, column], 1.0, 0.0)
            rows = [soil[layer, c, column : column + 1, :] for c in range(6)]
            out[layer, column] = jnp.concatenate(rows + [live, listed.astype(F32)], axis=0)


def rim_tile(index, layers, columns):
    side = index - 2 * columns
    on_side, last = side >= 0, index >= columns
    layer = jnp.where(on_side, 1 + (side >> 1), jnp.where(last, layers - 1, 0))
    column = jnp.where(
        on_side, (columns - 1) * (side & 1), jnp.where(last, index - columns, index)
    )
    return layer, column


def inner_kernel(codes, own, lefts, sums, btab):
    layers, columns = own.shape[0], own.shape[1]
    eye = eye_mask()
    fill_sources(own, btab, 0, layers, 0, columns)

    def turn(layer, carry):
        for column in range(columns):
            lefts[layer, column] = left_of(own, layer, column)
        return carry

    lax.fori_loop(0, layers, turn, 0)

    def step(layer, carry):
        for column in range(1, columns - 1):
            places = near(codes, layer, column, layer, column)
            row = fast_sum(lefts[layer, column], btab, places, eye)
            sums[layer, column : column + 1, :] = row
        return carry

    lax.fori_loop(1, layers - 1, step, 0)


def density_kernel(codes, own, west, east, up, down, lefts, inner, out, ext, btab, sums):
    layers, columns = own.shape[0], own.shape[1]
    assemble(own, west, east, up, down, ext)
    eye = eye_mask()
    fast = moderate(ext)
    sums[...] = inner[...]

    @pl.when(fast)
    def _():
        fill_sources(ext, btab, 1, layers + 3, 1, columns + 3)
        rim = 2 * columns + 2 * (layers - 2)

        def step(group, carry):
            for part in range(TILES):
                index = group * TILES + part
                layer, column = rim_tile(index, layers, columns)
                places = near(codes, layer, column, layer + 2, column + 2)
                row = fast_sum(lefts[layer, column], btab, places, eye)
                sums[layer, pl.ds(column, 1), :] = row
            return carry

        lax.fori_loop(0, rim // TILES, step, 0)

    @pl.when(jnp.logical_not(fast))
    def _():
        def step(tile, carry):
            layer, column = tile // columns, tile % columns
            places = near(codes, layer, column, layer + 2, column + 2)
            row = slow_sum(ext, layer + 2, column + 2, places, eye)
            sums[layer, pl.ds(column, 1), :] = row
            return carry

        lax.fori_loop(0, layers * columns, step, 0)

    for layer in range(layers):
        span = slice(layer * columns, (layer + 1) * columns)
        press, damp = state_of(sums[layer])
        live = jnp.concatenate([own[layer, c, 6:7, :] for c in range(columns)], axis=0)
        out[0, span, :] = press
        out[1, span, :] = damp
        out[2, span, :] = press * live
        out[3, span, :] = damp * live


def ring_kernel(
    codes, own, west, east, up, down, extra, ext, sources, ftab, press_ref, damp_ref, btab
):
    layers, columns = own.shape[0], own.shape[1]
    assemble(own, west, east, up, down, ext)
    eye = eye_mask()
    fast = moderate(ext)
    for layer in range(layers):
        span = slice(layer * columns, (layer + 1) * columns)
        press_ref[layer + 1, 1 : columns + 1, :] = extra[0, span, :]
        damp_ref[layer + 1, 1 : columns + 1, :] = extra[1, span, :]

    def ring(handle):
        def across(index, carry):
            handle(1, index + 1)
            handle(layers + 2, index + 1)
            return carry

        def along(index, carry):
            handle(index + 2, 1)
            handle(index + 2, columns + 2)
            return carry

        lax.fori_loop(0, columns + 2, across, 0)
        lax.fori_loop(0, layers, along, 0)

    def keep(row, col, summed):
        press, damp = state_of(summed)
        press_ref[row - 1, pl.ds(col - 1, 1), :] = press
        damp_ref[row - 1, pl.ds(col - 1, 1), :] = damp

    @pl.when(fast)
    def _():
        fill_sources(ext, btab, 0, layers + 4, 0, columns + 4)

        sources[...] = btab[1 : layers + 3, 1 : columns + 3]

        def ring_sum(row, col):
            places = near(codes, row, col, row, col)
            keep(row, col, fast_sum(left_of(ext, row, col), btab, places, eye))

        ring(ring_sum)

        def factors(row, carry):
            for col in range(1, columns + 3):
                raw = ext[row, col]
                press = jnp.broadcast_to(press_ref[row - 1, col - 1 : col, :], (8, TP))
                damp = jnp.broadcast_to(damp_ref[row - 1, col - 1 : col, :], (8, TP))
                value = jnp.concatenate([raw, press * raw, damp * raw], axis=0)
                high = value.astype(BF16).astype(F32)
                ftab[row - 1, col - 1] = jnp.concatenate([high, value - high], axis=0).astype(BF16)
            return carry

        lax.fori_loop(1, layers + 3, factors, 0)

    @pl.when(jnp.logical_not(fast))
    def _():
        def ring_sum(row, col):
            places = near(codes, row, col, row, col)
            keep(row, col, slow_sum(ext, row, col, places, eye))

        ring(ring_sum)


def accel_kernel(codes, ext, btab, ftab, press_ref, damp_ref, out, pairs, lefts):
    layers, columns = out.shape[0], out.shape[2]
    eye = eye_mask()
    fast = moderate(ext)

    def weigh(layer):
        for column in range(columns):
            lefts[column] = left_of(ext, layer + 2, column + 2)
        for column in range(columns):
            places = near(codes, layer, column, layer + 1, column + 1)
            for p, weight in enumerate(fast_weights(lefts[column], btab, places)):
                high = weight.astype(BF16)
                pairs[column, p, :, 0 : 2 * TP] = high
                pairs[column, p, :, 2 * TP : 4 * TP] = (weight - high.astype(F32)).astype(BF16)

    def gather(layer):
        for column in range(columns):
            row, col = layer + 2, column + 2
            places = near(codes, layer, column, row - 1, col - 1)
            summed = None
            for p in range(3):
                source = jnp.concatenate([ftab[places[2 * p]], ftab[places[2 * p + 1]]], axis=1)
                part = lax.dot_general(
                    jnp.concatenate([source, source], axis=1),
                    pairs[column, p],
                    NT,
                    preferred_element_type=F32,
                )
                summed = part if summed is None else summed + part
            summed = summed[0:24] + summed[24:48]
            plain, pressed, damped = summed[0:8], summed[8:16], summed[16:24]
            raw = ext[row, col]
            press = press_ref[row - 1, col - 1 : col, :]
            push = raw * (press * plain[6:7] + pressed[6:7]) - (press * plain + pressed)
            drag = damped - raw * damped[6:7]
            total = (push[0:3] + drag[3:6]) * (raw[6:7] * (1.0 / TP))
            for c in range(3):
                out[layer, c, column : column + 1, :] = total[c : c + 1]

    @pl.when(fast)
    def _():
        def step(layer, carry):
            weigh(layer)
            gather(layer)
            return carry

        lax.fori_loop(0, layers, step, 0)

    @pl.when(jnp.logical_not(fast))
    def _():
        def step(tile, carry):
            layer, column = tile // columns, tile % columns
            row, col = layer + 2, column + 2
            places = near(codes, layer, column, row, col)
            rows = slow_accel(ext, press_ref, damp_ref, row, col, places, eye)
            scale = ext[row, col, 6:7, :] * (1.0 / TP)
            for c in range(3):
                out[layer, c, pl.ds(column, 1), :] = rows[c] * scale
            return carry

        lax.fori_loop(0, layers * columns, step, 0)


def owner_lags():
    row = row_mask()
    return [(row + 8 * k) // 6 for k in range(3)]


def folded(rows):
    return (rows[0:6] + rows[6:12]) + (rows[12:18] + rows[18:24])


def share_kernel(blocks, out):
    quads = blocks.shape[0] // 24
    rows = folded(jnp.sum(blocks[...].reshape((quads, 24, TP)), axis=0))
    out[...] = jnp.concatenate([rows, jnp.zeros((2, TP), F32)], axis=0)


def marker_kernel(soil, extra, place, speed, tiles, owners, slots, out, table, lookup):
    layers, columns = soil.shape[0], soil.shape[2]
    count = layers * columns
    pairs = place.shape[1] // (2 * TP)
    quads = out.shape[0] // 24
    groups = TP // 16
    field_of = lambda f: jnp.concatenate([soil[layer, f] for layer in range(layers)], axis=0)
    spots = [field_of(c) for c in range(3)]
    moves = [field_of(3 + c) for c in range(3)]
    press, damp = extra[2], extra[3]
    scaled = [jnp.clip(spot, -CLIP, CLIP) * SCALE for spot in spots]
    norm = -0.5 * (scaled[0] * scaled[0] + scaled[1] * scaled[1] + scaled[2] * scaled[2])
    fields = scaled + [norm, press, damp]
    fields = fields + [damp * moves[c] - press * spots[c] for c in range(3)]
    for number, field in enumerate(fields):
        if number < ONEHOT:
            pieces = list(split3(field)) + [jnp.zeros((TP - 3 * count, TP), F32)]
            turned = jnp.transpose(jnp.concatenate(pieces, axis=0)).astype(BF16)
            for group in range(groups):
                at = (group * ONEHOT + number) * 16
                table[at : at + 16, :] = turned[group * 16 : group * 16 + 16]
        else:
            pieces = [field, jnp.zeros((TP - count, TP), F32)]
            lookup[number - ONEHOT] = jnp.transpose(jnp.concatenate(pieces, axis=0))
    entry = lax.broadcasted_iota(jnp.int32, (TP, TP), 0)
    listed = jnp.where(entry < 3 * count, lax.rem(entry, count), -1)
    out[...] = jnp.zeros(out.shape, F32)

    lags = owner_lags()

    def add_terms(pair, terms):
        left, right = [], []
        for part in range(2):
            block = pair * 2 + part
            value = terms[:, part * TP : (part + 1) * TP]
            high = value.astype(BF16).astype(F32)
            owner = jnp.broadcast_to(owners[pl.ds(block, 1), :], (8, TP))
            late = [owner - lag for lag in lags]
            slot = jnp.broadcast_to(slots[pl.ds(block, 1), :], (TP, TP))
            hot = jnp.where(slot == entry, 1.0, 0.0).astype(BF16)
            masks = [late[k] == 4 * quad for quad in range(quads) for k in range(3)]
            for piece in (high, value - high):
                turned = [
                    jnp.concatenate(
                        [piece[(8 * k + r) % 6 : (8 * k + r) % 6 + 1] for r in range(8)], axis=0
                    )
                    for k in range(3)
                ]
                left.append(
                    jnp.concatenate(
                        [jnp.where(mask, turned[n % 3], 0.0) for n, mask in enumerate(masks)],
                        axis=0,
                    ).astype(BF16)
                )
                right.append(hot)
        out[...] = out[...] + lax.dot_general(
            jnp.concatenate(left, axis=1),
            jnp.concatenate(right, axis=1),
            NT,
            preferred_element_type=F32,
        )

    def forces_on(pair):
        wide = 2 * TP
        lanes = pl.ds(pl.multiple_of(pair * wide, wide), wide)
        which = [
            jnp.broadcast_to(tiles[pl.ds(pair * 2 + part, 1), :], (TP, TP)) for part in range(2)
        ]
        hot = jnp.concatenate(
            [jnp.where(w == listed, 1.0, 0.0).astype(BF16) for w in which], axis=1
        )
        y = place[:, lanes]
        u = speed[:, lanes]
        spread = y * SCALE
        at = [jnp.broadcast_to(spread[c : c + 1], (16, wide)) for c in range(3)]
        totals = [jnp.zeros((16, wide), F32) for number in range(5)]
        for group in range(groups):
            span = slice(group * 16, group * 16 + 16)
            rows = slice(group * 16 * ONEHOT, (group + 1) * 16 * ONEHOT)
            got = []
            if ONEHOT:
                picked = lax.dot_general(
                    table[rows, :], hot, (((1,), (0,)), ((), ())), preferred_element_type=F32
                )
                got = [picked[16 * number : 16 * number + 16] for number in range(ONEHOT)]
            for number in range(9 - ONEHOT):
                source = lookup[number, span, :]
                got.append(
                    jnp.concatenate(
                        [jnp.take_along_axis(source, w[0:16], axis=1) for w in which], axis=1
                    )
                )
            power = (got[3] + at[0] * got[0]) + (at[1] * got[1] + at[2] * got[2])
            weight = jnp.exp2(power)
            for number in range(5):
                totals[number] = totals[number] + weight * got[4 + number]
        sums = [jnp.sum(total, axis=0, keepdims=True) for total in totals]
        square = spread * spread
        scale = jnp.exp2(-0.5 * (square[0:1] + square[1:2] + square[2:3])) * (1.0 / TP)
        where = [y[c : c + 1] for c in range(3)]
        force = [
            (where[c] * sums[0] + (sums[2 + c] - u[c : c + 1] * sums[1])) * scale
            for c in range(3)
        ]
        moment = cross(where, force)
        return jnp.concatenate(force + moment + [jnp.zeros((2, wide), F32)], axis=0)

    def step(turn, terms):
        first, second = terms
        ahead = forces_on(2 * turn)
        add_terms(jnp.maximum(2 * turn - 1, 0), second)
        behind = forces_on(2 * turn + 1)
        add_terms(2 * turn, ahead)
        return ahead, behind

    blank = jnp.zeros((8, 2 * TP), F32)
    _, terms = lax.fori_loop(0, pairs // 2, step, (blank, blank))
    add_terms(pairs - 1, terms)


def cross(a, b):
    return [
        a[1] * b[2] - a[2] * b[1],
        a[2] * b[0] - a[0] * b[2],
        a[0] * b[1] - a[1] * b[0],
    ]


def advance_kernel(first, second, third, fourth, state, inertia, out, sent):
    totals = (first[...] + second[...]) + (third[...] + fourth[...])
    row = lambda ref, r: ref[r : r + 1, :]
    force = [totals[c : c + 1] for c in range(3)]
    moments = [totals[3 + c : 4 + c] for c in range(3)]
    center = [row(state, c) for c in range(3)]
    velocity = [row(state, 3 + c) for c in range(3)]
    spin = [row(state, 6 + c) for c in range(3)]
    inv_mass = row(inertia, 0)
    moment = [row(inertia, 1 + c) for c in range(3)]
    arm = cross(center, force)
    gyro = cross(spin, [moment[c] * spin[c] for c in range(3)])
    pull = [0.0, 0.0, -gravity]
    new_vel = [velocity[c] + time_step * (inv_mass * force[c] + pull[c]) for c in range(3)]
    new_spin = [
        spin[c] + time_step * ((moments[c] - arm[c]) - gyro[c]) / moment[c] for c in range(3)
    ]
    new_center = [center[c] + time_step * new_vel[c] for c in range(3)]
    out[...] = jnp.concatenate(new_center + new_vel + new_spin, axis=0)
    swing = cross(new_spin, center)
    base = [new_vel[c] - swing[c] for c in range(3)]
    block = jnp.concatenate((base + new_spin) * 4, axis=0)
    quads = sent.shape[0] // 24
    sent[...] = jnp.broadcast_to(block[None], (quads, 24, TP)).reshape(sent.shape)


def pick_kernel(states, place, owners, slots, out):
    steps = place.shape[1] // (PICK * TP)
    quads = states.shape[0] // 24
    lags = owner_lags()

    def step(index, carry):
        for part in range(PICK):
            block = index * PICK + part
            lanes = pl.ds(pl.multiple_of(block * TP, TP), TP)
            slot = jnp.broadcast_to(slots[pl.ds(block, 1), :], (8, TP))
            owner = jnp.broadcast_to(owners[pl.ds(block, 1), :], (8, TP))
            late = [owner - lag for lag in lags]
            found = [jnp.zeros((8, TP), F32) for k in range(3)]
            for quad in range(quads):
                for k in range(3):
                    at = 24 * quad + 8 * k
                    here = jnp.take_along_axis(states[at : at + 8, :], slot, axis=1)
                    found[k] = jnp.where(late[k] == 4 * quad, here, found[k])
            picked = folded(jnp.concatenate(found, axis=0))
            y = place[:, lanes]
            turn = cross(
                [picked[3 + c : 4 + c] for c in range(3)], [y[c : c + 1] for c in range(3)]
            )
            out[:, lanes] = picked[0:3] + jnp.concatenate(turn, axis=0)
        return carry

    lax.fori_loop(0, steps, step, 0)


def shifted(shard, axis, dim, width):
    size, length = lax.axis_size(axis), shard.shape[dim]
    up = [(i, i + 1) for i in range(size - 1)]
    down = [(j, i) for i, j in up]
    last = lax.slice_in_dim(shard, length - width, length, axis=dim)
    first = lax.slice_in_dim(shard, 0, width, axis=dim)
    return lax.ppermute(last, axis, up), lax.ppermute(first, axis, down)


def local(
    soil_state,
    tile_count,
    tile_neighbors,
    marker_pos,
    marker_vel,
    marker_tile,
    marker_owner,
    marker_slot,
    body_state,
    body_inertia,
):
    layers, columns, fields, tile_size = soil_state.shape
    marker_count = marker_pos.shape[1]
    tile_devs = lax.axis_size("tile")
    depth_devs = lax.axis_size("depth")
    soil = jnp.transpose(soil_state, (0, 2, 1, 3))
    codes = jnp.transpose(tile_neighbors, (2, 0, 1))
    own = pl.pallas_call(
        prep_kernel,
        out_shape=jax.ShapeDtypeStruct((layers, columns, 8, TP), F32),
        in_specs=[pl.BlockSpec(memory_space=pltpu.HBM)] * 3,
        out_specs=vspec(),
        scratch_shapes=[
            SMEM((layers, columns), jnp.int32),
            SMEM((6, layers, columns), jnp.int32),
            VMEM((layers, fields, columns, TP), F32),
            pltpu.SemaphoreType.DMA((3,)),
        ],
        compiler_params=params(),
        name="prep",
    )(*[pltpu.with_memory_space_constraint(x, pltpu.HBM) for x in (tile_count, codes, soil)])
    lefts, inner = pl.pallas_call(
        inner_kernel,
        out_shape=(
            jax.ShapeDtypeStruct((layers, columns, TP, AUG), BF16),
            jax.ShapeDtypeStruct((layers, columns, TP), F32),
        ),
        in_specs=[sspec(), vspec()],
        out_specs=(vspec(), vspec()),
        scratch_shapes=[VMEM((layers, columns, AUG, TP), BF16)],
        cost_estimate=cost(4_000_000, 1 << 18, 1_000_000),
        compiler_params=params(),
        name="inner",
    )(codes, own)
    west, east = shifted(own, "tile", 1, 2)
    top = jnp.concatenate([west[:2], own[:2], east[:2]], axis=1)
    bottom = jnp.concatenate([west[-2:], own[-2:], east[-2:]], axis=1)
    rim = jnp.concatenate([top, bottom], axis=0)
    up, down = shifted(rim, "depth", 0, 2)
    pieces = (own, west, east, up, down)
    span, width = layers + 4, columns + 4
    pairs = layers * columns * 6 * TP * TP
    extra = pl.pallas_call(
        density_kernel,
        out_shape=jax.ShapeDtypeStruct((4, layers * columns, TP), F32),
        in_specs=[sspec()] + [vspec()] * 7,
        out_specs=vspec(),
        scratch_shapes=[
            VMEM((span, width, 8, TP), F32),
            VMEM((span, width, AUG, TP), BF16),
            VMEM((layers, columns, TP), F32),
        ],
        cost_estimate=cost(pairs * 12, 1 << 18, pairs),
        compiler_params=params(),
        name="density",
    )(codes, *pieces, lefts, inner)
    owners = marker_owner.reshape((marker_count // TP, TP))
    slots = marker_slot.reshape((marker_count // TP, TP))
    tiles = marker_tile.reshape((marker_count // TP, TP))
    partial_sums = pl.pallas_call(
        marker_kernel,
        out_shape=jax.ShapeDtypeStruct((tile_devs * 6, TP), F32),
        in_specs=[vspec()] * 7,
        out_specs=vspec(),
        scratch_shapes=[VMEM((9 * TP, TP), BF16), VMEM((9, TP, TP), F32)],
        cost_estimate=cost(marker_count * TP * 25, 1 << 19, marker_count * TP),
        compiler_params=params(),
        name="markers",
    )(soil, extra, marker_pos, marker_vel, tiles, owners, slots)
    partial_sums, extra = lax.optimization_barrier((partial_sums, extra))
    flat = (tile_devs, 1, 6 * TP)
    arrived = lax.all_to_all(partial_sums.reshape(flat), "tile", 0, 0, tiled=True)
    own, west, east, up, down = pieces
    ring_codes = jnp.concatenate(
        [
            part[:, :, 7, 0:6]
            for part in (up, jnp.concatenate([west, own, east], axis=1), down)
        ],
        axis=0,
    )
    ring_codes = jnp.transpose(ring_codes.astype(jnp.int32), (2, 0, 1))
    shapes = (
        jax.ShapeDtypeStruct((span, width, 8, TP), F32),
        jax.ShapeDtypeStruct((layers + 2, columns + 2, AUG, TP), BF16),
        jax.ShapeDtypeStruct((layers + 2, columns + 2, FACTORS, TP), BF16),
        jax.ShapeDtypeStruct((layers + 2, 16, TP), F32),
        jax.ShapeDtypeStruct((layers + 2, 16, TP), F32),
    )
    tables = pl.pallas_call(
        ring_kernel,
        out_shape=shapes,
        in_specs=[sspec()] + [vspec()] * 6,
        out_specs=(vspec(),) * 5,
        scratch_shapes=[VMEM((span, width, AUG, TP), BF16)],
        cost_estimate=cost(pairs * 15, 1 << 19, pairs),
        compiler_params=params(),
        name="ring",
    )(ring_codes, *pieces, extra)
    arrived, damp = lax.optimization_barrier((arrived, tables[4]))
    share = pl.pallas_call(
        share_kernel,
        out_shape=jax.ShapeDtypeStruct((8, TP), F32),
        in_specs=[vspec()],
        out_specs=vspec(),
        compiler_params=params(),
        name="share",
    )(arrived.reshape((tile_devs * 6, TP)))

    others = [
        lax.ppermute(share, "depth", [(i, (i + k) % depth_devs) for i in range(depth_devs)])
        for k in range(1, depth_devs)
    ]
    body_next, sent = pl.pallas_call(
        advance_kernel,
        out_shape=(
            jax.ShapeDtypeStruct((9, TP), F32),
            jax.ShapeDtypeStruct((tile_devs * 6, TP), F32),
        ),
        in_specs=[vspec()] * 6,
        out_specs=(vspec(), vspec()),
        compiler_params=params(),
        name="advance",
    )(share, *others, body_state, body_inertia)
    sent, damp = lax.optimization_barrier((sent, damp))
    states = lax.all_to_all(sent.reshape(flat), "tile", 0, 0, tiled=True)
    accel = pl.pallas_call(
        accel_kernel,
        out_shape=jax.ShapeDtypeStruct((layers, 3, columns, TP), F32),
        in_specs=[sspec()] + [vspec()] * 5,
        out_specs=vspec(),
        scratch_shapes=[VMEM((columns, 3, TP, 4 * TP), BF16), VMEM((columns, TP, AUG), BF16)],
        cost_estimate=cost(pairs * 15, 1 << 19, pairs),
        compiler_params=params(),
        name="accel",
    )(codes, *tables[:4], damp)
    states, accel = lax.optimization_barrier((states, accel))
    soil_accel = jnp.transpose(accel, (0, 2, 1, 3))
    marker_vel_next = pl.pallas_call(
        pick_kernel,
        out_shape=jax.ShapeDtypeStruct((3, marker_count), F32),
        in_specs=[vspec()] * 4,
        out_specs=vspec(),
        compiler_params=params(),
        name="pick",
    )(states.reshape((tile_devs * 6, TP)), marker_pos, owners, slots)
    return (soil_accel, body_next, marker_vel_next)


def solution(mesh):
    placed = (
        P("depth", "tile", None, None),
        P("depth", "tile"),
        P("depth", "tile", None),
        P(None, ("tile", "depth")),
        P(None, ("tile", "depth")),
        P(("tile", "depth")),
        P(("tile", "depth"), None),
        P(("tile", "depth")),
        P(None, "tile"),
        P(None, "tile"),
    )
    return jax.shard_map(
        local,
        mesh=mesh,
        in_specs=placed,
        out_specs=(P("depth", "tile", None, None), P(None, "tile"), P(None, ("tile", "depth"))),
        check_vma=False,
    )
```

```python
import functools

import jax
import jax.numpy as jnp
from jax import lax
from jax.experimental import pallas as pl
from jax.experimental.pallas import tpu as pltpu
from jax.sharding import PartitionSpec as P

stiffness = 40.0
rest_density = 2.0
viscosity = 20.0
time_step = 0.05
gravity = 1.0
VMEM = pltpu.VMEM
SMEM = pltpu.SMEM
TP = 128
ROWS = 16
AUG = 48
FACTORS = 48
TILES = 10
ONEHOT = 9
PICK = 8
SCALE = (2.0 * 1.4426950408889634) ** 0.5
FAR = 1e30
PLACE_LIMIT = 4.0
CLIP = 1e4
SPEED_LIMIT = 8.0
F32 = jnp.float32
BF16 = jnp.bfloat16
NT = (((1,), (1,)), ((), ()))


def vspec():
    return pl.BlockSpec(memory_space=VMEM)


def sspec():
    return pl.BlockSpec(memory_space=SMEM)


def params(limit=16 << 20):
    return pltpu.CompilerParams(vmem_limit_bytes=limit)


def cost(flops, moved, heavy=0):
    return pl.CostEstimate(flops=flops, bytes_accessed=moved, transcendentals=heavy)


def row_mask():
    return lax.broadcasted_iota(jnp.int32, (8, TP), 0)


def eye_mask():
    return lax.broadcasted_iota(jnp.int32, (TP, TP), 0) == lax.broadcasted_iota(
        jnp.int32, (TP, TP), 1
    )


def split3(value):
    high = value.astype(BF16).astype(F32)
    rest = value - high
    middle = rest.astype(BF16).astype(F32)
    return high, middle, rest - middle


def augmented(raw, source):
    row = row_mask()
    scaled = raw * SCALE
    square = scaled * scaled
    norm = -0.5 * (square[0:1] + square[1:2] + square[2:3])
    if source:
        third, fourth = norm + (raw[6:7] - 1.0) * FAR, jnp.ones((1, TP), F32)
    else:
        third, fourth = jnp.ones((1, TP), F32), norm
    full = jnp.where(
        row < 3, scaled, jnp.where(row == 3, third, jnp.where(row == 4, fourth, 0.0))
    )
    h, m, l = split3(full)
    return jnp.concatenate([h, m, h, m, l, h] if source else [h, h, m, m, h, l], axis=0)


def assemble(own, west, east, up, down, ext):
    layers, columns = own.shape[0], own.shape[1]
    ext[0:2] = up[...]
    ext[layers + 2 : layers + 4] = down[...]
    ext[2 : layers + 2, 0:2] = west[...]
    ext[2 : layers + 2, columns + 2 : columns + 4] = east[...]
    ext[2 : layers + 2, 2 : columns + 2] = own[...]


def moderate(ext):
    span, width = ext.shape[0], ext.shape[1]
    flat = ext[...].reshape((span * width, 8, TP))
    peak = jnp.max(jnp.abs(flat), axis=0)
    row = row_mask()
    ratio = jnp.where(
        row < 3, peak / PLACE_LIMIT, jnp.where(row < 6, peak / SPEED_LIMIT, 0.0)
    )
    return jnp.max(ratio) <= 1.0


def near(codes, layer, column, row, col):
    places = []
    for k in range(6):
        code = codes[k, layer, column]
        down = (code * 11) >> 5
        places.append((row + down - 1, col + code - 3 * down - 1))
    return places


def to_row(total, eye):
    sums = jnp.sum(total, axis=1, keepdims=True)
    return jnp.sum(jnp.where(eye, sums, 0.0), axis=0, keepdims=True)


def fast_weights(left, btab, places):
    weights = []
    for p in range(3):
        right = jnp.concatenate([btab[places[2 * p]], btab[places[2 * p + 1]]], axis=1)
        weights.append(
            jnp.exp2(lax.dot_general(left, right, (((1,), (0,)), ((), ())), preferred_element_type=F32))
        )
    return weights


def fast_sum(left, btab, places, eye):
    total = None
    for weight in fast_weights(left, btab, places):
        part = weight[:, 0:TP] + weight[:, TP : 2 * TP]
        total = part if total is None else total + part
    return to_row(total, eye)


def rows_of(ref, place, row, count):
    return jnp.broadcast_to(ref[place[0], place[1], row : row + 1, :], (count, TP))


def slow_sum(ext, row, col, places, eye):
    cols = jnp.transpose(ext[row, col])
    sums = []
    for block in range(TP // ROWS):
        here = cols[block * ROWS : (block + 1) * ROWS]
        spot = [jnp.broadcast_to(here[:, c : c + 1], (ROWS, TP)) for c in range(3)]
        total = jnp.zeros((ROWS, TP), F32)
        for place in places:
            distance = None
            for c in range(3):
                offset = spot[c] - rows_of(ext, place, c, ROWS)
                square = offset * offset
                distance = square if distance is None else distance + square
            total = total + rows_of(ext, place, 6, ROWS) * jnp.exp(-distance)
        sums.append(jnp.sum(total, axis=1, keepdims=True))
    return jnp.sum(jnp.where(eye, jnp.concatenate(sums, axis=0), 0.0), axis=0, keepdims=True)


def slow_accel(ext, press_ref, damp_ref, row, col, places, eye):
    cols = jnp.transpose(ext[row, col])
    more = jnp.transpose(
        jnp.broadcast_to(press_ref[row - 1, pl.ds(col - 1, 1), :], (8, TP))
    )
    sums = [[], [], []]
    for block in range(TP // ROWS):
        span = slice(block * ROWS, (block + 1) * ROWS)
        here = cols[span]
        spot = [jnp.broadcast_to(here[:, c : c + 1], (ROWS, TP)) for c in range(3)]
        speed = [jnp.broadcast_to(here[:, 3 + c : 4 + c], (ROWS, TP)) for c in range(3)]
        press_here = jnp.broadcast_to(more[span, 0:1], (ROWS, TP))
        total = [jnp.zeros((ROWS, TP), F32) for c in range(3)]
        for place in places:
            offsets = [spot[c] - rows_of(ext, place, c, ROWS) for c in range(3)]
            distance = offsets[0] * offsets[0] + offsets[1] * offsets[1]
            distance = distance + offsets[2] * offsets[2]
            weight = rows_of(ext, place, 6, ROWS) * jnp.exp(-distance)
            there = (place[0] - 1, pl.ds(place[1] - 1, 1), slice(None))
            press = weight * (press_here + jnp.broadcast_to(press_ref[there], (ROWS, TP)))
            damp = weight * jnp.broadcast_to(damp_ref[there], (ROWS, TP))
            for c in range(3):
                relative = rows_of(ext, place, 3 + c, ROWS) - speed[c]
                total[c] = total[c] + (press * offsets[c] + damp * relative)
        for c in range(3):
            sums[c].append(jnp.sum(total[c], axis=1, keepdims=True))
    return [
        jnp.sum(jnp.where(eye, jnp.concatenate(part, axis=0), 0.0), axis=0, keepdims=True)
        for part in sums
    ]


def state_of(summed):
    density = 1.0 + summed * (1.0 / TP)
    press = (2.0 * stiffness) * (density - rest_density) / (density * density)
    return press, viscosity / density


def fill_sources(ext, btab, first, last, left, right):
    def step(row, carry):
        for col in range(left, right):
            btab[row, col] = augmented(ext[row, col], True).astype(BF16)
        return carry

    lax.fori_loop(first, last, step, 0)


def left_of(ext, row, col):
    return jnp.transpose(augmented(ext[row, col], False)).astype(BF16)


def prep_kernel(counts_in, codes_in, soil_in, out, counts, codes, soil, sems):
    copies = [
        pltpu.make_async_copy(counts_in, counts, sems.at[0]),
        pltpu.make_async_copy(codes_in, codes, sems.at[1]),
        pltpu.make_async_copy(soil_in, soil, sems.at[2]),
    ]
    for copy in copies:
        copy.start()
    for copy in copies:
        copy.wait()
    layers, columns = out.shape[0], out.shape[1]
    lane = lax.broadcasted_iota(jnp.int32, (1, TP), 1)
    for layer in range(layers):
        for column in range(columns):
            listed = jnp.zeros((1, TP), jnp.int32)
            for k in range(6):
                listed = jnp.where(lane == k, codes[k, layer, column], listed)
            live = jnp.where(lane < counts[layer, column], 1.0, 0.0)
            rows = [soil[layer, c, column : column + 1, :] for c in range(6)]
            out[layer, column] = jnp.concatenate(rows + [live, listed.astype(F32)], axis=0)


def rim_tile(index, layers, columns):
    side = index - 2 * columns
    on_side, last = side >= 0, index >= columns
    layer = jnp.where(on_side, 1 + (side >> 1), jnp.where(last, layers - 1, 0))
    column = jnp.where(
        on_side, (columns - 1) * (side & 1), jnp.where(last, index - columns, index)
    )
    return layer, column


def turn_kernel(own, lefts, btab):
    layers, columns = own.shape[0], own.shape[1]
    fill_sources(own, btab, 0, layers, 0, columns)

    def turn(layer, carry):
        for column in range(columns):
            lefts[layer, column] = left_of(own, layer, column)
        return carry

    lax.fori_loop(0, layers, turn, 0)


def inner_kernel(codes, lefts, btab, sums):
    layers, columns = lefts.shape[0], lefts.shape[1]
    eye = eye_mask()

    def step(layer, carry):
        for column in range(1, columns - 1):
            places = near(codes, layer, column, layer, column)
            row = fast_sum(lefts[layer, column], btab, places, eye)
            sums[layer, column : column + 1, :] = row
        return carry

    lax.fori_loop(1, layers - 1, step, 0)


def density_kernel(
    codes, own, west, east, up, down, lefts, mine, inner, out, ext, btab, sums
):
    layers, columns = own.shape[0], own.shape[1]
    assemble(own, west, east, up, down, ext)
    eye = eye_mask()
    fast = moderate(ext)
    sums[...] = inner[...]

    @pl.when(fast)
    def _():
        btab[2 : layers + 2, 2 : columns + 2] = mine[...]
        for row in range(1, layers + 3):
            edge = row in (1, layers + 2)
            for col in range(1, columns + 3) if edge else (1, columns + 2):
                btab[row, col] = augmented(ext[row, col], True).astype(BF16)
        rim = 2 * columns + 2 * (layers - 2)

        def step(group, carry):
            for part in range(TILES):
                index = group * TILES + part
                layer, column = rim_tile(index, layers, columns)
                places = near(codes, layer, column, layer + 2, column + 2)
                row = fast_sum(lefts[layer, column], btab, places, eye)
                sums[layer, pl.ds(column, 1), :] = row
            return carry

        lax.fori_loop(0, rim // TILES, step, 0)

    @pl.when(jnp.logical_not(fast))
    def _():
        def step(tile, carry):
            layer, column = tile // columns, tile % columns
            places = near(codes, layer, column, layer + 2, column + 2)
            row = slow_sum(ext, layer + 2, column + 2, places, eye)
            sums[layer, pl.ds(column, 1), :] = row
            return carry

        lax.fori_loop(0, layers * columns, step, 0)

    for layer in range(layers):
        span = slice(layer * columns, (layer + 1) * columns)
        press, damp = state_of(sums[layer])
        live = jnp.concatenate([own[layer, c, 6:7, :] for c in range(columns)], axis=0)
        out[0, span, :] = press
        out[1, span, :] = damp
        out[2, span, :] = press * live
        out[3, span, :] = damp * live


def ring_kernel(
    codes, own, west, east, up, down, extra, ext, sources, ftab, press_ref, damp_ref, btab
):
    layers, columns = own.shape[0], own.shape[1]
    assemble(own, west, east, up, down, ext)
    eye = eye_mask()
    fast = moderate(ext)
    for layer in range(layers):
        span = slice(layer * columns, (layer + 1) * columns)
        press_ref[layer + 1, 1 : columns + 1, :] = extra[0, span, :]
        damp_ref[layer + 1, 1 : columns + 1, :] = extra[1, span, :]

    def ring(handle):
        def across(index, carry):
            handle(1, index + 1)
            handle(layers + 2, index + 1)
            return carry

        def along(index, carry):
            handle(index + 2, 1)
            handle(index + 2, columns + 2)
            return carry

        lax.fori_loop(0, columns + 2, across, 0)
        lax.fori_loop(0, layers, along, 0)

    def keep(row, col, summed):
        press, damp = state_of(summed)
        press_ref[row - 1, pl.ds(col - 1, 1), :] = press
        damp_ref[row - 1, pl.ds(col - 1, 1), :] = damp

    @pl.when(fast)
    def _():
        fill_sources(ext, btab, 0, layers + 4, 0, columns + 4)

        sources[...] = btab[1 : layers + 3, 1 : columns + 3]

        def ring_sum(row, col):
            places = near(codes, row, col, row, col)
            keep(row, col, fast_sum(left_of(ext, row, col), btab, places, eye))

        ring(ring_sum)

        def factors(row, carry):
            for col in range(1, columns + 3):
                raw = ext[row, col]
                press = jnp.broadcast_to(press_ref[row - 1, col - 1 : col, :], (8, TP))
                damp = jnp.broadcast_to(damp_ref[row - 1, col - 1 : col, :], (8, TP))
                value = jnp.concatenate([raw, press * raw, damp * raw], axis=0)
                high = value.astype(BF16).astype(F32)
                ftab[row - 1, col - 1] = jnp.concatenate([high, value - high], axis=0).astype(BF16)
            return carry

        lax.fori_loop(1, layers + 3, factors, 0)

    @pl.when(jnp.logical_not(fast))
    def _():
        def ring_sum(row, col):
            places = near(codes, row, col, row, col)
            keep(row, col, slow_sum(ext, row, col, places, eye))

        ring(ring_sum)


def accel_kernel(codes, ext, btab, ftab, press_ref, damp_ref, out, pairs, lefts):
    layers, columns = out.shape[0], out.shape[2]
    eye = eye_mask()
    fast = moderate(ext)

    def weigh(layer):
        for column in range(columns):
            lefts[column] = left_of(ext, layer + 2, column + 2)
        for column in range(columns):
            places = near(codes, layer, column, layer + 1, column + 1)
            for p, weight in enumerate(fast_weights(lefts[column], btab, places)):
                high = weight.astype(BF16)
                pairs[column, p, :, 0 : 2 * TP] = high
                pairs[column, p, :, 2 * TP : 4 * TP] = (weight - high.astype(F32)).astype(BF16)

    def gather(layer):
        for column in range(columns):
            row, col = layer + 2, column + 2
            places = near(codes, layer, column, row - 1, col - 1)
            summed = None
            for p in range(3):
                source = jnp.concatenate([ftab[places[2 * p]], ftab[places[2 * p + 1]]], axis=1)
                part = lax.dot_general(
                    jnp.concatenate([source, source], axis=1),
                    pairs[column, p],
                    NT,
                    preferred_element_type=F32,
                )
                summed = part if summed is None else summed + part
            summed = summed[0:24] + summed[24:48]
            plain, pressed, damped = summed[0:8], summed[8:16], summed[16:24]
            raw = ext[row, col]
            press = press_ref[row - 1, col - 1 : col, :]
            push = raw * (press * plain[6:7] + pressed[6:7]) - (press * plain + pressed)
            drag = damped - raw * damped[6:7]
            total = (push[0:3] + drag[3:6]) * (raw[6:7] * (1.0 / TP))
            for c in range(3):
                out[layer, c, column : column + 1, :] = total[c : c + 1]

    @pl.when(fast)
    def _():
        def step(layer, carry):
            weigh(layer)
            gather(layer)
            return carry

        lax.fori_loop(0, layers, step, 0)

    @pl.when(jnp.logical_not(fast))
    def _():
        def step(tile, carry):
            layer, column = tile // columns, tile % columns
            row, col = layer + 2, column + 2
            places = near(codes, layer, column, row, col)
            rows = slow_accel(ext, press_ref, damp_ref, row, col, places, eye)
            scale = ext[row, col, 6:7, :] * (1.0 / TP)
            for c in range(3):
                out[layer, c, pl.ds(column, 1), :] = rows[c] * scale
            return carry

        lax.fori_loop(0, layers * columns, step, 0)


def owner_lags():
    row = row_mask()
    return [(row + 8 * k) // 6 for k in range(3)]


def folded(rows):
    return (rows[0:6] + rows[6:12]) + (rows[12:18] + rows[18:24])


def share_kernel(blocks, out):
    quads = blocks.shape[0] // 24
    rows = folded(jnp.sum(blocks[...].reshape((quads, 24, TP)), axis=0))
    out[...] = jnp.concatenate([rows, jnp.zeros((2, TP), F32)], axis=0)


def marker_kernel(soil, extra, place, speed, tiles, owners, slots, out, table, lookup):
    layers, columns = soil.shape[0], soil.shape[2]
    count = layers * columns
    pairs = place.shape[1] // (2 * TP)
    quads = out.shape[0] // 24
    groups = TP // 16
    field_of = lambda f: jnp.concatenate([soil[layer, f] for layer in range(layers)], axis=0)
    spots = [field_of(c) for c in range(3)]
    moves = [field_of(3 + c) for c in range(3)]
    press, damp = extra[2], extra[3]
    scaled = [jnp.clip(spot, -CLIP, CLIP) * SCALE for spot in spots]
    norm = -0.5 * (scaled[0] * scaled[0] + scaled[1] * scaled[1] + scaled[2] * scaled[2])
    fields = scaled + [norm, press, damp]
    fields = fields + [damp * moves[c] - press * spots[c] for c in range(3)]
    for number, field in enumerate(fields):
        if number < ONEHOT:
            pieces = list(split3(field)) + [jnp.zeros((TP - 3 * count, TP), F32)]
            turned = jnp.transpose(jnp.concatenate(pieces, axis=0)).astype(BF16)
            for group in range(groups):
                at = (group * ONEHOT + number) * 16
                table[at : at + 16, :] = turned[group * 16 : group * 16 + 16]
        else:
            pieces = [field, jnp.zeros((TP - count, TP), F32)]
            lookup[number - ONEHOT] = jnp.transpose(jnp.concatenate(pieces, axis=0))
    entry = lax.broadcasted_iota(jnp.int32, (TP, TP), 0)
    listed = jnp.where(entry < 3 * count, lax.rem(entry, count), -1)
    out[...] = jnp.zeros(out.shape, F32)

    lags = owner_lags()

    def add_terms(pair, terms):
        left, right = [], []
        for part in range(2):
            block = pair * 2 + part
            value = terms[:, part * TP : (part + 1) * TP]
            high = value.astype(BF16).astype(F32)
            owner = jnp.broadcast_to(owners[pl.ds(block, 1), :], (8, TP))
            late = [owner - lag for lag in lags]
            slot = jnp.broadcast_to(slots[pl.ds(block, 1), :], (TP, TP))
            hot = jnp.where(slot == entry, 1.0, 0.0).astype(BF16)
            masks = [late[k] == 4 * quad for quad in range(quads) for k in range(3)]
            for piece in (high, value - high):
                turned = [
                    jnp.concatenate(
                        [piece[(8 * k + r) % 6 : (8 * k + r) % 6 + 1] for r in range(8)], axis=0
                    )
                    for k in range(3)
                ]
                left.append(
                    jnp.concatenate(
                        [jnp.where(mask, turned[n % 3], 0.0) for n, mask in enumerate(masks)],
                        axis=0,
                    ).astype(BF16)
                )
                right.append(hot)
        out[...] = out[...] + lax.dot_general(
            jnp.concatenate(left, axis=1),
            jnp.concatenate(right, axis=1),
            NT,
            preferred_element_type=F32,
        )

    def forces_on(pair):
        wide = 2 * TP
        lanes = pl.ds(pl.multiple_of(pair * wide, wide), wide)
        which = [
            jnp.broadcast_to(tiles[pl.ds(pair * 2 + part, 1), :], (TP, TP)) for part in range(2)
        ]
        hot = jnp.concatenate(
            [jnp.where(w == listed, 1.0, 0.0).astype(BF16) for w in which], axis=1
        )
        y = place[:, lanes]
        u = speed[:, lanes]
        spread = y * SCALE
        at = [jnp.broadcast_to(spread[c : c + 1], (16, wide)) for c in range(3)]
        totals = [jnp.zeros((16, wide), F32) for number in range(5)]
        for group in range(groups):
            span = slice(group * 16, group * 16 + 16)
            rows = slice(group * 16 * ONEHOT, (group + 1) * 16 * ONEHOT)
            got = []
            if ONEHOT:
                picked = lax.dot_general(
                    table[rows, :], hot, (((1,), (0,)), ((), ())), preferred_element_type=F32
                )
                got = [picked[16 * number : 16 * number + 16] for number in range(ONEHOT)]
            for number in range(9 - ONEHOT):
                source = lookup[number, span, :]
                got.append(
                    jnp.concatenate(
                        [jnp.take_along_axis(source, w[0:16], axis=1) for w in which], axis=1
                    )
                )
            power = (got[3] + at[0] * got[0]) + (at[1] * got[1] + at[2] * got[2])
            weight = jnp.exp2(power)
            for number in range(5):
                totals[number] = totals[number] + weight * got[4 + number]
        sums = [jnp.sum(total, axis=0, keepdims=True) for total in totals]
        square = spread * spread
        scale = jnp.exp2(-0.5 * (square[0:1] + square[1:2] + square[2:3])) * (1.0 / TP)
        where = [y[c : c + 1] for c in range(3)]
        force = [
            (where[c] * sums[0] + (sums[2 + c] - u[c : c + 1] * sums[1])) * scale
            for c in range(3)
        ]
        moment = cross(where, force)
        return jnp.concatenate(force + moment + [jnp.zeros((2, wide), F32)], axis=0)

    def step(turn, terms):
        first, second = terms
        ahead = forces_on(2 * turn)
        add_terms(jnp.maximum(2 * turn - 1, 0), second)
        behind = forces_on(2 * turn + 1)
        add_terms(2 * turn, ahead)
        return ahead, behind

    blank = jnp.zeros((8, 2 * TP), F32)
    _, terms = lax.fori_loop(0, pairs // 2, step, (blank, blank))
    add_terms(pairs - 1, terms)


def cross(a, b):
    return [
        a[1] * b[2] - a[2] * b[1],
        a[2] * b[0] - a[0] * b[2],
        a[0] * b[1] - a[1] * b[0],
    ]


def advance_kernel(first, second, third, fourth, state, inertia, out, sent):
    totals = (first[...] + second[...]) + (third[...] + fourth[...])
    row = lambda ref, r: ref[r : r + 1, :]
    force = [totals[c : c + 1] for c in range(3)]
    moments = [totals[3 + c : 4 + c] for c in range(3)]
    center = [row(state, c) for c in range(3)]
    velocity = [row(state, 3 + c) for c in range(3)]
    spin = [row(state, 6 + c) for c in range(3)]
    inv_mass = row(inertia, 0)
    moment = [row(inertia, 1 + c) for c in range(3)]
    arm = cross(center, force)
    gyro = cross(spin, [moment[c] * spin[c] for c in range(3)])
    pull = [0.0, 0.0, -gravity]
    new_vel = [velocity[c] + time_step * (inv_mass * force[c] + pull[c]) for c in range(3)]
    new_spin = [
        spin[c] + time_step * ((moments[c] - arm[c]) - gyro[c]) / moment[c] for c in range(3)
    ]
    new_center = [center[c] + time_step * new_vel[c] for c in range(3)]
    out[...] = jnp.concatenate(new_center + new_vel + new_spin, axis=0)
    swing = cross(new_spin, center)
    base = [new_vel[c] - swing[c] for c in range(3)]
    block = jnp.concatenate((base + new_spin) * 4, axis=0)
    quads = sent.shape[0] // 24
    sent[...] = jnp.broadcast_to(block[None], (quads, 24, TP)).reshape(sent.shape)


def pick_kernel(states, place, owners, slots, out):
    steps = place.shape[1] // (PICK * TP)
    quads = states.shape[0] // 24
    lags = owner_lags()

    def step(index, carry):
        for part in range(PICK):
            block = index * PICK + part
            lanes = pl.ds(pl.multiple_of(block * TP, TP), TP)
            slot = jnp.broadcast_to(slots[pl.ds(block, 1), :], (8, TP))
            owner = jnp.broadcast_to(owners[pl.ds(block, 1), :], (8, TP))
            late = [owner - lag for lag in lags]
            found = [jnp.zeros((8, TP), F32) for k in range(3)]
            for quad in range(quads):
                for k in range(3):
                    at = 24 * quad + 8 * k
                    here = jnp.take_along_axis(states[at : at + 8, :], slot, axis=1)
                    found[k] = jnp.where(late[k] == 4 * quad, here, found[k])
            picked = folded(jnp.concatenate(found, axis=0))
            y = place[:, lanes]
            turn = cross(
                [picked[3 + c : 4 + c] for c in range(3)], [y[c : c + 1] for c in range(3)]
            )
            out[:, lanes] = picked[0:3] + jnp.concatenate(turn, axis=0)
        return carry

    lax.fori_loop(0, steps, step, 0)


def shifted(shard, axis, dim, width):
    size, length = lax.axis_size(axis), shard.shape[dim]
    up = [(i, i + 1) for i in range(size - 1)]
    down = [(j, i) for i, j in up]
    last = lax.slice_in_dim(shard, length - width, length, axis=dim)
    first = lax.slice_in_dim(shard, 0, width, axis=dim)
    return lax.ppermute(last, axis, up), lax.ppermute(first, axis, down)


def local(
    soil_state,
    tile_count,
    tile_neighbors,
    marker_pos,
    marker_vel,
    marker_tile,
    marker_owner,
    marker_slot,
    body_state,
    body_inertia,
):
    layers, columns, fields, tile_size = soil_state.shape
    marker_count = marker_pos.shape[1]
    tile_devs = lax.axis_size("tile")
    depth_devs = lax.axis_size("depth")
    soil = jnp.transpose(soil_state, (0, 2, 1, 3))
    codes = jnp.transpose(tile_neighbors, (2, 0, 1))
    own = pl.pallas_call(
        prep_kernel,
        out_shape=jax.ShapeDtypeStruct((layers, columns, 8, TP), F32),
        in_specs=[pl.BlockSpec(memory_space=pltpu.HBM)] * 3,
        out_specs=vspec(),
        scratch_shapes=[
            SMEM((layers, columns), jnp.int32),
            SMEM((6, layers, columns), jnp.int32),
            VMEM((layers, fields, columns, TP), F32),
            pltpu.SemaphoreType.DMA((3,)),
        ],
        compiler_params=params(),
        name="prep",
    )(*[pltpu.with_memory_space_constraint(x, pltpu.HBM) for x in (tile_count, codes, soil)])
    west, east = shifted(own, "tile", 1, 2)
    lefts, mine = pl.pallas_call(
        turn_kernel,
        out_shape=(
            jax.ShapeDtypeStruct((layers, columns, TP, AUG), BF16),
            jax.ShapeDtypeStruct((layers, columns, AUG, TP), BF16),
        ),
        in_specs=[vspec()],
        out_specs=(vspec(), vspec()),
        cost_estimate=cost(1_000_000, 1 << 18),
        compiler_params=params(),
        name="turn",
    )(own)
    west, east, mine = lax.optimization_barrier((west, east, mine))
    inner = pl.pallas_call(
        inner_kernel,
        out_shape=jax.ShapeDtypeStruct((layers, columns, TP), F32),
        in_specs=[sspec(), vspec(), vspec()],
        out_specs=vspec(),
        cost_estimate=cost(4_000_000, 1 << 18, 1_000_000),
        compiler_params=params(),
        name="inner",
    )(codes, lefts, mine)
    top = jnp.concatenate([west[:2], own[:2], east[:2]], axis=1)
    bottom = jnp.concatenate([west[-2:], own[-2:], east[-2:]], axis=1)
    rim = jnp.concatenate([top, bottom], axis=0)
    up, down = shifted(rim, "depth", 0, 2)
    pieces = (own, west, east, up, down)
    span, width = layers + 4, columns + 4
    pairs = layers * columns * 6 * TP * TP
    extra = pl.pallas_call(
        density_kernel,
        out_shape=jax.ShapeDtypeStruct((4, layers * columns, TP), F32),
        in_specs=[sspec()] + [vspec()] * 8,
        out_specs=vspec(),
        scratch_shapes=[
            VMEM((span, width, 8, TP), F32),
            VMEM((span, width, AUG, TP), BF16),
            VMEM((layers, columns, TP), F32),
        ],
        cost_estimate=cost(pairs * 12, 1 << 18, pairs),
        compiler_params=params(),
        name="density",
    )(codes, *pieces, lefts, mine, inner)
    owners = marker_owner.reshape((marker_count // TP, TP))
    slots = marker_slot.reshape((marker_count // TP, TP))
    tiles = marker_tile.reshape((marker_count // TP, TP))
    partial_sums = pl.pallas_call(
        marker_kernel,
        out_shape=jax.ShapeDtypeStruct((tile_devs * 6, TP), F32),
        in_specs=[vspec()] * 7,
        out_specs=vspec(),
        scratch_shapes=[VMEM((9 * TP, TP), BF16), VMEM((9, TP, TP), F32)],
        cost_estimate=cost(marker_count * TP * 25, 1 << 19, marker_count * TP),
        compiler_params=params(),
        name="markers",
    )(soil, extra, marker_pos, marker_vel, tiles, owners, slots)
    partial_sums, extra = lax.optimization_barrier((partial_sums, extra))
    flat = (tile_devs, 1, 6 * TP)
    arrived = lax.all_to_all(partial_sums.reshape(flat), "tile", 0, 0, tiled=True)
    own, west, east, up, down = pieces
    ring_codes = jnp.concatenate(
        [
            part[:, :, 7, 0:6]
            for part in (up, jnp.concatenate([west, own, east], axis=1), down)
        ],
        axis=0,
    )
    ring_codes = jnp.transpose(ring_codes.astype(jnp.int32), (2, 0, 1))
    shapes = (
        jax.ShapeDtypeStruct((span, width, 8, TP), F32),
        jax.ShapeDtypeStruct((layers + 2, columns + 2, AUG, TP), BF16),
        jax.ShapeDtypeStruct((layers + 2, columns + 2, FACTORS, TP), BF16),
        jax.ShapeDtypeStruct((layers + 2, 16, TP), F32),
        jax.ShapeDtypeStruct((layers + 2, 16, TP), F32),
    )
    tables = pl.pallas_call(
        ring_kernel,
        out_shape=shapes,
        in_specs=[sspec()] + [vspec()] * 6,
        out_specs=(vspec(),) * 5,
        scratch_shapes=[VMEM((span, width, AUG, TP), BF16)],
        cost_estimate=cost(pairs * 15, 1 << 19, pairs),
        compiler_params=params(),
        name="ring",
    )(ring_codes, *pieces, extra)
    arrived, damp = lax.optimization_barrier((arrived, tables[4]))
    share = pl.pallas_call(
        share_kernel,
        out_shape=jax.ShapeDtypeStruct((8, TP), F32),
        in_specs=[vspec()],
        out_specs=vspec(),
        compiler_params=params(),
        name="share",
    )(arrived.reshape((tile_devs * 6, TP)))

    others = [
        lax.ppermute(share, "depth", [(i, (i + k) % depth_devs) for i in range(depth_devs)])
        for k in range(1, depth_devs)
    ]
    body_next, sent = pl.pallas_call(
        advance_kernel,
        out_shape=(
            jax.ShapeDtypeStruct((9, TP), F32),
            jax.ShapeDtypeStruct((tile_devs * 6, TP), F32),
        ),
        in_specs=[vspec()] * 6,
        out_specs=(vspec(), vspec()),
        compiler_params=params(),
        name="advance",
    )(share, *others, body_state, body_inertia)
    sent, damp = lax.optimization_barrier((sent, damp))
    states = lax.all_to_all(sent.reshape(flat), "tile", 0, 0, tiled=True)
    accel = pl.pallas_call(
        accel_kernel,
        out_shape=jax.ShapeDtypeStruct((layers, 3, columns, TP), F32),
        in_specs=[sspec()] + [vspec()] * 5,
        out_specs=vspec(),
        scratch_shapes=[VMEM((columns, 3, TP, 4 * TP), BF16), VMEM((columns, TP, AUG), BF16)],
        cost_estimate=cost(pairs * 15, 1 << 19, pairs),
        compiler_params=params(),
        name="accel",
    )(codes, *tables[:4], damp)
    states, accel = lax.optimization_barrier((states, accel))
    soil_accel = jnp.transpose(accel, (0, 2, 1, 3))
    marker_vel_next = pl.pallas_call(
        pick_kernel,
        out_shape=jax.ShapeDtypeStruct((3, marker_count), F32),
        in_specs=[vspec()] * 4,
        out_specs=vspec(),
        compiler_params=params(),
        name="pick",
    )(states.reshape((tile_devs * 6, TP)), marker_pos, owners, slots)
    return (soil_accel, body_next, marker_vel_next)


def solution(mesh):
    placed = (
        P("depth", "tile", None, None),
        P("depth", "tile"),
        P("depth", "tile", None),
        P(None, ("tile", "depth")),
        P(None, ("tile", "depth")),
        P(("tile", "depth")),
        P(("tile", "depth"), None),
        P(("tile", "depth")),
        P(None, "tile"),
        P(None, "tile"),
    )
    return jax.shard_map(
        local,
        mesh=mesh,
        in_specs=placed,
        out_specs=(P("depth", "tile", None, None), P(None, "tile"), P(None, ("tile", "depth"))),
        check_vma=False,
    )
```

```python
import functools

import jax
import jax.numpy as jnp
from jax import lax
from jax.experimental import pallas as pl
from jax.experimental.pallas import tpu as pltpu
from jax.sharding import PartitionSpec as P

stiffness = 40.0
rest_density = 2.0
viscosity = 20.0
time_step = 0.05
gravity = 1.0
VMEM = pltpu.VMEM
SMEM = pltpu.SMEM
TP = 128
ROWS = 16
AUG = 48
FACTORS = 48
TILES = 10
ONEHOT = 9
PICK = 8
SCALE = (2.0 * 1.4426950408889634) ** 0.5
FAR = 1e30
PLACE_LIMIT = 4.0
CLIP = 1e4
SPEED_LIMIT = 8.0
F32 = jnp.float32
BF16 = jnp.bfloat16
NT = (((1,), (1,)), ((), ()))


def vspec():
    return pl.BlockSpec(memory_space=VMEM)


def sspec():
    return pl.BlockSpec(memory_space=SMEM)


def params(limit=16 << 20):
    return pltpu.CompilerParams(vmem_limit_bytes=limit)


def cost(flops, moved, heavy=0):
    return pl.CostEstimate(flops=flops, bytes_accessed=moved, transcendentals=heavy)


def row_mask():
    return lax.broadcasted_iota(jnp.int32, (8, TP), 0)


def eye_mask():
    return lax.broadcasted_iota(jnp.int32, (TP, TP), 0) == lax.broadcasted_iota(
        jnp.int32, (TP, TP), 1
    )


def split3(value):
    high = value.astype(BF16).astype(F32)
    rest = value - high
    middle = rest.astype(BF16).astype(F32)
    return high, middle, rest - middle


def augmented(raw, source):
    row = row_mask()
    scaled = raw * SCALE
    square = scaled * scaled
    norm = -0.5 * (square[0:1] + square[1:2] + square[2:3])
    if source:
        third, fourth = norm + (raw[6:7] - 1.0) * FAR, jnp.ones((1, TP), F32)
    else:
        third, fourth = jnp.ones((1, TP), F32), norm
    full = jnp.where(
        row < 3, scaled, jnp.where(row == 3, third, jnp.where(row == 4, fourth, 0.0))
    )
    h, m, l = split3(full)
    return jnp.concatenate([h, m, h, m, l, h] if source else [h, h, m, m, h, l], axis=0)


def assemble(own, west, east, up, down, ext):
    layers, columns = own.shape[0], own.shape[1]
    ext[0:2, 2 : columns + 2] = up[...]
    ext[layers + 2 : layers + 4, 2 : columns + 2] = down[...]
    ext[:, 0:2] = west[...]
    ext[:, columns + 2 : columns + 4] = east[...]
    ext[2 : layers + 2, 2 : columns + 2] = own[...]


def moderate(ext):
    span, width = ext.shape[0], ext.shape[1]
    flat = ext[...].reshape((span * width, 8, TP))
    peak = jnp.max(jnp.abs(flat), axis=0)
    row = row_mask()
    ratio = jnp.where(
        row < 3, peak / PLACE_LIMIT, jnp.where(row < 6, peak / SPEED_LIMIT, 0.0)
    )
    return jnp.max(ratio) <= 1.0


def near(codes, layer, column, row, col):
    places = []
    for k in range(6):
        code = codes[k, layer, column]
        down = (code * 11) >> 5
        places.append((row + down - 1, col + code - 3 * down - 1))
    return places


def to_row(total, eye):
    sums = jnp.sum(total, axis=1, keepdims=True)
    return jnp.sum(jnp.where(eye, sums, 0.0), axis=0, keepdims=True)


def fast_weights(left, btab, places):
    weights = []
    for p in range(3):
        right = jnp.concatenate([btab[places[2 * p]], btab[places[2 * p + 1]]], axis=1)
        weights.append(
            jnp.exp2(lax.dot_general(left, right, (((1,), (0,)), ((), ())), preferred_element_type=F32))
        )
    return weights


def fast_sum(left, btab, places, eye):
    total = None
    for weight in fast_weights(left, btab, places):
        part = weight[:, 0:TP] + weight[:, TP : 2 * TP]
        total = part if total is None else total + part
    return to_row(total, eye)


def rows_of(ref, place, row, count):
    return jnp.broadcast_to(ref[place[0], place[1], row : row + 1, :], (count, TP))


def slow_sum(ext, row, col, places, eye):
    cols = jnp.transpose(ext[row, col])
    sums = []
    for block in range(TP // ROWS):
        here = cols[block * ROWS : (block + 1) * ROWS]
        spot = [jnp.broadcast_to(here[:, c : c + 1], (ROWS, TP)) for c in range(3)]
        total = jnp.zeros((ROWS, TP), F32)
        for place in places:
            distance = None
            for c in range(3):
                offset = spot[c] - rows_of(ext, place, c, ROWS)
                square = offset * offset
                distance = square if distance is None else distance + square
            total = total + rows_of(ext, place, 6, ROWS) * jnp.exp(-distance)
        sums.append(jnp.sum(total, axis=1, keepdims=True))
    return jnp.sum(jnp.where(eye, jnp.concatenate(sums, axis=0), 0.0), axis=0, keepdims=True)


def slow_accel(ext, press_ref, damp_ref, row, col, places, eye):
    cols = jnp.transpose(ext[row, col])
    more = jnp.transpose(
        jnp.broadcast_to(press_ref[row - 1, pl.ds(col - 1, 1), :], (8, TP))
    )
    sums = [[], [], []]
    for block in range(TP // ROWS):
        span = slice(block * ROWS, (block + 1) * ROWS)
        here = cols[span]
        spot = [jnp.broadcast_to(here[:, c : c + 1], (ROWS, TP)) for c in range(3)]
        speed = [jnp.broadcast_to(here[:, 3 + c : 4 + c], (ROWS, TP)) for c in range(3)]
        press_here = jnp.broadcast_to(more[span, 0:1], (ROWS, TP))
        total = [jnp.zeros((ROWS, TP), F32) for c in range(3)]
        for place in places:
            offsets = [spot[c] - rows_of(ext, place, c, ROWS) for c in range(3)]
            distance = offsets[0] * offsets[0] + offsets[1] * offsets[1]
            distance = distance + offsets[2] * offsets[2]
            weight = rows_of(ext, place, 6, ROWS) * jnp.exp(-distance)
            there = (place[0] - 1, pl.ds(place[1] - 1, 1), slice(None))
            press = weight * (press_here + jnp.broadcast_to(press_ref[there], (ROWS, TP)))
            damp = weight * jnp.broadcast_to(damp_ref[there], (ROWS, TP))
            for c in range(3):
                relative = rows_of(ext, place, 3 + c, ROWS) - speed[c]
                total[c] = total[c] + (press * offsets[c] + damp * relative)
        for c in range(3):
            sums[c].append(jnp.sum(total[c], axis=1, keepdims=True))
    return [
        jnp.sum(jnp.where(eye, jnp.concatenate(part, axis=0), 0.0), axis=0, keepdims=True)
        for part in sums
    ]


def state_of(summed):
    density = 1.0 + summed * (1.0 / TP)
    press = (2.0 * stiffness) * (density - rest_density) / (density * density)
    return press, viscosity / density


def fill_sources(ext, btab, first, last, left, right):
    def step(row, carry):
        for col in range(left, right):
            btab[row, col] = augmented(ext[row, col], True).astype(BF16)
        return carry

    lax.fori_loop(first, last, step, 0)


def left_of(ext, row, col):
    return jnp.transpose(augmented(ext[row, col], False)).astype(BF16)


def prep_kernel(counts_in, codes_in, soil_in, out, counts, codes, soil, sems):
    copies = [
        pltpu.make_async_copy(counts_in, counts, sems.at[0]),
        pltpu.make_async_copy(codes_in, codes, sems.at[1]),
        pltpu.make_async_copy(soil_in, soil, sems.at[2]),
    ]
    for copy in copies:
        copy.start()
    for copy in copies:
        copy.wait()
    layers, columns = out.shape[0], out.shape[1]
    lane = lax.broadcasted_iota(jnp.int32, (1, TP), 1)
    for layer in range(layers):
        for column in range(columns):
            listed = jnp.zeros((1, TP), jnp.int32)
            for k in range(6):
                listed = jnp.where(lane == k, codes[k, layer, column], listed)
            live = jnp.where(lane < counts[layer, column], 1.0, 0.0)
            rows = [soil[layer, c, column : column + 1, :] for c in range(6)]
            out[layer, column] = jnp.concatenate(rows + [live, listed.astype(F32)], axis=0)


def rim_tile(index, layers, columns):
    side = index - 2 * columns
    on_side, last = side >= 0, index >= columns
    layer = jnp.where(on_side, 1 + (side >> 1), jnp.where(last, layers - 1, 0))
    column = jnp.where(
        on_side, (columns - 1) * (side & 1), jnp.where(last, index - columns, index)
    )
    return layer, column


def turn_kernel(own, lefts, btab):
    layers, columns = own.shape[0], own.shape[1]
    fill_sources(own, btab, 0, layers, 0, columns)

    def turn(layer, carry):
        for column in range(columns):
            lefts[layer, column] = left_of(own, layer, column)
        return carry

    lax.fori_loop(0, layers, turn, 0)


def inner_kernel(codes, lefts, btab, sums):
    layers, columns = lefts.shape[0], lefts.shape[1]
    eye = eye_mask()

    def step(layer, carry):
        for column in range(1, columns - 1):
            places = near(codes, layer, column, layer, column)
            row = fast_sum(lefts[layer, column], btab, places, eye)
            sums[layer, column : column + 1, :] = row
        return carry

    lax.fori_loop(1, layers - 1, step, 0)


def density_kernel(
    codes, own, west, east, up, down, lefts, mine, inner, out, ext, btab, sums
):
    layers, columns = own.shape[0], own.shape[1]
    assemble(own, west, east, up, down, ext)
    eye = eye_mask()
    fast = moderate(ext)
    sums[...] = inner[...]

    @pl.when(fast)
    def _():
        btab[2 : layers + 2, 2 : columns + 2] = mine[...]
        for row in range(1, layers + 3):
            edge = row in (1, layers + 2)
            for col in range(1, columns + 3) if edge else (1, columns + 2):
                btab[row, col] = augmented(ext[row, col], True).astype(BF16)
        rim = 2 * columns + 2 * (layers - 2)

        def step(group, carry):
            for part in range(TILES):
                index = group * TILES + part
                layer, column = rim_tile(index, layers, columns)
                places = near(codes, layer, column, layer + 2, column + 2)
                row = fast_sum(lefts[layer, column], btab, places, eye)
                sums[layer, pl.ds(column, 1), :] = row
            return carry

        lax.fori_loop(0, rim // TILES, step, 0)

    @pl.when(jnp.logical_not(fast))
    def _():
        def step(tile, carry):
            layer, column = tile // columns, tile % columns
            places = near(codes, layer, column, layer + 2, column + 2)
            row = slow_sum(ext, layer + 2, column + 2, places, eye)
            sums[layer, pl.ds(column, 1), :] = row
            return carry

        lax.fori_loop(0, layers * columns, step, 0)

    for layer in range(layers):
        span = slice(layer * columns, (layer + 1) * columns)
        press, damp = state_of(sums[layer])
        live = jnp.concatenate([own[layer, c, 6:7, :] for c in range(columns)], axis=0)
        out[0, span, :] = press
        out[1, span, :] = damp
        out[2, span, :] = press * live
        out[3, span, :] = damp * live


def ring_kernel(
    codes, own, west, east, up, down, extra, ext, sources, ftab, press_ref, damp_ref, btab
):
    layers, columns = own.shape[0], own.shape[1]
    assemble(own, west, east, up, down, ext)
    eye = eye_mask()
    fast = moderate(ext)
    for layer in range(layers):
        span = slice(layer * columns, (layer + 1) * columns)
        press_ref[layer + 1, 1 : columns + 1, :] = extra[0, span, :]
        damp_ref[layer + 1, 1 : columns + 1, :] = extra[1, span, :]

    def ring(handle):
        def across(index, carry):
            handle(1, index + 1)
            handle(layers + 2, index + 1)
            return carry

        def along(index, carry):
            handle(index + 2, 1)
            handle(index + 2, columns + 2)
            return carry

        lax.fori_loop(0, columns + 2, across, 0)
        lax.fori_loop(0, layers, along, 0)

    def keep(row, col, summed):
        press, damp = state_of(summed)
        press_ref[row - 1, pl.ds(col - 1, 1), :] = press
        damp_ref[row - 1, pl.ds(col - 1, 1), :] = damp

    @pl.when(fast)
    def _():
        fill_sources(ext, btab, 0, layers + 4, 0, columns + 4)

        sources[...] = btab[1 : layers + 3, 1 : columns + 3]

        def ring_sum(row, col):
            places = near(codes, row, col, row, col)
            keep(row, col, fast_sum(left_of(ext, row, col), btab, places, eye))

        ring(ring_sum)

        def factors(row, carry):
            for col in range(1, columns + 3):
                raw = ext[row, col]
                press = jnp.broadcast_to(press_ref[row - 1, col - 1 : col, :], (8, TP))
                damp = jnp.broadcast_to(damp_ref[row - 1, col - 1 : col, :], (8, TP))
                value = jnp.concatenate([raw, press * raw, damp * raw], axis=0)
                high = value.astype(BF16).astype(F32)
                ftab[row - 1, col - 1] = jnp.concatenate([high, value - high], axis=0).astype(BF16)
            return carry

        lax.fori_loop(1, layers + 3, factors, 0)

    @pl.when(jnp.logical_not(fast))
    def _():
        def ring_sum(row, col):
            places = near(codes, row, col, row, col)
            keep(row, col, slow_sum(ext, row, col, places, eye))

        ring(ring_sum)


def accel_kernel(codes, ext, btab, ftab, press_ref, damp_ref, out, pairs, lefts):
    layers, columns = out.shape[0], out.shape[2]
    eye = eye_mask()
    fast = moderate(ext)

    def weigh(layer):
        for column in range(columns):
            lefts[column] = left_of(ext, layer + 2, column + 2)
        for column in range(columns):
            places = near(codes, layer, column, layer + 1, column + 1)
            for p, weight in enumerate(fast_weights(lefts[column], btab, places)):
                high = weight.astype(BF16)
                pairs[column, p, :, 0 : 2 * TP] = high
                pairs[column, p, :, 2 * TP : 4 * TP] = (weight - high.astype(F32)).astype(BF16)

    def gather(layer):
        for column in range(columns):
            row, col = layer + 2, column + 2
            places = near(codes, layer, column, row - 1, col - 1)
            summed = None
            for p in range(3):
                source = jnp.concatenate([ftab[places[2 * p]], ftab[places[2 * p + 1]]], axis=1)
                part = lax.dot_general(
                    jnp.concatenate([source, source], axis=1),
                    pairs[column, p],
                    NT,
                    preferred_element_type=F32,
                )
                summed = part if summed is None else summed + part
            summed = summed[0:24] + summed[24:48]
            plain, pressed, damped = summed[0:8], summed[8:16], summed[16:24]
            raw = ext[row, col]
            press = press_ref[row - 1, col - 1 : col, :]
            push = raw * (press * plain[6:7] + pressed[6:7]) - (press * plain + pressed)
            drag = damped - raw * damped[6:7]
            total = (push[0:3] + drag[3:6]) * (raw[6:7] * (1.0 / TP))
            for c in range(3):
                out[layer, c, column : column + 1, :] = total[c : c + 1]

    @pl.when(fast)
    def _():
        def step(layer, carry):
            weigh(layer)
            gather(layer)
            return carry

        lax.fori_loop(0, layers, step, 0)

    @pl.when(jnp.logical_not(fast))
    def _():
        def step(tile, carry):
            layer, column = tile // columns, tile % columns
            row, col = layer + 2, column + 2
            places = near(codes, layer, column, row, col)
            rows = slow_accel(ext, press_ref, damp_ref, row, col, places, eye)
            scale = ext[row, col, 6:7, :] * (1.0 / TP)
            for c in range(3):
                out[layer, c, pl.ds(column, 1), :] = rows[c] * scale
            return carry

        lax.fori_loop(0, layers * columns, step, 0)


def owner_lags():
    row = row_mask()
    return [(row + 8 * k) // 6 for k in range(3)]


def folded(rows):
    return (rows[0:6] + rows[6:12]) + (rows[12:18] + rows[18:24])


def share_kernel(blocks, out):
    quads = blocks.shape[0] // 24
    rows = folded(jnp.sum(blocks[...].reshape((quads, 24, TP)), axis=0))
    out[...] = jnp.concatenate([rows, jnp.zeros((2, TP), F32)], axis=0)


def marker_kernel(soil, extra, place, speed, tiles, owners, slots, out, table, lookup):
    layers, columns = soil.shape[0], soil.shape[2]
    count = layers * columns
    pairs = place.shape[1] // (2 * TP)
    quads = out.shape[0] // 24
    groups = TP // 16
    field_of = lambda f: jnp.concatenate([soil[layer, f] for layer in range(layers)], axis=0)
    spots = [field_of(c) for c in range(3)]
    moves = [field_of(3 + c) for c in range(3)]
    press, damp = extra[2], extra[3]
    scaled = [jnp.clip(spot, -CLIP, CLIP) * SCALE for spot in spots]
    norm = -0.5 * (scaled[0] * scaled[0] + scaled[1] * scaled[1] + scaled[2] * scaled[2])
    fields = scaled + [norm, press, damp]
    fields = fields + [damp * moves[c] - press * spots[c] for c in range(3)]
    for number, field in enumerate(fields):
        if number < ONEHOT:
            pieces = list(split3(field)) + [jnp.zeros((TP - 3 * count, TP), F32)]
            turned = jnp.transpose(jnp.concatenate(pieces, axis=0)).astype(BF16)
            for group in range(groups):
                at = (group * ONEHOT + number) * 16
                table[at : at + 16, :] = turned[group * 16 : group * 16 + 16]
        else:
            pieces = [field, jnp.zeros((TP - count, TP), F32)]
            lookup[number - ONEHOT] = jnp.transpose(jnp.concatenate(pieces, axis=0))
    entry = lax.broadcasted_iota(jnp.int32, (TP, TP), 0)
    listed = jnp.where(entry < 3 * count, lax.rem(entry, count), -1)
    out[...] = jnp.zeros(out.shape, F32)

    lags = owner_lags()

    def add_terms(pair, terms):
        left, right = [], []
        for part in range(2):
            block = pair * 2 + part
            value = terms[:, part * TP : (part + 1) * TP]
            high = value.astype(BF16).astype(F32)
            owner = jnp.broadcast_to(owners[pl.ds(block, 1), :], (8, TP))
            late = [owner - lag for lag in lags]
            slot = jnp.broadcast_to(slots[pl.ds(block, 1), :], (TP, TP))
            hot = jnp.where(slot == entry, 1.0, 0.0).astype(BF16)
            masks = [late[k] == 4 * quad for quad in range(quads) for k in range(3)]
            for piece in (high, value - high):
                turned = [
                    jnp.concatenate(
                        [piece[(8 * k + r) % 6 : (8 * k + r) % 6 + 1] for r in range(8)], axis=0
                    )
                    for k in range(3)
                ]
                left.append(
                    jnp.concatenate(
                        [jnp.where(mask, turned[n % 3], 0.0) for n, mask in enumerate(masks)],
                        axis=0,
                    ).astype(BF16)
                )
                right.append(hot)
        out[...] = out[...] + lax.dot_general(
            jnp.concatenate(left, axis=1),
            jnp.concatenate(right, axis=1),
            NT,
            preferred_element_type=F32,
        )

    def forces_on(pair):
        wide = 2 * TP
        lanes = pl.ds(pl.multiple_of(pair * wide, wide), wide)
        which = [
            jnp.broadcast_to(tiles[pl.ds(pair * 2 + part, 1), :], (TP, TP)) for part in range(2)
        ]
        hot = jnp.concatenate(
            [jnp.where(w == listed, 1.0, 0.0).astype(BF16) for w in which], axis=1
        )
        y = place[:, lanes]
        u = speed[:, lanes]
        spread = y * SCALE
        at = [jnp.broadcast_to(spread[c : c + 1], (16, wide)) for c in range(3)]
        totals = [jnp.zeros((16, wide), F32) for number in range(5)]
        for group in range(groups):
            span = slice(group * 16, group * 16 + 16)
            rows = slice(group * 16 * ONEHOT, (group + 1) * 16 * ONEHOT)
            got = []
            if ONEHOT:
                picked = lax.dot_general(
                    table[rows, :], hot, (((1,), (0,)), ((), ())), preferred_element_type=F32
                )
                got = [picked[16 * number : 16 * number + 16] for number in range(ONEHOT)]
            for number in range(9 - ONEHOT):
                source = lookup[number, span, :]
                got.append(
                    jnp.concatenate(
                        [jnp.take_along_axis(source, w[0:16], axis=1) for w in which], axis=1
                    )
                )
            power = (got[3] + at[0] * got[0]) + (at[1] * got[1] + at[2] * got[2])
            weight = jnp.exp2(power)
            for number in range(5):
                totals[number] = totals[number] + weight * got[4 + number]
        sums = [jnp.sum(total, axis=0, keepdims=True) for total in totals]
        square = spread * spread
        scale = jnp.exp2(-0.5 * (square[0:1] + square[1:2] + square[2:3])) * (1.0 / TP)
        where = [y[c : c + 1] for c in range(3)]
        force = [
            (where[c] * sums[0] + (sums[2 + c] - u[c : c + 1] * sums[1])) * scale
            for c in range(3)
        ]
        moment = cross(where, force)
        return jnp.concatenate(force + moment + [jnp.zeros((2, wide), F32)], axis=0)

    def step(turn, terms):
        first, second = terms
        ahead = forces_on(2 * turn)
        add_terms(jnp.maximum(2 * turn - 1, 0), second)
        behind = forces_on(2 * turn + 1)
        add_terms(2 * turn, ahead)
        return ahead, behind

    blank = jnp.zeros((8, 2 * TP), F32)
    _, terms = lax.fori_loop(0, pairs // 2, step, (blank, blank))
    add_terms(pairs - 1, terms)


def cross(a, b):
    return [
        a[1] * b[2] - a[2] * b[1],
        a[2] * b[0] - a[0] * b[2],
        a[0] * b[1] - a[1] * b[0],
    ]


def advance_kernel(first, second, third, fourth, state, inertia, out, sent):
    totals = (first[...] + second[...]) + (third[...] + fourth[...])
    row = lambda ref, r: ref[r : r + 1, :]
    force = [totals[c : c + 1] for c in range(3)]
    moments = [totals[3 + c : 4 + c] for c in range(3)]
    center = [row(state, c) for c in range(3)]
    velocity = [row(state, 3 + c) for c in range(3)]
    spin = [row(state, 6 + c) for c in range(3)]
    inv_mass = row(inertia, 0)
    moment = [row(inertia, 1 + c) for c in range(3)]
    arm = cross(center, force)
    gyro = cross(spin, [moment[c] * spin[c] for c in range(3)])
    pull = [0.0, 0.0, -gravity]
    new_vel = [velocity[c] + time_step * (inv_mass * force[c] + pull[c]) for c in range(3)]
    new_spin = [
        spin[c] + time_step * ((moments[c] - arm[c]) - gyro[c]) / moment[c] for c in range(3)
    ]
    new_center = [center[c] + time_step * new_vel[c] for c in range(3)]
    out[...] = jnp.concatenate(new_center + new_vel + new_spin, axis=0)
    swing = cross(new_spin, center)
    base = [new_vel[c] - swing[c] for c in range(3)]
    block = jnp.concatenate((base + new_spin) * 4, axis=0)
    quads = sent.shape[0] // 24
    sent[...] = jnp.broadcast_to(block[None], (quads, 24, TP)).reshape(sent.shape)


def pick_kernel(states, place, owners, slots, out):
    steps = place.shape[1] // (PICK * TP)
    quads = states.shape[0] // 24
    lags = owner_lags()

    def step(index, carry):
        for part in range(PICK):
            block = index * PICK + part
            lanes = pl.ds(pl.multiple_of(block * TP, TP), TP)
            slot = jnp.broadcast_to(slots[pl.ds(block, 1), :], (8, TP))
            owner = jnp.broadcast_to(owners[pl.ds(block, 1), :], (8, TP))
            late = [owner - lag for lag in lags]
            found = [jnp.zeros((8, TP), F32) for k in range(3)]
            for quad in range(quads):
                for k in range(3):
                    at = 24 * quad + 8 * k
                    here = jnp.take_along_axis(states[at : at + 8, :], slot, axis=1)
                    found[k] = jnp.where(late[k] == 4 * quad, here, found[k])
            picked = folded(jnp.concatenate(found, axis=0))
            y = place[:, lanes]
            turn = cross(
                [picked[3 + c : 4 + c] for c in range(3)], [y[c : c + 1] for c in range(3)]
            )
            out[:, lanes] = picked[0:3] + jnp.concatenate(turn, axis=0)
        return carry

    lax.fori_loop(0, steps, step, 0)


def shifted(shard, axis, dim, width):
    size, length = lax.axis_size(axis), shard.shape[dim]
    up = [(i, i + 1) for i in range(size - 1)]
    down = [(j, i) for i, j in up]
    last = lax.slice_in_dim(shard, length - width, length, axis=dim)
    first = lax.slice_in_dim(shard, 0, width, axis=dim)
    return lax.ppermute(last, axis, up), lax.ppermute(first, axis, down)


def local(
    soil_state,
    tile_count,
    tile_neighbors,
    marker_pos,
    marker_vel,
    marker_tile,
    marker_owner,
    marker_slot,
    body_state,
    body_inertia,
):
    layers, columns, fields, tile_size = soil_state.shape
    marker_count = marker_pos.shape[1]
    tile_devs = lax.axis_size("tile")
    depth_devs = lax.axis_size("depth")
    soil = jnp.transpose(soil_state, (0, 2, 1, 3))
    codes = jnp.transpose(tile_neighbors, (2, 0, 1))
    own = pl.pallas_call(
        prep_kernel,
        out_shape=jax.ShapeDtypeStruct((layers, columns, 8, TP), F32),
        in_specs=[pl.BlockSpec(memory_space=pltpu.HBM)] * 3,
        out_specs=vspec(),
        scratch_shapes=[
            SMEM((layers, columns), jnp.int32),
            SMEM((6, layers, columns), jnp.int32),
            VMEM((layers, fields, columns, TP), F32),
            pltpu.SemaphoreType.DMA((3,)),
        ],
        compiler_params=params(),
        name="prep",
    )(*[pltpu.with_memory_space_constraint(x, pltpu.HBM) for x in (tile_count, codes, soil)])
    up, down = shifted(own, "depth", 0, 2)
    lefts, mine = pl.pallas_call(
        turn_kernel,
        out_shape=(
            jax.ShapeDtypeStruct((layers, columns, TP, AUG), BF16),
            jax.ShapeDtypeStruct((layers, columns, AUG, TP), BF16),
        ),
        in_specs=[vspec()],
        out_specs=(vspec(), vspec()),
        cost_estimate=cost(1_000_000, 1 << 18),
        compiler_params=params(),
        name="turn",
    )(own)
    up, down, mine = lax.optimization_barrier((up, down, mine))
    west, east = shifted(jnp.concatenate([up, own, down], axis=0), "tile", 1, 2)
    inner = pl.pallas_call(
        inner_kernel,
        out_shape=jax.ShapeDtypeStruct((layers, columns, TP), F32),
        in_specs=[sspec(), vspec(), vspec()],
        out_specs=vspec(),
        cost_estimate=cost(4_000_000, 1 << 18, 1_000_000),
        compiler_params=params(),
        name="inner",
    )(codes, lefts, mine)
    pieces = (own, west, east, up, down)
    span, width = layers + 4, columns + 4
    pairs = layers * columns * 6 * TP * TP
    extra = pl.pallas_call(
        density_kernel,
        out_shape=jax.ShapeDtypeStruct((4, layers * columns, TP), F32),
        in_specs=[sspec()] + [vspec()] * 8,
        out_specs=vspec(),
        scratch_shapes=[
            VMEM((span, width, 8, TP), F32),
            VMEM((span, width, AUG, TP), BF16),
            VMEM((layers, columns, TP), F32),
        ],
        cost_estimate=cost(pairs * 12, 1 << 18, pairs),
        compiler_params=params(),
        name="density",
    )(codes, *pieces, lefts, mine, inner)
    owners = marker_owner.reshape((marker_count // TP, TP))
    slots = marker_slot.reshape((marker_count // TP, TP))
    tiles = marker_tile.reshape((marker_count // TP, TP))
    partial_sums = pl.pallas_call(
        marker_kernel,
        out_shape=jax.ShapeDtypeStruct((tile_devs * 6, TP), F32),
        in_specs=[vspec()] * 7,
        out_specs=vspec(),
        scratch_shapes=[VMEM((9 * TP, TP), BF16), VMEM((9, TP, TP), F32)],
        cost_estimate=cost(marker_count * TP * 25, 1 << 19, marker_count * TP),
        compiler_params=params(),
        name="markers",
    )(soil, extra, marker_pos, marker_vel, tiles, owners, slots)
    partial_sums, extra = lax.optimization_barrier((partial_sums, extra))
    flat = (tile_devs, 1, 6 * TP)
    arrived = lax.all_to_all(partial_sums.reshape(flat), "tile", 0, 0, tiled=True)
    own, west, east, up, down = pieces
    ring_codes = jnp.concatenate(
        [
            part[:, :, 7, 0:6]
            for part in (west, jnp.concatenate([up, own, down], axis=0), east)
        ],
        axis=1,
    )
    ring_codes = jnp.transpose(ring_codes.astype(jnp.int32), (2, 0, 1))
    shapes = (
        jax.ShapeDtypeStruct((span, width, 8, TP), F32),
        jax.ShapeDtypeStruct((layers + 2, columns + 2, AUG, TP), BF16),
        jax.ShapeDtypeStruct((layers + 2, columns + 2, FACTORS, TP), BF16),
        jax.ShapeDtypeStruct((layers + 2, 16, TP), F32),
        jax.ShapeDtypeStruct((layers + 2, 16, TP), F32),
    )
    tables = pl.pallas_call(
        ring_kernel,
        out_shape=shapes,
        in_specs=[sspec()] + [vspec()] * 6,
        out_specs=(vspec(),) * 5,
        scratch_shapes=[VMEM((span, width, AUG, TP), BF16)],
        cost_estimate=cost(pairs * 15, 1 << 19, pairs),
        compiler_params=params(),
        name="ring",
    )(ring_codes, *pieces, extra)
    arrived, damp = lax.optimization_barrier((arrived, tables[4]))
    share = pl.pallas_call(
        share_kernel,
        out_shape=jax.ShapeDtypeStruct((8, TP), F32),
        in_specs=[vspec()],
        out_specs=vspec(),
        compiler_params=params(),
        name="share",
    )(arrived.reshape((tile_devs * 6, TP)))

    others = [
        lax.ppermute(share, "depth", [(i, (i + k) % depth_devs) for i in range(depth_devs)])
        for k in range(1, depth_devs)
    ]
    body_next, sent = pl.pallas_call(
        advance_kernel,
        out_shape=(
            jax.ShapeDtypeStruct((9, TP), F32),
            jax.ShapeDtypeStruct((tile_devs * 6, TP), F32),
        ),
        in_specs=[vspec()] * 6,
        out_specs=(vspec(), vspec()),
        compiler_params=params(),
        name="advance",
    )(share, *others, body_state, body_inertia)
    sent, damp = lax.optimization_barrier((sent, damp))
    states = lax.all_to_all(sent.reshape(flat), "tile", 0, 0, tiled=True)
    accel = pl.pallas_call(
        accel_kernel,
        out_shape=jax.ShapeDtypeStruct((layers, 3, columns, TP), F32),
        in_specs=[sspec()] + [vspec()] * 5,
        out_specs=vspec(),
        scratch_shapes=[VMEM((columns, 3, TP, 4 * TP), BF16), VMEM((columns, TP, AUG), BF16)],
        cost_estimate=cost(pairs * 15, 1 << 19, pairs),
        compiler_params=params(),
        name="accel",
    )(codes, *tables[:4], damp)
    states, accel = lax.optimization_barrier((states, accel))
    soil_accel = jnp.transpose(accel, (0, 2, 1, 3))
    marker_vel_next = pl.pallas_call(
        pick_kernel,
        out_shape=jax.ShapeDtypeStruct((3, marker_count), F32),
        in_specs=[vspec()] * 4,
        out_specs=vspec(),
        compiler_params=params(),
        name="pick",
    )(states.reshape((tile_devs * 6, TP)), marker_pos, owners, slots)
    return (soil_accel, body_next, marker_vel_next)


def solution(mesh):
    placed = (
        P("depth", "tile", None, None),
        P("depth", "tile"),
        P("depth", "tile", None),
        P(None, ("tile", "depth")),
        P(None, ("tile", "depth")),
        P(("tile", "depth")),
        P(("tile", "depth"), None),
        P(("tile", "depth")),
        P(None, "tile"),
        P(None, "tile"),
    )
    return jax.shard_map(
        local,
        mesh=mesh,
        in_specs=placed,
        out_specs=(P("depth", "tile", None, None), P(None, "tile"), P(None, ("tile", "depth"))),
        check_vma=False,
    )
```
